32 devices in a mesh: scene: 2 (over y), seq: 4 (over z), head: 2 (over x), band: 2 (over core).
Axes of the slice: x: 2, y: 2, z: 4, core: 2. Of those that a mesh axis runs over, the one named last changes fastest.
Arguments:
- tokens: bfloat16 [8, 12, 37, 1024], P(('scene', 'seq'), ('head', 'band')), parts along dimension 0, may hold values from -6 to 6
- frame_gain: float32 [1024], replicated, may hold values from 0.5 to 1.5
- frame_qkv: bfloat16 [3, 1024, 1024], P(None, None, 'head'), may hold values from -6 to 6
- frame_out: bfloat16 [1024, 1024], P('head'), may hold values from -0.1875 to 0.1875
- global_gain: float32 [1024], replicated, may hold values from 0.5 to 1.5
- global_qkv: bfloat16 [3, 1024, 1024], P(None, None, 'head'), may hold values from -6 to 6
- global_out: bfloat16 [1024, 1024], P('head'), may hold values from -0.1875 to 0.1875
- head_gain: float32 [2048], replicated, may hold values from 0.5 to 1.5
- head_proj: bfloat16 [2048, 256], replicated, may hold values from -0.125 to 0.125
- head_bias: float32 [256], replicated, may hold values from -3 to 3
- head_conv: bfloat16 [3, 3, 256, 256], replicated, may hold values from -0.125 to 0.125
Outputs:
- blocks: bfloat16 [8, 12, 37, 1024], P(('scene', 'seq'), ('head', 'band')), parts along dimension 0
- features: bfloat16 [8, 12, 37, 256], P(('scene', 'seq'), ('head', 'band')), parts along dimension 0
The draws below stay inside these ranges and needn't reach their ends.
There are 2 independent parts, one for each index of `scene`. The reference program is written for one: setup_inputs(seed, part) draws one part's arguments, and reference() takes and returns one part's arrays. A program takes and returns all parts, laid end to end along the dimension named above; an argument that names none is the same for every part. Nothing has to cross between parts.
All inputs are finite; a program needn't handle non-finite values.
Results may differ from the reference program's by a relative error of at most 0.017.
Values may be sent and summed in bfloat16 or wider, within the bound.
A program may use at most 256 MiB of HBM per device.

```python
import math
import jax
import jax.numpy as jnp
from jax import lax

D = 1024
HEADS = 16
HD = 64
CH = 256
PC = 37
PR = 12
FRAMES = 4


def projection_draw(key):
    first_key, second_key = jax.random.split(key, 2)
    base = jax.random.truncated_normal(first_key, -6.0, 6.0, (3, D, D), jnp.float32) * D ** (-0.5)
    head_scale = jnp.exp(jax.random.uniform(second_key, (2, HEADS), jnp.float32, math.log(1.3), math.log(2.2)))
    columns = jnp.repeat(head_scale, HD, axis=1)
    queries = base[0] * columns[0]
    keys_part = base[1] * columns[1]
    stacked = jnp.stack([queries, keys_part, base[2]])
    return jnp.clip(stacked, -6.0, 6.0).astype(jnp.bfloat16)


def draw_frame_qkv(key, part):
    return projection_draw(jax.random.fold_in(key, 11))


def draw_global_qkv(key, part):
    return projection_draw(jax.random.fold_in(key, 23))


def level_of(key, shape, cuts, low, largest):
    level, own = 1.0, jax.random.fold_in(key, 6)
    for axis_at, blocks in cuts:
        heights = jnp.exp(jax.random.uniform(jax.random.fold_in(own, axis_at), (blocks,), jnp.float32, low / len(cuts), largest / len(cuts)))
        level = level * jnp.repeat(heights, shape[axis_at] // blocks).reshape([-1 if axis == axis_at else 1 for axis in range(len(shape))])
    return level


def noise(own_key, shape, scale, most, shards=(), held_as=jnp.bfloat16):
    values = jax.random.normal(own_key, shape, jnp.float32) * scale
    if len(shards) > 0:
        values = level_of(own_key, shape, shards, -0.22, 0.18) * values
    return jnp.clip(values, min=-most, max=most).astype(held_as)


def setup_inputs(seed: int = 0, part: int = 0) -> dict:
    key_of = jax.random.split(jax.random.key(seed), 12)
    own_keys = jax.random.split(jax.random.fold_in(key_of[11], part), 12)
    tokens = noise(own_keys[0], (FRAMES, PR, PC, D), 1.0, 6.0, ((0, 4), (1, 4)))
    frame_gain = jnp.clip(1.0 + 0.1 * jax.random.normal(key_of[1], (D,), jnp.float32), 0.5, 1.5)
    frame_qkv = draw_frame_qkv(jax.random.fold_in(key_of[11], 71), part)
    frame_out = noise(key_of[3], (D, D), D ** -0.5, 0.1875, ((0, 2),))
    global_gain = jnp.clip(1.0 + 0.1 * jax.random.normal(key_of[4], (D,), jnp.float32), 0.5, 1.5)
    global_qkv = draw_global_qkv(jax.random.fold_in(key_of[11], 71), part)
    global_out = noise(key_of[6], (D, D), D ** -0.5, 0.1875, ((0, 2),))
    head_gain = jnp.clip(1.0 + 0.1 * jax.random.normal(key_of[7], (2 * D,), jnp.float32), 0.5, 1.5)
    head_proj = noise(key_of[8], (2 * D, CH), (2 * D) ** -0.5, 0.125)
    head_bias = noise(key_of[9], (CH,), 0.5, 3.0, (), jnp.float32)
    head_conv = noise(key_of[10], (3, 3, CH, CH), (9 * CH) ** -0.5, 0.125)
    return {"tokens": tokens, "frame_gain": frame_gain, "frame_qkv": frame_qkv, "frame_out": frame_out, "global_gain": global_gain, "global_qkv": global_qkv, "global_out": global_out, "head_gain": head_gain, "head_proj": head_proj, "head_bias": head_bias, "head_conv": head_conv}


norm_eps = 1e-06
head_eps = 1e-05

def layer_norm(values, gain, epsilon):
    centre = values - lax.optimization_barrier(jnp.mean(values, axis=-1, keepdims=True))
    spread = lax.optimization_barrier(jnp.mean(centre * centre, axis=-1, keepdims=True))
    return centre * lax.rsqrt(spread + epsilon) * gain

def attend_head(triple):
    queries, keys_all, values_all = triple
    scores = jnp.dot(queries, keys_all.T, preferred_element_type=jnp.float32) * HD ** (-0.5)
    probs = jnp.exp(scores - lax.optimization_barrier(jnp.max(scores, axis=-1, keepdims=True)))
    mixed = jnp.dot(probs.astype(jnp.bfloat16), values_all, preferred_element_type=jnp.float32)
    return mixed / lax.optimization_barrier(jnp.sum(probs, axis=-1, keepdims=True))

def by_heads(matrix):
    return matrix.reshape(matrix.shape[0], HEADS, HD).transpose(1, 0, 2)

def attention(queries, keys_all, values_all):
    mixed = lax.map(attend_head, (by_heads(queries), by_heads(keys_all), by_heads(values_all)))
    return mixed.transpose(1, 0, 2).reshape(queries.shape[0], D).astype(jnp.bfloat16)

def attention_block(inputs, gain, qkv_weight, out_weight, wide):
    frames_now, per_frame = (inputs.shape[0], inputs.shape[1])
    normed = layer_norm(inputs.astype(jnp.float32), gain, norm_eps).astype(jnp.bfloat16)
    flattened = normed.reshape(frames_now * per_frame, D)
    query_rows = jnp.dot(flattened, qkv_weight[0], preferred_element_type=jnp.float32).astype(jnp.bfloat16)
    key_rows = jnp.dot(flattened, qkv_weight[1], preferred_element_type=jnp.float32).astype(jnp.bfloat16)
    value_rows = jnp.dot(flattened, qkv_weight[2], preferred_element_type=jnp.float32).astype(jnp.bfloat16)
    query_frames = query_rows.reshape(frames_now, per_frame, D)
    if wide:

        def one_frame(frame_queries):
            return attention(frame_queries, key_rows, value_rows)
        mixed = lax.map(one_frame, query_frames)
    else:

        def own_frame(triple):
            return attention(triple[0], triple[1], triple[2])
        mixed = lax.map(own_frame, (query_frames, key_rows.reshape(frames_now, per_frame, D), value_rows.reshape(frames_now, per_frame, D)))
    branch = jnp.dot(mixed.reshape(-1, D), out_weight, preferred_element_type=jnp.float32)
    merged = inputs.astype(jnp.float32).reshape(-1, D) + branch
    return merged.astype(jnp.bfloat16).reshape(inputs.shape)

def reference(tokens, frame_gain, frame_qkv, frame_out, global_gain, global_qkv, global_out, head_gain, head_proj, head_bias, head_conv):
    inputs = tokens.reshape(FRAMES, PR * PC, D)
    first = attention_block(inputs, frame_gain, frame_qkv, frame_out, False)
    second = attention_block(first, global_gain, global_qkv, global_out, True)
    stacked = jnp.concatenate([first.astype(jnp.float32), second.astype(jnp.float32)], axis=-1)
    normed = layer_norm(stacked, head_gain, head_eps).astype(jnp.bfloat16)
    projected = jnp.dot(normed.reshape(-1, 2 * D), head_proj, preferred_element_type=jnp.float32) + head_bias
    projected = projected.astype(jnp.bfloat16).reshape(FRAMES, PR, PC, CH)
    padded = jnp.pad(projected, ((0, 0), (1, 1), (1, 1), (0, 0)))
    totals = jnp.zeros((FRAMES, PR, PC, CH), jnp.float32)
    for offset_row in range(3):
        for offset_col in range(3):
            window = padded[:, offset_row:offset_row + PR, offset_col:offset_col + PC].astype(jnp.float32)
            totals = totals + jnp.einsum('frcx,xy->frcy', window, head_conv[offset_row, offset_col].astype(jnp.float32))
    return (second.reshape(FRAMES, PR, PC, D), totals.astype(jnp.bfloat16))
```

```python
import functools
import math

import jax
import jax.numpy as jnp
from jax import lax
from jax.experimental import pallas as pl
from jax.experimental.pallas import tpu as pltpu
from jax.sharding import PartitionSpec as P

HD = 64


norm_eps = 1e-06
head_eps = 1e-05


def padded_2(block, sides, width):
    for axis, dim in sides:
        count = lax.axis_size(axis)
        forward = [(i, i + 1) for i in range(count - 1)]
        backward = [(target, source) for source, target in forward]
        low = lax.ppermute(
            lax.slice_in_dim(block, block.shape[dim] - width, None, axis=dim), axis, forward
        )
        high = lax.ppermute(lax.slice_in_dim(block, 0, width, axis=dim), axis, backward)
        block = jnp.concatenate([low, block, high], axis=dim)
    return block


def layer_norm(values, gain, epsilon):
    centre = values - jnp.mean(values, axis=-1, keepdims=True)
    spread = jnp.mean(centre * centre, axis=-1, keepdims=True)
    return centre * lax.rsqrt(spread + epsilon) * gain


def by_heads(matrix):
    return matrix.reshape(matrix.shape[0], matrix.shape[1] // HD, HD)


def attend_local(queries, keys_all, values_all):
    scores = jnp.einsum(
        "qhd,khd->qhk", by_heads(queries), by_heads(keys_all), preferred_element_type=jnp.float32
    ) * HD ** (-0.5)
    probs = jnp.exp(scores - jnp.max(scores, axis=-1, keepdims=True))
    mixed = jnp.einsum(
        "qhk,khd->qhd",
        probs.astype(jnp.bfloat16),
        by_heads(values_all),
        preferred_element_type=jnp.float32,
    )
    mixed = mixed / jnp.sum(probs, axis=-1)[..., None]
    return mixed.reshape(queries.shape).astype(jnp.bfloat16)


def key_step(local_rows, portion_rows):
    amount = portion_rows // local_rows
    best = 1
    for factor in range(1, amount + 1):
        if amount % factor == 0 and local_rows * factor <= max(local_rows, 1024):
            best = factor
    return local_rows * best


def fresh_carry(queries):
    heads_q = by_heads(queries)
    return (
        jnp.full(heads_q.shape[:2], -jnp.inf, jnp.float32),
        jnp.zeros(heads_q.shape[:2], jnp.float32),
        jnp.zeros(heads_q.shape, jnp.float32),
    )


def finish(carry, queries):
    return (carry[2] / carry[1][..., None]).reshape(queries.shape).astype(jnp.bfloat16)


def fold_keys(queries, carry, portions, local_rows):
    keys_in, values_in = portions
    step_rows = key_step(local_rows, keys_in.shape[0])
    heads_q = by_heads(queries)
    key_blocks = keys_in.reshape(-1, step_rows, keys_in.shape[1])
    value_blocks = values_in.reshape(-1, step_rows, values_in.shape[1])

    def absorb(states, blocks_pair):
        running_max, running_sum, weighted = states
        scores = jnp.einsum(
            "qhd,khd->qhk", heads_q, by_heads(blocks_pair[0]), preferred_element_type=jnp.float32
        ) * HD ** (-0.5)
        new_max = jnp.maximum(running_max, jnp.max(scores, axis=-1))
        decay = jnp.exp(running_max - new_max)
        probs = jnp.exp(scores - new_max[..., None])
        running_sum = running_sum * decay + jnp.sum(probs, axis=-1)
        weighted = weighted * decay[..., None] + jnp.einsum(
            "qhk,khd->qhd",
            probs.astype(jnp.bfloat16),
            by_heads(blocks_pair[1]),
            preferred_element_type=jnp.float32,
        )
        return ((new_max, running_sum, weighted), None)

    carry, ignored = lax.scan(absorb, carry, (key_blocks, value_blocks))
    return carry


def attention_block(inputs, gain, qkv_weight, out_weight, wide):
    normed = layer_norm(inputs.astype(jnp.float32), gain, norm_eps).astype(jnp.bfloat16)
    gathered = lax.all_gather(normed, "head", axis=1, tiled=True)
    flattened = gathered.reshape(-1, gathered.shape[-1])
    query_rows = jnp.dot(flattened, qkv_weight[0], preferred_element_type=jnp.float32).astype(
        jnp.bfloat16
    )
    key_rows = jnp.dot(flattened, qkv_weight[1], preferred_element_type=jnp.float32).astype(
        jnp.bfloat16
    )
    value_rows = jnp.dot(flattened, qkv_weight[2], preferred_element_type=jnp.float32).astype(
        jnp.bfloat16
    )
    if wide:
        carry = fold_keys(
            query_rows,
            fresh_carry(query_rows),
            (
                lax.all_gather(key_rows, ("seq", "band"), axis=0, tiled=True),
                lax.all_gather(value_rows, ("seq", "band"), axis=0, tiled=True),
            ),
            key_rows.shape[0],
        )
        attended = finish(carry, query_rows)
    else:
        keys_all, values_all = (
            lax.all_gather(key_rows, "band", axis=0, tiled=True),
            lax.all_gather(value_rows, "band", axis=0, tiled=True),
        )
        attended = attend_local(query_rows, keys_all, values_all)
    band_rows = inputs.shape[1] * inputs.shape[2]
    own_rows = lax.all_to_all(attended, "head", split_axis=0, concat_axis=1, tiled=True)
    branch = jnp.dot(
        own_rows,
        lax.all_gather(out_weight, "head", axis=0, tiled=True),
        preferred_element_type=jnp.float32,
    )
    merged = inputs.astype(jnp.float32).reshape(band_rows, -1) + branch
    return merged.astype(jnp.bfloat16).reshape(inputs.shape)


def on_device(
    tokens,
    frame_gain,
    frame_qkv,
    frame_out,
    global_gain,
    global_qkv,
    global_out,
    head_gain,
    head_proj,
    head_bias,
    head_conv,
):
    first = attention_block(tokens, frame_gain, frame_qkv, frame_out, False)
    second = attention_block(first, global_gain, global_qkv, global_out, True)
    band_height = tokens.shape[1]
    grid_width = tokens.shape[2]
    stacked = jnp.concatenate([first.astype(jnp.float32), second.astype(jnp.float32)], axis=-1)
    normed = layer_norm(stacked, head_gain, head_eps).astype(jnp.bfloat16)
    projected = (
        jnp.dot(
            normed.reshape(-1, stacked.shape[-1]), head_proj, preferred_element_type=jnp.float32
        )
        + head_bias
    )
    projected = projected.astype(jnp.bfloat16).reshape(
        tokens.shape[0], band_height, grid_width, head_proj.shape[1]
    )
    padded = padded_2(projected, ((("head", "band"), 1),), 1)
    padded = jnp.pad(padded, ((0, 0), (0, 0), (1, 1), (0, 0)))
    totals = jnp.zeros(projected.shape, jnp.float32)
    for offset_row in range(3):
        for offset_col in range(3):
            window = padded[
                :, offset_row : offset_row + band_height, offset_col : offset_col + grid_width
            ]
            totals = totals + jnp.einsum(
                "frcx,xy->frcy",
                window,
                head_conv[offset_row, offset_col],
                preferred_element_type=jnp.float32,
            )
    return (second, totals.astype(jnp.bfloat16))


BF = jnp.bfloat16
F32 = jnp.float32
TILE = 16
LANES = 2 * HD
QSCALE = HD ** (-0.5) * math.log2(math.e)


def up(count):
    return -(-count // TILE) * TILE


def mm(a, b):
    return jnp.dot(a, b, preferred_element_type=F32)


def swap(values):
    return pltpu.roll(values, HD, axis=1)


def dot_t(a, b):
    return lax.dot_general(a, b, (((1,), (1,)), ((), ())), preferred_element_type=F32)


def row_parts(rows):
    first = up(rows // 2)
    return [(0, first), (first, rows - first)]


def step_list(rows):
    steps, at = [], 0
    for j in range(2):
        for start, size in row_parts(rows):
            steps.append((j, start, size, at))
            at += 2 * size
    return steps


def sem_layout(seq, pairs):
    names = [
        ("tok", 1), ("tok_x", 2), ("tok_f", 2), ("att", 4), ("part", 4), ("norm", 4),
        ("kv", 4 * seq), ("q", 4 * seq), ("o", 4 * seq), ("go", 2), ("halo", 2),
    ]
    at, table = 0, {}
    for name, size in names:
        table[name] = at
        at += size
    return table, at


def scene_kernel(
    seq,
    height,
    width,
    tok_ref,
    f_gain,
    f_qkv,
    f_out,
    g_gain,
    g_qkv,
    g_out,
    h_gain,
    h_proj,
    h_bias,
    h_conv,
    blocks_ref,
    feat_ref,
    stage,
    toks,
    wf,
    wg,
    wkv1,
    wkv2,
    fo,
    go,
    wp,
    wc,
    q1,
    kv1,
    vx1,
    att,
    att_in,
    p_own,
    p_out,
    p_in,
    n_own,
    n_in,
    fst,
    q2,
    skv,
    kv,
    vx,
    sq,
    rq,
    so,
    ro,
    a2,
    pj,
    halo,
    xbuf,
    send,
    recv,
    local,
):
    s, z = lax.axis_index("scene"), lax.axis_index("seq")
    x, c = lax.axis_index("head"), lax.axis_index("band")
    real = height * width
    rows, dim = fst.shape
    cols = wf.shape[2]
    pairs = cols // LANES
    frame = 4 * rows
    half = rows // 2
    steps = step_list(rows)
    parts = row_parts(rows)
    sems, _ = sem_layout(seq, pairs)
    core, across = (s, z, x, 1 - c), (s, z, 1 - x, c)
    place = 2 * x + c

    def z_peer(offset):
        return (s, lax.rem(z + offset, seq), x, c)

    def remote(name, index, source, target, device, back=None):
        return pltpu.make_async_remote_copy(
            src_ref=source,
            dst_ref=target,
            send_sem=send.at[sems[name] + index],
            recv_sem=recv.at[sems[name] + (index if back is None else back)],
            device_id=device,
            device_id_type=pl.DeviceIdType.MESH,
        )

    started = []

    def put(name, index, source, target, device):
        copy = remote(name, index, source, target, device)
        copy.start()
        started.append(copy)
        return copy

    own_cols = pl.ds(pl.multiple_of(c * cols, cols), cols)
    loads = []

    def load(source, target):
        copy = pltpu.make_async_copy(source, target, local.at[len(loads)])
        copy.start()
        loads.append(copy)
        return copy

    wf_load = load(f_qkv.at[:, :, own_cols], wf)
    fo_loads = []
    for r in range(2):
        owner = c if r == 0 else 1 - c
        for i in range(2 * pairs):
            source = f_out.at[pl.ds(pl.multiple_of(owner * cols + i * HD, HD), HD)]
            fo_loads.append(load(source, fo.at[pl.ds(r * cols + (i ^ 1) * HD, HD)]))
    wg_load = load(g_qkv.at[:, :, own_cols], wg)
    half_rows = pl.ds(pl.multiple_of(x * 2 * cols, 2 * cols), 2 * cols)
    late_loads = [load(g_out, go.at[half_rows]), load(h_proj, wp), load(h_conv, wc)]

    barrier = pltpu.get_barrier_semaphore()
    everyone = [core, across, (s, z, 1 - x, 1 - c)] + [z_peer(d) for d in range(1, seq)]
    for device in everyone:
        pl.semaphore_signal(
            barrier, inc=1, device_id=device, device_id_type=pl.DeviceIdType.MESH
        )
    for r in range(height):
        stage[r * width : (r + 1) * width, :] = tok_ref[0, r].astype(F32)
    for r in range(real, rows):
        stage[r : r + 1, :] = stage[real - 1 : real, :]
    toks[0] = stage[0:rows, :].astype(BF)
    pl.semaphore_wait(barrier, len(everyone))

    tok_x = []
    for k, (start, size) in enumerate(parts):
        at = pl.ds(start, size)
        tok_x.append(put("tok_x", k, toks.at[0, at], toks.at[2, at], across))
    tok_core = put("tok", 0, toks.at[0], toks.at[1], core)

    low = lax.broadcasted_iota(jnp.int32, (1, LANES), 1) < HD
    lane = lax.broadcasted_iota(jnp.int32, (1, 2 * cols), 1)
    v_lanes = lax.rem(lax.div(lane, HD), 4)
    v_lanes = jnp.logical_or(v_lanes == 1, v_lanes == 2)

    def valid_rows(start, size):
        return lax.broadcasted_iota(jnp.int32, (size, 1), 0) + start < real

    wf_load.wait()
    for p in range(pairs):
        at = pl.ds(p * LANES, LANES)
        k_part, v_part = wf[1, :, at], swap(wf[2, :, at].astype(F32)).astype(BF)
        wkv1[:, pl.ds(2 * p * LANES, LANES)] = jnp.where(low, k_part, v_part)
        wkv1[:, pl.ds((2 * p + 1) * LANES, LANES)] = jnp.where(low, v_part, k_part)

    def qkv1(slot, start, size, band):
        n = layer_norm(toks[slot, pl.ds(start, size)].astype(F32), f_gain[...], norm_eps).astype(BF)
        at = pl.ds(pl.multiple_of(band * rows + start, TILE), size)
        q1[at, :] = (mm(n, wf[0]) * QSCALE).astype(BF)
        both = mm(n, wkv1[...]).astype(BF)
        kv1[at, :] = both
        one = jnp.where(v_lanes, both, jnp.ones_like(both))
        vx1[at, :] = jnp.where(valid_rows(start, size), one, jnp.zeros_like(one))

    qkv1(0, 0, rows, place)
    tok_core.wait_recv()
    qkv1(1, 0, rows, 2 * x + 1 - c)
    wg_load.wait()
    for p in range(pairs):
        at = pl.ds(p * LANES, LANES)
        k_part, v_part = wg[1, :, at], wg[2, :, at]
        k_swap, v_swap = swap(k_part.astype(F32)).astype(BF), swap(v_part.astype(F32)).astype(BF)
        wkv2[:, pl.ds(2 * p * LANES, LANES)] = jnp.where(low, k_part, v_swap)
        wkv2[:, pl.ds((2 * p + 1) * LANES, LANES)] = jnp.where(low, k_swap, v_part)
    tok_f = []
    for k, (start, size) in enumerate(parts):
        at = pl.ds(start, size)
        tok_x[k].wait_recv()
        tok_f.append(put("tok_f", k, toks.at[2, at], toks.at[3, at], core))
        qkv1(2, start, size, 2 * (1 - x) + c)
    for k, (start, size) in enumerate(parts):
        tok_f[k].wait_recv()
        qkv1(3, start, size, 2 * (1 - x) + 1 - c)

    att_copies, p_copies, n_copies = [], [], []

    def attend(k):
        j, start, size, _ = steps[k]
        for p in range(pairs):
            at = pl.ds(p * LANES, LANES)
            qp = jnp.concatenate(
                [q1[pl.ds((2 * j + b) * rows + start, size), at] for b in range(2)], axis=0
            )
            mixed = []
            for e in range(2):
                tile = pl.ds((2 * p + e) * LANES, LANES)
                zero = jnp.zeros_like(qp)
                lhs = jnp.where(low, qp, zero) if e == 0 else jnp.where(low, zero, qp)
                scores = dot_t(lhs, kv1[:, tile])
                probs = jnp.exp2(scores - jnp.max(scores, axis=-1, keepdims=True))
                mixed.append(mm(probs.astype(BF), vx1[:, tile]))
            top = jnp.where(low, mixed[1], mixed[0])
            bottom = swap(jnp.where(low, mixed[0], mixed[1]))
            out = (top / bottom).astype(BF)
            for b in range(2):
                att[k, b, pl.ds(0, size), at] = out[b * size : (b + 1) * size]
        at = pl.ds(0, size)
        att_copies.append(put("att", k, att.at[k, 1 - c, at], att_in.at[k, at], core))

    def project(k):
        j, start, size, _ = steps[k]
        at = pl.ds(0, size)
        att_copies[k].wait_recv()
        lhs = jnp.concatenate([att[k, c, at], att_in[k, at]], axis=1)
        partial = mm(lhs, fo[...])
        p_own[k, at] = partial
        p_out[k, at] = partial.astype(BF)
        p_copies.append(put("part", k, p_out.at[k, at], p_in.at[k, at], across))

    def norm2(k):
        j, start, size, _ = steps[k]
        at = pl.ds(0, size)
        slot = jnp.where(x == j, 0, 2)
        p_copies[k].wait_recv()
        tok = toks[slot, pl.ds(start, size)].astype(F32)
        first = (tok + p_own[k, at] + p_in[k, at].astype(F32)).astype(BF)

        @pl.when(x == j)
        def _():
            fst[pl.ds(start, size), :] = first

        n_own[k, at] = layer_norm(first.astype(F32), g_gain[...], norm_eps).astype(BF)
        n_copies.append(put("norm", k, n_own.at[k, at], n_in.at[k, at], core))

    kv_copies, q_copies = [], []
    base_row = pl.multiple_of(z * frame, frame)

    def qkv2(k):
        j, start, size, offset = steps[k]
        n_copies[k].wait_recv()
        at = pl.ds(0, size)
        n = jnp.concatenate([n_own[k, at], n_in[k, at]], axis=0)
        both = mm(n, wkv2[...]).astype(BF)
        for h in range(2 * pairs):
            skv[h, pl.ds(offset, 2 * size), :] = both[:, h * LANES : (h + 1) * LANES]
        to = pl.ds(pl.multiple_of(z * frame + offset, TILE), 2 * size)
        for d in range(1, seq):
            peer = lax.rem(z + d, seq)
            kv_copies.append(
                put("kv", k * seq + d, skv.at[peer, pl.ds(offset, 2 * size)], kv.at[to], z_peer(d))
            )
        kv[to, :] = skv[z, pl.ds(offset, 2 * size), :]
        queries = mm(n, wg[0]) * QSCALE
        q2[2 * j + c, pl.ds(start, size), :] = queries[:size]
        q2[2 * j + 1 - c, pl.ds(start, size), :] = queries[size:]

    for copy in fo_loads:
        copy.wait()
    attend(0)
    attend(1)
    project(0)
    attend(2)
    project(1)
    attend(3)
    project(2)
    project(3)
    go_part = pl.ds(pl.multiple_of(x * 2 * cols + c * cols, cols), cols)
    go_from = pl.ds(pl.multiple_of((1 - x) * 2 * cols + c * cols, cols), cols)
    go_x = put("go", 0, g_out.at[own_cols], go.at[go_part], across)
    norm2(0)
    norm2(1)
    qkv2(0)
    qkv2(1)
    norm2(2)
    norm2(3)
    qkv2(2)
    qkv2(3)
    for b in range(4):
        for p in range(pairs):
            tile = q2[b, :, pl.ds(p * LANES, LANES)]
            top, under = tile[:half], tile[half:]
            sq[2 * p, b] = jnp.where(low, top, swap(under)).astype(BF)
            sq[2 * p + 1, b] = jnp.where(low, swap(top), under).astype(BF)
        for d in range(1, seq):
            peer = lax.rem(z + d, seq)
            q_copies.append(put("q", b * seq + d, sq.at[peer, b], rq.at[z, b], z_peer(d)))
    rq[z] = sq[z]

    frame_valid = jnp.concatenate(
        [valid_rows(start, size) for j, start, size, _ in steps for b in range(2)], axis=0
    )

    def spread(origin):
        at = pl.ds(pl.multiple_of(origin * frame, frame), frame)
        both = kv[at, :]
        one = jnp.where(low, jnp.ones_like(both), both)
        vx[at, :] = jnp.where(frame_valid, one, jnp.zeros_like(one))

    spread(z)
    for d in range(1, seq):
        for k in range(len(steps)):
            kv_copies[k * (seq - 1) + d - 1].wait_recv()
        spread(lax.rem(z + seq - d, seq))

    mine = place * seq + z

    def q_copy(d, b):
        origin = lax.rem(z + seq - d, seq)
        return remote("q", b * seq + d, sq.at[0, b], rq.at[origin, b], z_peer(d))

    def o_copy(d, b):
        origin = lax.rem(z + seq - d, seq)
        device = (s, origin, b // 2, b % 2)
        return remote("o", d * 4 + b, so.at[d, b], ro.at[mine], device, mine)

    def each_o(d, b, act):
        itself = jnp.logical_and(d == 0, place == b)

        @pl.when(jnp.logical_not(itself))
        def _():
            act(o_copy(d, b))

    @pl.loop(0, seq)
    def _(d):
        origin = lax.rem(z + seq - d, seq)
        for b in range(4):

            @pl.when(d > 0)
            def _():
                q_copy(d, b).wait_recv()

        for b in range(4):
            packed = rq[origin, b].astype(F32)
            q = jnp.concatenate([packed, swap(packed)], axis=0)
            q = jnp.where(low, q, 0.0).astype(BF)
            scores = dot_t(q, kv[...])
            probs = jnp.exp2(scores - jnp.max(scores, axis=-1, keepdims=True))
            mixed = mm(probs.astype(BF), vx[...])
            out = mixed / jnp.where(low, 1.0, swap(mixed))
            so[d, b] = jnp.where(low, swap(out)[:half], out[half:]).astype(BF)
            each_o(d, b, lambda copy: copy.start())

    ro_own = so[0, place]
    ro[mine] = ro_own
    go_x.wait_recv()
    go_f = put("go", 1, go.at[go_from], go.at[go_from], core)
    for copy in late_loads:
        copy.wait()
    for slot in range(4 * seq):

        @pl.when(slot != mine)
        def _():
            remote("o", 0, so.at[0, 0], ro.at[slot], core, slot).wait_recv()

    for i in range(2 * seq):
        at = pl.ds(i * LANES, LANES)
        even, odd = ro[2 * i].astype(F32), ro[2 * i + 1].astype(F32)
        pair = [jnp.where(low, even, swap(odd)), jnp.where(low, swap(even), odd)]
        a2[:, at] = jnp.concatenate(pair, axis=0).astype(BF)
    first = fst[...].astype(F32)
    go_f.wait_recv()
    second = (first + mm(a2[...], go[...])).astype(BF).astype(F32)
    stacked = jnp.concatenate([first, second], axis=-1)
    n3 = layer_norm(stacked, h_gain[...], head_eps).astype(BF)
    pj[...] = (mm(n3, wp[...]) + h_bias[...]).astype(BF)

    after = lax.rem(place + 1, 4)
    before = lax.rem(place + 3, 4)

    def frame_peer(index):
        return (s, z, index // 2, lax.rem(index, 2))

    start = (real - width) // TILE * TILE
    slab = halo.shape[1]
    down = put(
        "halo", 0, pj.at[pl.ds(start, rows - start)], halo.at[0, pl.ds(0, rows - start)],
        frame_peer(after),
    )
    upward = put("halo", 1, pj.at[pl.ds(0, slab)], halo.at[1], frame_peer(before))
    stage[0:rows, :] = second
    for r in range(height):
        blocks_ref[0, r] = stage[r * width : (r + 1) * width, :].astype(BF)
    base = 8
    xbuf[...] = jnp.zeros_like(xbuf)
    xbuf[base + width : base + width + real, :] = pj[...].astype(F32)[:real]
    down.wait_recv()
    upward.wait_recv()
    skip = real - width - start
    lower = jnp.where(place > 0, halo[0].astype(F32), 0.0)
    upper = jnp.where(place < 3, halo[1].astype(F32), 0.0)
    xbuf[base : base + width, :] = lower[skip : skip + width]
    xbuf[base + width + real : base + 2 * width + real, :] = upper[:width]
    col = lax.rem(lax.broadcasted_iota(jnp.int32, (rows, 1), 0), width)
    channels = pj.shape[1]
    total = jnp.zeros((rows, channels), F32)
    for i in range(3):
        for j in range(3):
            first_row = base + width * i + j - 1
            window = xbuf[first_row : first_row + rows, :]
            if j == 0:
                window = jnp.where(col > 0, window, 0.0)
            if j == 2:
                window = jnp.where(col < width - 1, window, 0.0)
            total = total + mm(window.astype(BF), wc[3 * i + j])
    stage[0:rows, 0:channels] = total
    for r in range(height):
        feat_ref[0, r] = stage[r * width : (r + 1) * width, 0:channels].astype(BF)

    for copy in started:
        copy.wait_send()

    @pl.loop(0, seq)
    def _(d):
        for b in range(4):
            each_o(d, b, lambda copy: copy.wait_send())


def scene_program(seq, *arrays):
    (tokens, f_gain, f_qkv, f_out, g_gain, g_qkv, g_out, h_gain, h_proj, h_bias, h_conv) = arrays
    height, width, dim = tokens.shape[1:]
    real = height * width
    rows = up(real)
    cols = f_qkv.shape[2] // 2
    pairs = cols // LANES
    channels = h_proj.shape[1]
    frame = 4 * rows
    half = rows // 2
    most = row_parts(rows)[0][1]
    vmem = pl.BlockSpec(memory_space=pltpu.VMEM)
    hbm = pl.BlockSpec(memory_space=pl.ANY)
    start = (real - width) // TILE * TILE
    slab = max(up(width), rows - start)
    _, copies = sem_layout(seq, pairs)
    return pl.pallas_call(
        functools.partial(scene_kernel, seq, height, width),
        out_shape=(
            jax.ShapeDtypeStruct(tokens.shape, BF),
            jax.ShapeDtypeStruct((1, height, width, channels), BF),
        ),
        in_specs=[vmem, vmem, hbm, hbm, vmem, hbm, hbm, vmem, hbm, vmem, hbm],
        out_specs=(vmem, vmem),
        scratch_shapes=[
            pltpu.VMEM((rows, dim), F32),
            pltpu.VMEM((4, rows, dim), BF),
            pltpu.VMEM((3, dim, cols), BF),
            pltpu.VMEM((3, dim, cols), BF),
            pltpu.VMEM((dim, 2 * cols), BF),
            pltpu.VMEM((dim, 2 * cols), BF),
            pltpu.VMEM((2 * cols, dim), BF),
            pltpu.VMEM((4 * cols, dim), BF),
            pltpu.VMEM(h_proj.shape, BF),
            pltpu.VMEM((9, channels, channels), BF),
            pltpu.VMEM((frame, cols), BF),
            pltpu.VMEM((frame, 2 * cols), BF),
            pltpu.VMEM((frame, 2 * cols), BF),
            pltpu.VMEM((4, 2, most, cols), BF),
            pltpu.VMEM((4, most, cols), BF),
            pltpu.VMEM((4, most, dim), F32),
            pltpu.VMEM((4, most, dim), BF),
            pltpu.VMEM((4, most, dim), BF),
            pltpu.VMEM((4, most, dim), BF),
            pltpu.VMEM((4, most, dim), BF),
            pltpu.VMEM((rows, dim), BF),
            pltpu.VMEM((4, rows, cols), F32),
            pltpu.VMEM((seq, frame, LANES), BF),
            pltpu.VMEM((seq * frame, LANES), BF),
            pltpu.VMEM((seq * frame, LANES), BF),
            pltpu.VMEM((seq, 4, half, LANES), BF),
            pltpu.VMEM((seq, 4, half, LANES), BF),
            pltpu.VMEM((seq, 4, half, LANES), BF),
            pltpu.VMEM((4 * seq, half, LANES), BF),
            pltpu.VMEM((rows, 4 * cols), BF),
            pltpu.VMEM((rows, channels), BF),
            pltpu.VMEM((2, slab, channels), BF),
            pltpu.VMEM((up(rows + 2 * width + 2 * TILE), channels), F32),
            pltpu.SemaphoreType.DMA((copies,)),
            pltpu.SemaphoreType.DMA((copies,)),
            pltpu.SemaphoreType.DMA((5 + 4 * pairs,)),
        ],
        compiler_params=pltpu.CompilerParams(collective_id=0, has_side_effects=True),
    )(
        tokens,
        f_gain.reshape(1, -1),
        f_qkv,
        f_out,
        g_gain.reshape(1, -1),
        g_qkv,
        g_out,
        h_gain.reshape(1, -1),
        h_proj,
        h_bias.reshape(1, -1),
        h_conv.reshape(9, channels, channels),
    )


def routed(mesh, *arrays):
    sizes = mesh.shape
    frames, height, width = arrays[0].shape[:3]
    heads = arrays[2].shape[2] // HD
    fits = (
        sizes["head"] == 2
        and sizes["band"] == 2
        and frames == 1
        and heads == 2 * sizes["seq"]
        and sizes["seq"] % 2 == 0
        and arrays[0].shape[3] == 2 * arrays[2].shape[2]
        and arrays[10].shape[2] <= arrays[0].shape[3]
        and height * width >= up(width)
        and up(height * width) >= 2 * TILE
    )
    if fits:
        return scene_program(sizes["seq"], *arrays)
    return on_device(*arrays)


def solution(mesh):
    return jax.shard_map(
        functools.partial(routed, mesh),
        mesh=mesh,
        in_specs=(
            P(("scene", "seq"), ("head", "band"), None, None),
            P(),
            P(None, None, "head"),
            P("head", None),
            P(),
            P(None, None, "head"),
            P("head", None),
            P(),
            P(),
            P(),
            P(),
        ),
        out_specs=(
            P(("scene", "seq"), ("head", "band"), None, None),
            P(("scene", "seq"), ("head", "band"), None, None),
        ),
        check_vma=False,
    )
```

```python
import functools
import math

import jax
import jax.numpy as jnp
from jax import lax
from jax.experimental import pallas as pl
from jax.experimental.pallas import tpu as pltpu
from jax.sharding import PartitionSpec as P

HD = 64


norm_eps = 1e-06
head_eps = 1e-05


def padded_2(block, sides, width):
    for axis, dim in sides:
        count = lax.axis_size(axis)
        forward = [(i, i + 1) for i in range(count - 1)]
        backward = [(target, source) for source, target in forward]
        low = lax.ppermute(
            lax.slice_in_dim(block, block.shape[dim] - width, None, axis=dim), axis, forward
        )
        high = lax.ppermute(lax.slice_in_dim(block, 0, width, axis=dim), axis, backward)
        block = jnp.concatenate([low, block, high], axis=dim)
    return block


def layer_norm(values, gain, epsilon):
    centre = values - jnp.mean(values, axis=-1, keepdims=True)
    spread = jnp.mean(centre * centre, axis=-1, keepdims=True)
    return centre * lax.rsqrt(spread + epsilon) * gain


def by_heads(matrix):
    return matrix.reshape(matrix.shape[0], matrix.shape[1] // HD, HD)


def attend_local(queries, keys_all, values_all):
    scores = jnp.einsum(
        "qhd,khd->qhk", by_heads(queries), by_heads(keys_all), preferred_element_type=jnp.float32
    ) * HD ** (-0.5)
    probs = jnp.exp(scores - jnp.max(scores, axis=-1, keepdims=True))
    mixed = jnp.einsum(
        "qhk,khd->qhd",
        probs.astype(jnp.bfloat16),
        by_heads(values_all),
        preferred_element_type=jnp.float32,
    )
    mixed = mixed / jnp.sum(probs, axis=-1)[..., None]
    return mixed.reshape(queries.shape).astype(jnp.bfloat16)


def key_step(local_rows, portion_rows):
    amount = portion_rows // local_rows
    best = 1
    for factor in range(1, amount + 1):
        if amount % factor == 0 and local_rows * factor <= max(local_rows, 1024):
            best = factor
    return local_rows * best


def fresh_carry(queries):
    heads_q = by_heads(queries)
    return (
        jnp.full(heads_q.shape[:2], -jnp.inf, jnp.float32),
        jnp.zeros(heads_q.shape[:2], jnp.float32),
        jnp.zeros(heads_q.shape, jnp.float32),
    )


def finish(carry, queries):
    return (carry[2] / carry[1][..., None]).reshape(queries.shape).astype(jnp.bfloat16)


def fold_keys(queries, carry, portions, local_rows):
    keys_in, values_in = portions
    step_rows = key_step(local_rows, keys_in.shape[0])
    heads_q = by_heads(queries)
    key_blocks = keys_in.reshape(-1, step_rows, keys_in.shape[1])
    value_blocks = values_in.reshape(-1, step_rows, values_in.shape[1])

    def absorb(states, blocks_pair):
        running_max, running_sum, weighted = states
        scores = jnp.einsum(
            "qhd,khd->qhk", heads_q, by_heads(blocks_pair[0]), preferred_element_type=jnp.float32
        ) * HD ** (-0.5)
        new_max = jnp.maximum(running_max, jnp.max(scores, axis=-1))
        decay = jnp.exp(running_max - new_max)
        probs = jnp.exp(scores - new_max[..., None])
        running_sum = running_sum * decay + jnp.sum(probs, axis=-1)
        weighted = weighted * decay[..., None] + jnp.einsum(
            "qhk,khd->qhd",
            probs.astype(jnp.bfloat16),
            by_heads(blocks_pair[1]),
            preferred_element_type=jnp.float32,
        )
        return ((new_max, running_sum, weighted), None)

    carry, ignored = lax.scan(absorb, carry, (key_blocks, value_blocks))
    return carry


def attention_block(inputs, gain, qkv_weight, out_weight, wide):
    normed = layer_norm(inputs.astype(jnp.float32), gain, norm_eps).astype(jnp.bfloat16)
    gathered = lax.all_gather(normed, "head", axis=1, tiled=True)
    flattened = gathered.reshape(-1, gathered.shape[-1])
    query_rows = jnp.dot(flattened, qkv_weight[0], preferred_element_type=jnp.float32).astype(
        jnp.bfloat16
    )
    key_rows = jnp.dot(flattened, qkv_weight[1], preferred_element_type=jnp.float32).astype(
        jnp.bfloat16
    )
    value_rows = jnp.dot(flattened, qkv_weight[2], preferred_element_type=jnp.float32).astype(
        jnp.bfloat16
    )
    if wide:
        carry = fold_keys(
            query_rows,
            fresh_carry(query_rows),
            (
                lax.all_gather(key_rows, ("seq", "band"), axis=0, tiled=True),
                lax.all_gather(value_rows, ("seq", "band"), axis=0, tiled=True),
            ),
            key_rows.shape[0],
        )
        attended = finish(carry, query_rows)
    else:
        keys_all, values_all = (
            lax.all_gather(key_rows, "band", axis=0, tiled=True),
            lax.all_gather(value_rows, "band", axis=0, tiled=True),
        )
        attended = attend_local(query_rows, keys_all, values_all)
    band_rows = inputs.shape[1] * inputs.shape[2]
    own_rows = lax.all_to_all(attended, "head", split_axis=0, concat_axis=1, tiled=True)
    branch = jnp.dot(
        own_rows,
        lax.all_gather(out_weight, "head", axis=0, tiled=True),
        preferred_element_type=jnp.float32,
    )
    merged = inputs.astype(jnp.float32).reshape(band_rows, -1) + branch
    return merged.astype(jnp.bfloat16).reshape(inputs.shape)


def on_device(
    tokens,
    frame_gain,
    frame_qkv,
    frame_out,
    global_gain,
    global_qkv,
    global_out,
    head_gain,
    head_proj,
    head_bias,
    head_conv,
):
    first = attention_block(tokens, frame_gain, frame_qkv, frame_out, False)
    second = attention_block(first, global_gain, global_qkv, global_out, True)
    band_height = tokens.shape[1]
    grid_width = tokens.shape[2]
    stacked = jnp.concatenate([first.astype(jnp.float32), second.astype(jnp.float32)], axis=-1)
    normed = layer_norm(stacked, head_gain, head_eps).astype(jnp.bfloat16)
    projected = (
        jnp.dot(
            normed.reshape(-1, stacked.shape[-1]), head_proj, preferred_element_type=jnp.float32
        )
        + head_bias
    )
    projected = projected.astype(jnp.bfloat16).reshape(
        tokens.shape[0], band_height, grid_width, head_proj.shape[1]
    )
    padded = padded_2(projected, ((("head", "band"), 1),), 1)
    padded = jnp.pad(padded, ((0, 0), (0, 0), (1, 1), (0, 0)))
    totals = jnp.zeros(projected.shape, jnp.float32)
    for offset_row in range(3):
        for offset_col in range(3):
            window = padded[
                :, offset_row : offset_row + band_height, offset_col : offset_col + grid_width
            ]
            totals = totals + jnp.einsum(
                "frcx,xy->frcy",
                window,
                head_conv[offset_row, offset_col],
                preferred_element_type=jnp.float32,
            )
    return (second, totals.astype(jnp.bfloat16))


BF = jnp.bfloat16
F32 = jnp.float32
TILE = 16
LANES = 2 * HD
QSCALE = HD ** (-0.5) * math.log2(math.e)


def up(count):
    return -(-count // TILE) * TILE


def mm(a, b):
    return jnp.dot(a, b, preferred_element_type=F32)


def swap(values):
    return pltpu.roll(values, HD, axis=1)


def dot_t(a, b):
    return lax.dot_general(a, b, (((1,), (1,)), ((), ())), preferred_element_type=F32)


def row_parts(rows):
    first = up(rows // 2)
    return [(0, first), (first, rows - first)]


def step_list(rows):
    steps, at = [], 0
    for j in range(2):
        for start, size in row_parts(rows):
            steps.append((j, start, size, at))
            at += 2 * size
    return steps


def sem_layout(seq, pairs):
    names = [
        ("tok", 1), ("tok_x", 2), ("tok_f", 2), ("att", 4), ("part", 4), ("norm", 4),
        ("kv", 4 * seq), ("q", 4 * seq), ("o", 4 * seq), ("go", 2), ("halo", 2),
    ]
    at, table = 0, {}
    for name, size in names:
        table[name] = at
        at += size
    return table, at


def scene_kernel(
    seq,
    height,
    width,
    tok_hbm,
    f_gain_hbm,
    f_qkv,
    f_out,
    g_gain_hbm,
    g_qkv,
    g_out,
    h_gain_hbm,
    h_proj,
    h_bias_hbm,
    h_conv,
    blocks_ref,
    feat_ref,
    tok_ref,
    f_gain,
    g_gain,
    h_gain,
    h_bias,
    stage,
    toks,
    wf,
    wg,
    wkv1,
    wkv2,
    fo,
    go,
    wp,
    wc,
    q1,
    kv1,
    vx1,
    att,
    att_in,
    p_own,
    p_out,
    p_in,
    n_own,
    n_in,
    fst,
    q2,
    skv,
    kv,
    vx,
    sq,
    rq,
    so,
    ro,
    a2,
    pj,
    halo,
    xbuf,
    send,
    recv,
    local,
):
    s, z = lax.axis_index("scene"), lax.axis_index("seq")
    x, c = lax.axis_index("head"), lax.axis_index("band")
    real = height * width
    rows, dim = fst.shape
    cols = wf.shape[2]
    pairs = cols // LANES
    frame = 4 * rows
    half = rows // 2
    steps = step_list(rows)
    parts = row_parts(rows)
    sems, _ = sem_layout(seq, pairs)
    core, across = (s, z, x, 1 - c), (s, z, 1 - x, c)
    place = 2 * x + c

    def paired(k):
        bits = [1 << i for i in range(seq.bit_length()) if k >> i & 1]
        return z + sum(bit - 2 * bit * lax.rem(lax.div(z, bit), 2) for bit in bits)

    def z_peer(k):
        return (s, paired(k), x, c)

    def remote(name, index, source, target, device, back=None):
        return pltpu.make_async_remote_copy(
            src_ref=source,
            dst_ref=target,
            send_sem=send.at[sems[name] + index],
            recv_sem=recv.at[sems[name] + (index if back is None else back)],
            device_id=device,
            device_id_type=pl.DeviceIdType.MESH,
        )

    barrier = pltpu.get_barrier_semaphore()
    everyone = [core, across, (s, z, 1 - x, 1 - c)] + [z_peer(d) for d in range(1, seq)]
    for device in everyone:
        pl.semaphore_signal(
            barrier, inc=1, device_id=device, device_id_type=pl.DeviceIdType.MESH
        )

    started = []

    def put(name, index, source, target, device):
        copy = remote(name, index, source, target, device)
        copy.start()
        started.append(copy)
        return copy

    own_cols = pl.ds(pl.multiple_of(c * cols, cols), cols)
    loads = []

    def load(source, target):
        copy = pltpu.make_async_copy(source, target, local.at[len(loads)])
        copy.start()
        loads.append(copy)
        return copy

    tok_load = load(tok_hbm, tok_ref)
    f_gain_load = load(f_gain_hbm, f_gain)
    wf_load = load(f_qkv.at[:, :, own_cols], wf)
    fo_loads = []
    for r in range(2):
        owner = c if r == 0 else 1 - c
        for i in range(2 * pairs):
            source = f_out.at[pl.ds(pl.multiple_of(owner * cols + i * HD, HD), HD)]
            fo_loads.append(load(source, fo.at[pl.ds(r * cols + (i ^ 1) * HD, HD)]))
    wg_load = load(g_qkv.at[:, :, own_cols], wg)
    half_rows = pl.ds(pl.multiple_of(x * 2 * cols, 2 * cols), 2 * cols)
    g_gain_load = load(g_gain_hbm, g_gain)
    late_loads = [load(g_out, go.at[half_rows]), load(h_proj, wp), load(h_conv, wc)]
    late_loads += [load(h_gain_hbm, h_gain), load(h_bias_hbm, h_bias)]

    tok_load.wait()
    for r in range(height):
        stage[r * width : (r + 1) * width, :] = tok_ref[0, r].astype(F32)
    for r in range(real, rows):
        stage[r : r + 1, :] = stage[real - 1 : real, :]
    toks[0] = stage[0:rows, :].astype(BF)
    pl.semaphore_wait(barrier, len(everyone))

    tok_x = []
    for k, (start, size) in enumerate(parts):
        at = pl.ds(start, size)
        tok_x.append(put("tok_x", k, toks.at[0, at], toks.at[2, at], across))
    tok_core = put("tok", 0, toks.at[0], toks.at[1], core)

    low = lax.broadcasted_iota(jnp.int32, (1, LANES), 1) < HD
    lane = lax.broadcasted_iota(jnp.int32, (1, 2 * cols), 1)
    v_lanes = lax.rem(lax.div(lane, HD), 4)
    v_lanes = jnp.logical_or(v_lanes == 1, v_lanes == 2)

    def valid_rows(start, size):
        return lax.broadcasted_iota(jnp.int32, (size, 1), 0) + start < real

    f_gain_load.wait()
    wf_load.wait()
    for p in range(pairs):
        at = pl.ds(p * LANES, LANES)
        k_part, v_part = wf[1, :, at], swap(wf[2, :, at].astype(F32)).astype(BF)
        wkv1[:, pl.ds(2 * p * LANES, LANES)] = jnp.where(low, k_part, v_part)
        wkv1[:, pl.ds((2 * p + 1) * LANES, LANES)] = jnp.where(low, v_part, k_part)

    def qkv1(slot, start, size, band):
        n = layer_norm(toks[slot, pl.ds(start, size)].astype(F32), f_gain[...], norm_eps).astype(BF)
        at = pl.ds(pl.multiple_of(band * rows + start, TILE), size)
        q1[at, :] = (mm(n, wf[0]) * QSCALE).astype(BF)
        both = mm(n, wkv1[...]).astype(BF)
        kv1[at, :] = both
        one = jnp.where(v_lanes, both, jnp.ones_like(both))
        vx1[at, :] = jnp.where(valid_rows(start, size), one, jnp.zeros_like(one))

    qkv1(0, 0, rows, place)
    tok_core.wait_recv()
    qkv1(1, 0, rows, 2 * x + 1 - c)
    g_gain_load.wait()
    wg_load.wait()
    for p in range(pairs):
        at = pl.ds(p * LANES, LANES)
        k_part, v_part = wg[1, :, at], wg[2, :, at]
        k_swap, v_swap = swap(k_part.astype(F32)).astype(BF), swap(v_part.astype(F32)).astype(BF)
        wkv2[:, pl.ds(2 * p * LANES, LANES)] = jnp.where(low, k_part, v_swap)
        wkv2[:, pl.ds((2 * p + 1) * LANES, LANES)] = jnp.where(low, k_swap, v_part)
    tok_f = []
    for k, (start, size) in enumerate(parts):
        at = pl.ds(start, size)
        tok_x[k].wait_recv()
        tok_f.append(put("tok_f", k, toks.at[2, at], toks.at[3, at], core))
        qkv1(2, start, size, 2 * (1 - x) + c)
    for k, (start, size) in enumerate(parts):
        tok_f[k].wait_recv()
        qkv1(3, start, size, 2 * (1 - x) + 1 - c)

    att_copies, p_copies, n_copies = [], [], []

    def attend(k):
        j, start, size, _ = steps[k]
        for p in range(pairs):
            at = pl.ds(p * LANES, LANES)
            qp = jnp.concatenate(
                [q1[pl.ds((2 * j + b) * rows + start, size), at] for b in range(2)], axis=0
            )
            mixed = []
            for e in range(2):
                tile = pl.ds((2 * p + e) * LANES, LANES)
                zero = jnp.zeros_like(qp)
                lhs = jnp.where(low, qp, zero) if e == 0 else jnp.where(low, zero, qp)
                scores = dot_t(lhs, kv1[:, tile])
                probs = jnp.exp2(scores - jnp.max(scores, axis=-1, keepdims=True))
                mixed.append(mm(probs.astype(BF), vx1[:, tile]))
            top = jnp.where(low, mixed[1], mixed[0])
            bottom = swap(jnp.where(low, mixed[0], mixed[1]))
            out = (top / bottom).astype(BF)
            for b in range(2):
                att[k, b, pl.ds(0, size), at] = out[b * size : (b + 1) * size]
        at = pl.ds(0, size)
        att_copies.append(put("att", k, att.at[k, 1 - c, at], att_in.at[k, at], core))

    def project(k):
        j, start, size, _ = steps[k]
        at = pl.ds(0, size)
        att_copies[k].wait_recv()
        lhs = jnp.concatenate([att[k, c, at], att_in[k, at]], axis=1)
        partial = mm(lhs, fo[...])
        p_own[k, at] = partial
        p_out[k, at] = partial.astype(BF)
        p_copies.append(put("part", k, p_out.at[k, at], p_in.at[k, at], across))

    def norm2(k):
        j, start, size, _ = steps[k]
        at = pl.ds(0, size)
        slot = jnp.where(x == j, 0, 2)
        p_copies[k].wait_recv()
        tok = toks[slot, pl.ds(start, size)].astype(F32)
        first = (tok + p_own[k, at] + p_in[k, at].astype(F32)).astype(BF)

        @pl.when(x == j)
        def _():
            fst[pl.ds(start, size), :] = first

        n_own[k, at] = layer_norm(first.astype(F32), g_gain[...], norm_eps).astype(BF)
        n_copies.append(put("norm", k, n_own.at[k, at], n_in.at[k, at], core))

    kv_copies = [[] for _ in range(seq)]

    def qkv2(k):
        j, start, size, offset = steps[k]
        n_copies[k].wait_recv()
        at = pl.ds(0, size)
        n = jnp.concatenate([n_own[k, at], n_in[k, at]], axis=0)
        both = mm(n, wkv2[...]).astype(BF)
        for h in range(2 * pairs):
            skv[h, pl.ds(offset, 2 * size), :] = both[:, h * LANES : (h + 1) * LANES]
        to = pl.ds(pl.multiple_of(z * frame + offset, TILE), 2 * size)
        for d in reversed(range(1, seq)):
            source = skv.at[paired(d), pl.ds(offset, 2 * size)]
            kv_copies[d].append(put("kv", k * seq + d, source, kv.at[to], z_peer(d)))
        kv[to, :] = skv[z, pl.ds(offset, 2 * size), :]
        queries = mm(n, wg[0]) * QSCALE
        q2[2 * j + c, pl.ds(start, size), :] = queries[:size]
        q2[2 * j + 1 - c, pl.ds(start, size), :] = queries[size:]

    for copy in fo_loads:
        copy.wait()
    attend(0)
    project(0)
    for k in range(1, len(steps)):
        attend(k)
        project(k)
    go_part = pl.ds(pl.multiple_of(x * 2 * cols + c * cols, cols), cols)
    go_from = pl.ds(pl.multiple_of((1 - x) * 2 * cols + c * cols, cols), cols)
    go_x = put("go", 0, g_out.at[own_cols], go.at[go_part], across)
    for k in range(len(steps)):
        norm2(k)
        qkv2(k)
    for b in range(4):
        for p in range(pairs):
            tile = q2[b, :, pl.ds(p * LANES, LANES)]
            top, under = tile[:half], tile[half:]
            sq[2 * p, b] = jnp.where(low, top, swap(under)).astype(BF)
            sq[2 * p + 1, b] = jnp.where(low, swap(top), under).astype(BF)
    for d in range(1, seq):
        for b in range(4):
            put("q", b * seq + d, sq.at[paired(d), b], rq.at[z, b], z_peer(d))
    rq[z] = sq[z]

    frame_valid = jnp.concatenate(
        [valid_rows(start, size) for j, start, size, _ in steps for b in range(2)], axis=0
    )

    def spread(origin):
        at = pl.ds(pl.multiple_of(origin * frame, frame), frame)
        both = kv[at, :]
        one = jnp.where(low, jnp.ones_like(both), both)
        vx[at, :] = jnp.where(frame_valid, one, jnp.zeros_like(one))

    spread(z)
    for d in range(1, seq):
        for copy in kv_copies[d]:
            copy.wait_recv()
        spread(paired(d))

    mine = place * seq + z

    def q_copy(d, b, origin):
        device = (s, origin, x, c)
        return remote("q", b * seq + d, sq.at[0, b], rq.at[origin, b], device)

    def o_copy(d, b, origin):
        device = (s, origin, b // 2, b % 2)
        return remote("o", d * 4 + b, so.at[d, b], ro.at[mine], device, mine)

    def origin_of(d):
        origin = z
        for i in range((seq - 1).bit_length()):
            bit = 1 << i
            flip = lax.rem(lax.div(d, bit), 2)
            origin = origin + flip * (bit - 2 * bit * lax.rem(lax.div(z, bit), 2))
        return origin

    def each_o(d, b, origin, act):
        itself = jnp.logical_and(d == 0, place == b)

        @pl.when(jnp.logical_not(itself))
        def _():
            act(o_copy(d, b, origin))

    @pl.loop(0, seq)
    def _(d):
        origin = origin_of(d)
        for b in range(4):

            @pl.when(d > 0)
            def _():
                q_copy(d, b, origin).wait_recv()

        for pair in range(2):
            q = []
            for b in (2 * pair, 2 * pair + 1):
                packed = rq[origin, b].astype(F32)
                q += [packed, swap(packed)]
            q = jnp.where(low, jnp.concatenate(q, axis=0), 0.0).astype(BF)
            scores = dot_t(q, kv[...])
            probs = jnp.exp2(scores - jnp.max(scores, axis=-1, keepdims=True))
            mixed = mm(probs.astype(BF), vx[...])
            out = mixed / jnp.where(low, 1.0, swap(mixed))
            for i in range(2):
                b = 2 * pair + i
                o = out[i * rows : (i + 1) * rows]
                so[d, b] = jnp.where(low, swap(o)[:half], o[half:]).astype(BF)
                each_o(d, b, origin, lambda copy: copy.start())

    ro_own = so[0, place]
    ro[mine] = ro_own
    go_x.wait_recv()
    go_f = put("go", 1, go.at[go_from], go.at[go_from], core)
    for copy in late_loads:
        copy.wait()
    for slot in range(4 * seq):

        @pl.when(slot != mine)
        def _():
            remote("o", 0, so.at[0, 0], ro.at[slot], core, slot).wait_recv()

    for i in range(2 * seq):
        at = pl.ds(i * LANES, LANES)
        even, odd = ro[2 * i].astype(F32), ro[2 * i + 1].astype(F32)
        pair = [jnp.where(low, even, swap(odd)), jnp.where(low, swap(even), odd)]
        a2[:, at] = jnp.concatenate(pair, axis=0).astype(BF)
    first = fst[...].astype(F32)
    go_f.wait_recv()
    second = (first + mm(a2[...], go[...])).astype(BF).astype(F32)
    stacked = jnp.concatenate([first, second], axis=-1)
    n3 = layer_norm(stacked, h_gain[...], head_eps).astype(BF)
    pj[...] = (mm(n3, wp[...]) + h_bias[...]).astype(BF)

    after = lax.rem(place + 1, 4)
    before = lax.rem(place + 3, 4)

    def frame_peer(index):
        return (s, z, index // 2, lax.rem(index, 2))

    start = (real - width) // TILE * TILE
    slab = halo.shape[1]
    down = put(
        "halo", 0, pj.at[pl.ds(start, rows - start)], halo.at[0, pl.ds(0, rows - start)],
        frame_peer(after),
    )
    upward = put("halo", 1, pj.at[pl.ds(0, slab)], halo.at[1], frame_peer(before))
    stage[0:rows, :] = second
    for r in range(height):
        blocks_ref[0, r] = stage[r * width : (r + 1) * width, :].astype(BF)
    base = 8
    xbuf[...] = jnp.zeros_like(xbuf)
    xbuf[base + width : base + width + real, :] = pj[...].astype(F32)[:real]
    down.wait_recv()
    upward.wait_recv()
    skip = real - width - start
    lower = jnp.where(place > 0, halo[0].astype(F32), 0.0)
    upper = jnp.where(place < 3, halo[1].astype(F32), 0.0)
    xbuf[base : base + width, :] = lower[skip : skip + width]
    xbuf[base + width + real : base + 2 * width + real, :] = upper[:width]
    col = lax.rem(lax.broadcasted_iota(jnp.int32, (rows, 1), 0), width)
    channels = pj.shape[1]
    total = jnp.zeros((rows, channels), F32)
    for i in range(3):
        for j in range(3):
            first_row = base + width * i + j - 1
            window = xbuf[first_row : first_row + rows, :]
            if j == 0:
                window = jnp.where(col > 0, window, 0.0)
            if j == 2:
                window = jnp.where(col < width - 1, window, 0.0)
            total = total + mm(window.astype(BF), wc[3 * i + j])
    stage[0:rows, 0:channels] = total
    for r in range(height):
        feat_ref[0, r] = stage[r * width : (r + 1) * width, 0:channels].astype(BF)

    for copy in started:
        copy.wait_send()

    @pl.loop(0, seq)
    def _(d):
        for b in range(4):
            each_o(d, b, origin_of(d), lambda copy: copy.wait_send())


def scene_program(seq, *arrays):
    (tokens, f_gain, f_qkv, f_out, g_gain, g_qkv, g_out, h_gain, h_proj, h_bias, h_conv) = arrays
    height, width, dim = tokens.shape[1:]
    real = height * width
    rows = up(real)
    cols = f_qkv.shape[2] // 2
    pairs = cols // LANES
    channels = h_proj.shape[1]
    frame = 4 * rows
    half = rows // 2
    most = row_parts(rows)[0][1]
    vmem = pl.BlockSpec(memory_space=pltpu.VMEM)
    hbm = pl.BlockSpec(memory_space=pltpu.HBM)
    start = (real - width) // TILE * TILE
    slab = max(up(width), rows - start)
    _, copies = sem_layout(seq, pairs)
    return pl.pallas_call(
        functools.partial(scene_kernel, seq, height, width),
        out_shape=(
            jax.ShapeDtypeStruct(tokens.shape, BF),
            jax.ShapeDtypeStruct((1, height, width, channels), BF),
        ),
        in_specs=[hbm] * 11,
        out_specs=(vmem, vmem),
        scratch_shapes=[
            pltpu.VMEM(tokens.shape, BF),
            pltpu.VMEM((1, dim), F32),
            pltpu.VMEM((1, dim), F32),
            pltpu.VMEM((1, 2 * dim), F32),
            pltpu.VMEM((1, channels), F32),
            pltpu.VMEM((rows, dim), F32),
            pltpu.VMEM((4, rows, dim), BF),
            pltpu.VMEM((3, dim, cols), BF),
            pltpu.VMEM((3, dim, cols), BF),
            pltpu.VMEM((dim, 2 * cols), BF),
            pltpu.VMEM((dim, 2 * cols), BF),
            pltpu.VMEM((2 * cols, dim), BF),
            pltpu.VMEM((4 * cols, dim), BF),
            pltpu.VMEM(h_proj.shape, BF),
            pltpu.VMEM((9, channels, channels), BF),
            pltpu.VMEM((frame, cols), BF),
            pltpu.VMEM((frame, 2 * cols), BF),
            pltpu.VMEM((frame, 2 * cols), BF),
            pltpu.VMEM((4, 2, most, cols), BF),
            pltpu.VMEM((4, most, cols), BF),
            pltpu.VMEM((4, most, dim), F32),
            pltpu.VMEM((4, most, dim), BF),
            pltpu.VMEM((4, most, dim), BF),
            pltpu.VMEM((4, most, dim), BF),
            pltpu.VMEM((4, most, dim), BF),
            pltpu.VMEM((rows, dim), BF),
            pltpu.VMEM((4, rows, cols), F32),
            pltpu.VMEM((seq, frame, LANES), BF),
            pltpu.VMEM((seq * frame, LANES), BF),
            pltpu.VMEM((seq * frame, LANES), BF),
            pltpu.VMEM((seq, 4, half, LANES), BF),
            pltpu.VMEM((seq, 4, half, LANES), BF),
            pltpu.VMEM((seq, 4, half, LANES), BF),
            pltpu.VMEM((4 * seq, half, LANES), BF),
            pltpu.VMEM((rows, 4 * cols), BF),
            pltpu.VMEM((rows, channels), BF),
            pltpu.VMEM((2, slab, channels), BF),
            pltpu.VMEM((up(rows + 2 * width + 2 * TILE), channels), F32),
            pltpu.SemaphoreType.DMA((copies,)),
            pltpu.SemaphoreType.DMA((copies,)),
            pltpu.SemaphoreType.DMA((10 + 4 * pairs,)),
        ],
        compiler_params=pltpu.CompilerParams(
            collective_id=0, has_side_effects=True, vmem_limit_bytes=40 * 2**20
        ),
    )(
        *[
            pltpu.with_memory_space_constraint(array, pltpu.HBM)
            for array in (
                tokens,
                f_gain.reshape(1, -1),
                f_qkv,
                f_out,
                g_gain.reshape(1, -1),
                g_qkv,
                g_out,
                h_gain.reshape(1, -1),
                h_proj,
                h_bias.reshape(1, -1),
                h_conv.reshape(9, channels, channels),
            )
        ]
    )


def routed(mesh, *arrays):
    sizes = mesh.shape
    frames, height, width = arrays[0].shape[:3]
    heads = arrays[2].shape[2] // HD
    fits = (
        sizes["head"] == 2
        and sizes["band"] == 2
        and frames == 1
        and heads == 2 * sizes["seq"]
        and sizes["seq"] & (sizes["seq"] - 1) == 0
        and sizes["seq"] >= 2
        and arrays[0].shape[3] == 2 * arrays[2].shape[2]
        and arrays[10].shape[2] <= arrays[0].shape[3]
        and height * width >= up(width)
        and up(height * width) >= 2 * TILE
    )
    if fits:
        return scene_program(sizes["seq"], *arrays)
    return on_device(*arrays)


def solution(mesh):
    return jax.shard_map(
        functools.partial(routed, mesh),
        mesh=mesh,
        in_specs=(
            P(("scene", "seq"), ("head", "band"), None, None),
            P(),
            P(None, None, "head"),
            P("head", None),
            P(),
            P(None, None, "head"),
            P("head", None),
            P(),
            P(),
            P(),
            P(),
        ),
        out_specs=(
            P(("scene", "seq"), ("head", "band"), None, None),
            P(("scene", "seq"), ("head", "band"), None, None),
        ),
        check_vma=False,
    )
```

```python
import functools
import math

import jax
import jax.numpy as jnp
from jax import lax
from jax.experimental import pallas as pl
from jax.experimental.pallas import tpu as pltpu
from jax.sharding import PartitionSpec as P

HD = 64


norm_eps = 1e-06
head_eps = 1e-05


def padded_2(block, sides, width):
    for axis, dim in sides:
        count = lax.axis_size(axis)
        forward = [(i, i + 1) for i in range(count - 1)]
        backward = [(target, source) for source, target in forward]
        low = lax.ppermute(
            lax.slice_in_dim(block, block.shape[dim] - width, None, axis=dim), axis, forward
        )
        high = lax.ppermute(lax.slice_in_dim(block, 0, width, axis=dim), axis, backward)
        block = jnp.concatenate([low, block, high], axis=dim)
    return block


def layer_norm(values, gain, epsilon):
    centre = values - jnp.mean(values, axis=-1, keepdims=True)
    spread = jnp.mean(centre * centre, axis=-1, keepdims=True)
    return centre * lax.rsqrt(spread + epsilon) * gain


def by_heads(matrix):
    return matrix.reshape(matrix.shape[0], matrix.shape[1] // HD, HD)


def attend_local(queries, keys_all, values_all):
    scores = jnp.einsum(
        "qhd,khd->qhk", by_heads(queries), by_heads(keys_all), preferred_element_type=jnp.float32
    ) * HD ** (-0.5)
    probs = jnp.exp(scores - jnp.max(scores, axis=-1, keepdims=True))
    mixed = jnp.einsum(
        "qhk,khd->qhd",
        probs.astype(jnp.bfloat16),
        by_heads(values_all),
        preferred_element_type=jnp.float32,
    )
    mixed = mixed / jnp.sum(probs, axis=-1)[..., None]
    return mixed.reshape(queries.shape).astype(jnp.bfloat16)


def key_step(local_rows, portion_rows):
    amount = portion_rows // local_rows
    best = 1
    for factor in range(1, amount + 1):
        if amount % factor == 0 and local_rows * factor <= max(local_rows, 1024):
            best = factor
    return local_rows * best


def fresh_carry(queries):
    heads_q = by_heads(queries)
    return (
        jnp.full(heads_q.shape[:2], -jnp.inf, jnp.float32),
        jnp.zeros(heads_q.shape[:2], jnp.float32),
        jnp.zeros(heads_q.shape, jnp.float32),
    )


def finish(carry, queries):
    return (carry[2] / carry[1][..., None]).reshape(queries.shape).astype(jnp.bfloat16)


def fold_keys(queries, carry, portions, local_rows):
    keys_in, values_in = portions
    step_rows = key_step(local_rows, keys_in.shape[0])
    heads_q = by_heads(queries)
    key_blocks = keys_in.reshape(-1, step_rows, keys_in.shape[1])
    value_blocks = values_in.reshape(-1, step_rows, values_in.shape[1])

    def absorb(states, blocks_pair):
        running_max, running_sum, weighted = states
        scores = jnp.einsum(
            "qhd,khd->qhk", heads_q, by_heads(blocks_pair[0]), preferred_element_type=jnp.float32
        ) * HD ** (-0.5)
        new_max = jnp.maximum(running_max, jnp.max(scores, axis=-1))
        decay = jnp.exp(running_max - new_max)
        probs = jnp.exp(scores - new_max[..., None])
        running_sum = running_sum * decay + jnp.sum(probs, axis=-1)
        weighted = weighted * decay[..., None] + jnp.einsum(
            "qhk,khd->qhd",
            probs.astype(jnp.bfloat16),
            by_heads(blocks_pair[1]),
            preferred_element_type=jnp.float32,
        )
        return ((new_max, running_sum, weighted), None)

    carry, ignored = lax.scan(absorb, carry, (key_blocks, value_blocks))
    return carry


def attention_block(inputs, gain, qkv_weight, out_weight, wide):
    normed = layer_norm(inputs.astype(jnp.float32), gain, norm_eps).astype(jnp.bfloat16)
    gathered = lax.all_gather(normed, "head", axis=1, tiled=True)
    flattened = gathered.reshape(-1, gathered.shape[-1])
    query_rows = jnp.dot(flattened, qkv_weight[0], preferred_element_type=jnp.float32).astype(
        jnp.bfloat16
    )
    key_rows = jnp.dot(flattened, qkv_weight[1], preferred_element_type=jnp.float32).astype(
        jnp.bfloat16
    )
    value_rows = jnp.dot(flattened, qkv_weight[2], preferred_element_type=jnp.float32).astype(
        jnp.bfloat16
    )
    if wide:
        carry = fold_keys(
            query_rows,
            fresh_carry(query_rows),
            (
                lax.all_gather(key_rows, ("seq", "band"), axis=0, tiled=True),
                lax.all_gather(value_rows, ("seq", "band"), axis=0, tiled=True),
            ),
            key_rows.shape[0],
        )
        attended = finish(carry, query_rows)
    else:
        keys_all, values_all = (
            lax.all_gather(key_rows, "band", axis=0, tiled=True),
            lax.all_gather(value_rows, "band", axis=0, tiled=True),
        )
        attended = attend_local(query_rows, keys_all, values_all)
    band_rows = inputs.shape[1] * inputs.shape[2]
    own_rows = lax.all_to_all(attended, "head", split_axis=0, concat_axis=1, tiled=True)
    branch = jnp.dot(
        own_rows,
        lax.all_gather(out_weight, "head", axis=0, tiled=True),
        preferred_element_type=jnp.float32,
    )
    merged = inputs.astype(jnp.float32).reshape(band_rows, -1) + branch
    return merged.astype(jnp.bfloat16).reshape(inputs.shape)


def on_device(
    tokens,
    frame_gain,
    frame_qkv,
    frame_out,
    global_gain,
    global_qkv,
    global_out,
    head_gain,
    head_proj,
    head_bias,
    head_conv,
):
    first = attention_block(tokens, frame_gain, frame_qkv, frame_out, False)
    second = attention_block(first, global_gain, global_qkv, global_out, True)
    band_height = tokens.shape[1]
    grid_width = tokens.shape[2]
    stacked = jnp.concatenate([first.astype(jnp.float32), second.astype(jnp.float32)], axis=-1)
    normed = layer_norm(stacked, head_gain, head_eps).astype(jnp.bfloat16)
    projected = (
        jnp.dot(
            normed.reshape(-1, stacked.shape[-1]), head_proj, preferred_element_type=jnp.float32
        )
        + head_bias
    )
    projected = projected.astype(jnp.bfloat16).reshape(
        tokens.shape[0], band_height, grid_width, head_proj.shape[1]
    )
    padded = padded_2(projected, ((("head", "band"), 1),), 1)
    padded = jnp.pad(padded, ((0, 0), (0, 0), (1, 1), (0, 0)))
    totals = jnp.zeros(projected.shape, jnp.float32)
    for offset_row in range(3):
        for offset_col in range(3):
            window = padded[
                :, offset_row : offset_row + band_height, offset_col : offset_col + grid_width
            ]
            totals = totals + jnp.einsum(
                "frcx,xy->frcy",
                window,
                head_conv[offset_row, offset_col],
                preferred_element_type=jnp.float32,
            )
    return (second, totals.astype(jnp.bfloat16))


BF = jnp.bfloat16
F32 = jnp.float32
TILE = 16
LANES = 2 * HD
QSCALE = HD ** (-0.5) * math.log2(math.e)


def up(count):
    return -(-count // TILE) * TILE


def mm(a, b):
    return jnp.dot(a, b, preferred_element_type=F32)


def swap(values):
    return pltpu.roll(values, HD, axis=1)


def dot_t(a, b):
    return lax.dot_general(a, b, (((1,), (1,)), ((), ())), preferred_element_type=F32)


def row_parts(rows):
    first = up(rows // 2)
    return [(0, first), (first, rows - first)]


def step_list(rows):
    steps, at = [], 0
    for j in range(2):
        long, short = (size for _, size in row_parts(rows))
        for start, size in [(0, short), (short, long)] if j == 0 else [(0, long), (long, short)]:
            steps.append((j, start, size, at))
            at += 2 * size
    return steps


def sem_layout(seq, pairs):
    names = [
        ("tok", 1), ("tok_x", 2), ("tok_f", 2), ("att", 4), ("part", 4), ("norm", 4),
        ("kv", 4 * seq), ("q", 4 * seq), ("o", 4 * seq), ("go", 2), ("halo", 2),
    ]
    at, table = 0, {}
    for name, size in names:
        table[name] = at
        at += size
    return table, at


def scene_kernel(
    seq,
    height,
    width,
    tok_hbm,
    f_gain_hbm,
    f_qkv,
    f_out,
    g_gain_hbm,
    g_qkv,
    g_out,
    h_gain_hbm,
    h_proj,
    h_bias_hbm,
    h_conv,
    blocks_ref,
    feat_ref,
    tok_ref,
    f_gain,
    g_gain,
    h_gain,
    h_bias,
    stage,
    toks,
    wf,
    wg,
    wkv1,
    wkv2,
    fo,
    go,
    wp,
    wc,
    q1,
    kv1,
    vx1,
    att,
    att_in,
    p_own,
    p_out,
    p_in,
    n_own,
    n_in,
    fst,
    q2,
    skv,
    kv,
    vx,
    sq,
    rq,
    so,
    ro,
    a2,
    pj,
    halo,
    xbuf,
    send,
    recv,
    local,
):
    s, z = lax.axis_index("scene"), lax.axis_index("seq")
    x, c = lax.axis_index("head"), lax.axis_index("band")
    real = height * width
    rows, dim = fst.shape
    cols = wf.shape[2]
    pairs = cols // LANES
    frame = 4 * rows
    half = rows // 2
    steps = step_list(rows)
    parts = row_parts(rows)
    sems, _ = sem_layout(seq, pairs)
    core, across = (s, z, x, 1 - c), (s, z, 1 - x, c)
    place = 2 * x + c

    def paired(k):
        bits = [1 << i for i in range(seq.bit_length()) if k >> i & 1]
        return z + sum(bit - 2 * bit * lax.rem(lax.div(z, bit), 2) for bit in bits)

    def z_peer(k):
        return (s, paired(k), x, c)

    def remote(name, index, source, target, device, back=None):
        return pltpu.make_async_remote_copy(
            src_ref=source,
            dst_ref=target,
            send_sem=send.at[sems[name] + index],
            recv_sem=recv.at[sems[name] + (index if back is None else back)],
            device_id=device,
            device_id_type=pl.DeviceIdType.MESH,
        )

    barrier = pltpu.get_barrier_semaphore()
    everyone = [core, across, (s, z, 1 - x, 1 - c)] + [z_peer(d) for d in range(1, seq)]
    for device in everyone:
        pl.semaphore_signal(
            barrier, inc=1, device_id=device, device_id_type=pl.DeviceIdType.MESH
        )

    started = []

    def put(name, index, source, target, device):
        copy = remote(name, index, source, target, device)
        copy.start()
        started.append(copy)
        return copy

    own_cols = pl.ds(pl.multiple_of(c * cols, cols), cols)
    loads = []

    def load(source, target):
        copy = pltpu.make_async_copy(source, target, local.at[len(loads)])
        copy.start()
        loads.append(copy)
        return copy

    tok_load = load(tok_hbm, tok_ref)
    f_gain_load = load(f_gain_hbm, f_gain)
    wf_load = load(f_qkv.at[:, :, own_cols], wf)
    fo_loads = []
    for r in range(2):
        owner = c if r == 0 else 1 - c
        for i in range(2 * pairs):
            source = f_out.at[pl.ds(pl.multiple_of(owner * cols + i * HD, HD), HD)]
            fo_loads.append(load(source, fo.at[pl.ds(r * cols + (i ^ 1) * HD, HD)]))
    wg_load = load(g_qkv.at[:, :, own_cols], wg)
    half_rows = pl.ds(pl.multiple_of(x * 2 * cols, 2 * cols), 2 * cols)
    g_gain_load = load(g_gain_hbm, g_gain)
    late_loads = [load(g_out, go.at[half_rows]), load(h_proj, wp), load(h_conv, wc)]
    late_loads += [load(h_gain_hbm, h_gain), load(h_bias_hbm, h_bias)]

    tok_load.wait()
    for r in range(height):
        stage[r * width : (r + 1) * width, :] = tok_ref[0, r].astype(F32)
    for r in range(real, rows):
        stage[r : r + 1, :] = stage[real - 1 : real, :]
    toks[0] = stage[0:rows, :].astype(BF)
    pl.semaphore_wait(barrier, len(everyone))

    tok_x = []
    for k, (start, size) in enumerate(parts):
        at = pl.ds(start, size)
        tok_x.append(put("tok_x", k, toks.at[0, at], toks.at[2, at], across))
    tok_core = put("tok", 0, toks.at[0], toks.at[1], core)

    low = lax.broadcasted_iota(jnp.int32, (1, LANES), 1) < HD
    lane = lax.broadcasted_iota(jnp.int32, (1, 2 * cols), 1)
    v_lanes = lax.rem(lax.div(lane, HD), 4)
    v_lanes = jnp.logical_or(v_lanes == 1, v_lanes == 2)

    def valid_rows(start, size):
        return lax.broadcasted_iota(jnp.int32, (size, 1), 0) + start < real

    f_gain_load.wait()
    wf_load.wait()
    for p in range(pairs):
        at = pl.ds(p * LANES, LANES)
        k_part, v_part = wf[1, :, at], swap(wf[2, :, at].astype(F32)).astype(BF)
        wkv1[:, pl.ds(2 * p * LANES, LANES)] = jnp.where(low, k_part, v_part)
        wkv1[:, pl.ds((2 * p + 1) * LANES, LANES)] = jnp.where(low, v_part, k_part)

    def qkv1(slot, start, size, band):
        n = layer_norm(toks[slot, pl.ds(start, size)].astype(F32), f_gain[...], norm_eps).astype(BF)
        at = pl.ds(pl.multiple_of(band * rows + start, TILE), size)
        q1[at, :] = (mm(n, wf[0]) * QSCALE).astype(BF)
        both = mm(n, wkv1[...]).astype(BF)
        kv1[at, :] = both
        one = jnp.where(v_lanes, both, jnp.ones_like(both))
        vx1[at, :] = jnp.where(valid_rows(start, size), one, jnp.zeros_like(one))

    qkv1(0, 0, rows, place)
    tok_core.wait_recv()
    qkv1(1, 0, rows, 2 * x + 1 - c)
    g_gain_load.wait()
    wg_load.wait()
    for p in range(pairs):
        at = pl.ds(p * LANES, LANES)
        k_part, v_part = wg[1, :, at], wg[2, :, at]
        k_swap, v_swap = swap(k_part.astype(F32)).astype(BF), swap(v_part.astype(F32)).astype(BF)
        wkv2[:, pl.ds(2 * p * LANES, LANES)] = jnp.where(low, k_part, v_swap)
        wkv2[:, pl.ds((2 * p + 1) * LANES, LANES)] = jnp.where(low, k_swap, v_part)
    tok_f = []
    for k, (start, size) in enumerate(parts):
        at = pl.ds(start, size)
        tok_x[k].wait_recv()
        tok_f.append(put("tok_f", k, toks.at[2, at], toks.at[3, at], core))
        qkv1(2, start, size, 2 * (1 - x) + c)
    for k, (start, size) in enumerate(parts):
        tok_f[k].wait_recv()
        qkv1(3, start, size, 2 * (1 - x) + 1 - c)

    att_copies, p_copies, n_copies = [], [], []

    def attend(k, p):
        j, start, size, _ = steps[k]
        at = pl.ds(p * LANES, LANES)
        qp = jnp.concatenate(
            [q1[pl.ds((2 * j + b) * rows + start, size), at] for b in range(2)], axis=0
        )
        mixed = []
        for e in range(2):
            tile = pl.ds((2 * p + e) * LANES, LANES)
            zero = jnp.zeros_like(qp)
            lhs = jnp.where(low, qp, zero) if e == 0 else jnp.where(low, zero, qp)
            scores = dot_t(lhs, kv1[:, tile])
            probs = jnp.exp2(scores - jnp.max(scores, axis=-1, keepdims=True))
            mixed.append(mm(probs.astype(BF), vx1[:, tile]))
        top = jnp.where(low, mixed[1], mixed[0])
        bottom = swap(jnp.where(low, mixed[0], mixed[1]))
        out = (top / bottom).astype(BF)
        for b in range(2):
            att[k, b, pl.ds(0, size), at] = out[b * size : (b + 1) * size]

    def send_att(k):
        at = pl.ds(0, steps[k][2])
        att_copies.append(put("att", k, att.at[k, 1 - c, at], att_in.at[k, at], core))

    def project(k):
        j, start, size, _ = steps[k]
        at = pl.ds(0, size)
        att_copies[k].wait_recv()
        lhs = jnp.concatenate([att[k, c, at], att_in[k, at]], axis=1)
        partial = mm(lhs, fo[...])
        p_own[k, at] = partial
        p_out[k, at] = partial.astype(BF)
        p_copies.append(put("part", k, p_out.at[k, at], p_in.at[k, at], across))

    def norm2(k):
        j, start, size, _ = steps[k]
        at = pl.ds(0, size)
        slot = jnp.where(x == j, 0, 2)
        p_copies[k].wait_recv()
        tok = toks[slot, pl.ds(start, size)].astype(F32)
        first = (tok + p_own[k, at] + p_in[k, at].astype(F32)).astype(BF)

        @pl.when(x == j)
        def _():
            fst[pl.ds(start, size), :] = first

        n_own[k, at] = layer_norm(first.astype(F32), g_gain[...], norm_eps).astype(BF)
        n_copies.append(put("norm", k, n_own.at[k, at], n_in.at[k, at], core))

    kv_copies = [[] for _ in range(seq)]

    def qkv2(k):
        j, start, size, offset = steps[k]
        n_copies[k].wait_recv()
        at = pl.ds(0, size)
        n = jnp.concatenate([n_own[k, at], n_in[k, at]], axis=0)
        both = mm(n, wkv2[...]).astype(BF)
        for h in range(2 * pairs):
            skv[h, pl.ds(offset, 2 * size), :] = both[:, h * LANES : (h + 1) * LANES]
        to = pl.ds(pl.multiple_of(z * frame + offset, TILE), 2 * size)
        for d in range(1, seq):
            source = skv.at[paired(d), pl.ds(offset, 2 * size)]
            kv_copies[d].append(put("kv", k * seq + d, source, kv.at[to], z_peer(d)))
        kv[to, :] = skv[z, pl.ds(offset, 2 * size), :]
        queries = mm(n, wg[0]) * QSCALE
        q2[2 * j + c, pl.ds(start, size), :] = queries[:size]
        q2[2 * j + 1 - c, pl.ds(start, size), :] = queries[size:]

    for copy in fo_loads:
        copy.wait()
    for p in range(pairs):
        attend(0, p)
    send_att(0)
    for k in range(1, len(steps)):
        for p in range(pairs):
            attend(k, p)
            if p == 0:
                project(k - 1)
        send_att(k)
    project(len(steps) - 1)
    go_part = pl.ds(pl.multiple_of(x * 2 * cols + c * cols, cols), cols)
    go_from = pl.ds(pl.multiple_of((1 - x) * 2 * cols + c * cols, cols), cols)
    go_x = put("go", 0, g_out.at[own_cols], go.at[go_part], across)
    for k in range(len(steps)):
        norm2(k)
        qkv2(k)
    for b in range(4):
        for p in range(pairs):
            tile = q2[b, :, pl.ds(p * LANES, LANES)]
            top, under = tile[:half], tile[half:]
            sq[2 * p, b] = jnp.where(low, top, swap(under)).astype(BF)
            sq[2 * p + 1, b] = jnp.where(low, swap(top), under).astype(BF)
    for pair in range(2):
        for d in range(1, seq):
            for b in (2 * pair, 2 * pair + 1):
                put("q", b * seq + d, sq.at[paired(d), b], rq.at[z, b], z_peer(d))
    rq[z] = sq[z]

    frame_valid = jnp.concatenate(
        [valid_rows(start, size) for j, start, size, _ in steps for b in range(2)], axis=0
    )

    def spread(origin):
        at = pl.ds(pl.multiple_of(origin * frame, frame), frame)
        both = kv[at, :]
        one = jnp.where(low, jnp.ones_like(both), both)
        vx[at, :] = jnp.where(frame_valid, one, jnp.zeros_like(one))

    spread(z)
    for d in range(1, seq):
        for copy in kv_copies[d]:
            copy.wait_recv()
        spread(paired(d))

    mine = place * seq + z

    def q_copy(d, b, origin):
        device = (s, origin, x, c)
        return remote("q", b * seq + d, sq.at[0, b], rq.at[origin, b], device)

    def o_copy(d, pair, i, origin):
        b = 2 * pair + i
        device = (s, origin, pair, i)
        return remote("o", d * 4 + b, so.at[d, b], ro.at[mine], device, mine)

    def origin_of(d):
        origin = z
        for i in range((seq - 1).bit_length()):
            bit = 1 << i
            flip = lax.rem(lax.div(d, bit), 2)
            origin = origin + flip * (bit - 2 * bit * lax.rem(lax.div(z, bit), 2))
        return origin

    def each_o(d, pair, i, origin, act):
        itself = jnp.logical_and(d == 0, place == 2 * pair + i)

        @pl.when(jnp.logical_not(itself))
        def _():
            act(o_copy(d, pair, i, origin))

    @pl.loop(0, 2 * seq)
    def _(turn):
        pair, d = lax.div(turn, seq), lax.rem(turn, seq)
        origin = origin_of(d)
        for i in range(2):

            @pl.when(d > 0)
            def _():
                q_copy(d, 2 * pair + i, origin).wait_recv()

        q = []
        for i in range(2):
            packed = rq[origin, 2 * pair + i].astype(F32)
            q += [packed, swap(packed)]
        q = jnp.where(low, jnp.concatenate(q, axis=0), 0.0).astype(BF)
        scores = dot_t(q, kv[...])
        probs = jnp.exp2(scores - jnp.max(scores, axis=-1, keepdims=True))
        mixed = mm(probs.astype(BF), vx[...])
        out = mixed / jnp.where(low, 1.0, swap(mixed))
        for i in range(2):
            o = out[i * rows : (i + 1) * rows]
            so[d, 2 * pair + i] = jnp.where(low, swap(o)[:half], o[half:]).astype(BF)
            each_o(d, pair, i, origin, lambda copy: copy.start())

    ro_own = so[0, place]
    ro[mine] = ro_own
    go_x.wait_recv()
    go_f = put("go", 1, go.at[go_from], go.at[go_from], core)
    for copy in late_loads:
        copy.wait()
    for slot in range(4 * seq):

        @pl.when(slot != mine)
        def _():
            remote("o", 0, so.at[0, 0], ro.at[slot], core, slot).wait_recv()

    for i in range(2 * seq):
        at = pl.ds(i * LANES, LANES)
        even, odd = ro[2 * i].astype(F32), ro[2 * i + 1].astype(F32)
        pair = [jnp.where(low, even, swap(odd)), jnp.where(low, swap(even), odd)]
        a2[:, at] = jnp.concatenate(pair, axis=0).astype(BF)
    first = fst[...].astype(F32)
    go_f.wait_recv()
    second = (first + mm(a2[...], go[...])).astype(BF).astype(F32)
    stacked = jnp.concatenate([first, second], axis=-1)
    n3 = layer_norm(stacked, h_gain[...], head_eps).astype(BF)
    pj[...] = (mm(n3, wp[...]) + h_bias[...]).astype(BF)

    after = lax.rem(place + 1, 4)
    before = lax.rem(place + 3, 4)

    def frame_peer(index):
        return (s, z, index // 2, lax.rem(index, 2))

    start = (real - width) // TILE * TILE
    slab = halo.shape[1]
    down = put(
        "halo", 0, pj.at[pl.ds(start, rows - start)], halo.at[0, pl.ds(0, rows - start)],
        frame_peer(after),
    )
    upward = put("halo", 1, pj.at[pl.ds(0, slab)], halo.at[1], frame_peer(before))
    stage[0:rows, :] = second
    for r in range(height):
        blocks_ref[0, r] = stage[r * width : (r + 1) * width, :].astype(BF)
    base = 8
    xbuf[...] = jnp.zeros_like(xbuf)
    xbuf[base + width : base + width + real, :] = pj[...].astype(F32)[:real]
    down.wait_recv()
    upward.wait_recv()
    skip = real - width - start
    lower = jnp.where(place > 0, halo[0].astype(F32), 0.0)
    upper = jnp.where(place < 3, halo[1].astype(F32), 0.0)
    xbuf[base : base + width, :] = lower[skip : skip + width]
    xbuf[base + width + real : base + 2 * width + real, :] = upper[:width]
    col = lax.rem(lax.broadcasted_iota(jnp.int32, (rows, 1), 0), width)
    channels = pj.shape[1]
    total = jnp.zeros((rows, channels), F32)
    for i in range(3):
        for j in range(3):
            first_row = base + width * i + j - 1
            window = xbuf[first_row : first_row + rows, :]
            if j == 0:
                window = jnp.where(col > 0, window, 0.0)
            if j == 2:
                window = jnp.where(col < width - 1, window, 0.0)
            total = total + mm(window.astype(BF), wc[3 * i + j])
    stage[0:rows, 0:channels] = total
    for r in range(height):
        feat_ref[0, r] = stage[r * width : (r + 1) * width, 0:channels].astype(BF)

    for copy in started:
        copy.wait_send()

    @pl.loop(0, seq)
    def _(d):
        for b in range(4):
            each_o(d, b // 2, b % 2, origin_of(d), lambda copy: copy.wait_send())


def scene_program(seq, *arrays):
    (tokens, f_gain, f_qkv, f_out, g_gain, g_qkv, g_out, h_gain, h_proj, h_bias, h_conv) = arrays
    height, width, dim = tokens.shape[1:]
    real = height * width
    rows = up(real)
    cols = f_qkv.shape[2] // 2
    pairs = cols // LANES
    channels = h_proj.shape[1]
    frame = 4 * rows
    half = rows // 2
    most = row_parts(rows)[0][1]
    vmem = pl.BlockSpec(memory_space=pltpu.VMEM)
    hbm = pl.BlockSpec(memory_space=pltpu.HBM)
    start = (real - width) // TILE * TILE
    slab = max(up(width), rows - start)
    _, copies = sem_layout(seq, pairs)
    return pl.pallas_call(
        functools.partial(scene_kernel, seq, height, width),
        out_shape=(
            jax.ShapeDtypeStruct(tokens.shape, BF),
            jax.ShapeDtypeStruct((1, height, width, channels), BF),
        ),
        in_specs=[hbm] * 11,
        out_specs=(vmem, vmem),
        scratch_shapes=[
            pltpu.VMEM(tokens.shape, BF),
            pltpu.VMEM((1, dim), F32),
            pltpu.VMEM((1, dim), F32),
            pltpu.VMEM((1, 2 * dim), F32),
            pltpu.VMEM((1, channels), F32),
            pltpu.VMEM((rows, dim), F32),
            pltpu.VMEM((4, rows, dim), BF),
            pltpu.VMEM((3, dim, cols), BF),
            pltpu.VMEM((3, dim, cols), BF),
            pltpu.VMEM((dim, 2 * cols), BF),
            pltpu.VMEM((dim, 2 * cols), BF),
            pltpu.VMEM((2 * cols, dim), BF),
            pltpu.VMEM((4 * cols, dim), BF),
            pltpu.VMEM(h_proj.shape, BF),
            pltpu.VMEM((9, channels, channels), BF),
            pltpu.VMEM((frame, cols), BF),
            pltpu.VMEM((frame, 2 * cols), BF),
            pltpu.VMEM((frame, 2 * cols), BF),
            pltpu.VMEM((4, 2, most, cols), BF),
            pltpu.VMEM((4, most, cols), BF),
            pltpu.VMEM((4, most, dim), F32),
            pltpu.VMEM((4, most, dim), BF),
            pltpu.VMEM((4, most, dim), BF),
            pltpu.VMEM((4, most, dim), BF),
            pltpu.VMEM((4, most, dim), BF),
            pltpu.VMEM((rows, dim), BF),
            pltpu.VMEM((4, rows, cols), F32),
            pltpu.VMEM((seq, frame, LANES), BF),
            pltpu.VMEM((seq * frame, LANES), BF),
            pltpu.VMEM((seq * frame, LANES), BF),
            pltpu.VMEM((seq, 4, half, LANES), BF),
            pltpu.VMEM((seq, 4, half, LANES), BF),
            pltpu.VMEM((seq, 4, half, LANES), BF),
            pltpu.VMEM((4 * seq, half, LANES), BF),
            pltpu.VMEM((rows, 4 * cols), BF),
            pltpu.VMEM((rows, channels), BF),
            pltpu.VMEM((2, slab, channels), BF),
            pltpu.VMEM((up(rows + 2 * width + 2 * TILE), channels), F32),
            pltpu.SemaphoreType.DMA((copies,)),
            pltpu.SemaphoreType.DMA((copies,)),
            pltpu.SemaphoreType.DMA((10 + 4 * pairs,)),
        ],
        compiler_params=pltpu.CompilerParams(
            collective_id=0, has_side_effects=True, vmem_limit_bytes=40 * 2**20
        ),
    )(
        *[
            pltpu.with_memory_space_constraint(array, pltpu.HBM)
            for array in (
                tokens,
                f_gain.reshape(1, -1),
                f_qkv,
                f_out,
                g_gain.reshape(1, -1),
                g_qkv,
                g_out,
                h_gain.reshape(1, -1),
                h_proj,
                h_bias.reshape(1, -1),
                h_conv.reshape(9, channels, channels),
            )
        ]
    )


def routed(mesh, *arrays):
    sizes = mesh.shape
    frames, height, width = arrays[0].shape[:3]
    heads = arrays[2].shape[2] // HD
    fits = (
        sizes["head"] == 2
        and sizes["band"] == 2
        and frames == 1
        and heads == 2 * sizes["seq"]
        and sizes["seq"] & (sizes["seq"] - 1) == 0
        and sizes["seq"] >= 2
        and arrays[0].shape[3] == 2 * arrays[2].shape[2]
        and arrays[10].shape[2] <= arrays[0].shape[3]
        and height * width >= up(width)
        and up(height * width) >= 2 * TILE
    )
    if fits:
        return scene_program(sizes["seq"], *arrays)
    return on_device(*arrays)


def solution(mesh):
    return jax.shard_map(
        functools.partial(routed, mesh),
        mesh=mesh,
        in_specs=(
            P(("scene", "seq"), ("head", "band"), None, None),
            P(),
            P(None, None, "head"),
            P("head", None),
            P(),
            P(None, None, "head"),
            P("head", None),
            P(),
            P(),
            P(),
            P(),
        ),
        out_specs=(
            P(("scene", "seq"), ("head", "band"), None, None),
            P(("scene", "seq"), ("head", "band"), None, None),
        ),
        check_vma=False,
    )
```

```python
import functools
import math

import jax
import jax.numpy as jnp
from jax import lax
from jax.experimental import pallas as pl
from jax.experimental.pallas import tpu as pltpu
from jax.sharding import PartitionSpec as P

HD = 64


norm_eps = 1e-06
head_eps = 1e-05


def padded_2(block, sides, width):
    for axis, dim in sides:
        count = lax.axis_size(axis)
        forward = [(i, i + 1) for i in range(count - 1)]
        backward = [(target, source) for source, target in forward]
        low = lax.ppermute(
            lax.slice_in_dim(block, block.shape[dim] - width, None, axis=dim), axis, forward
        )
        high = lax.ppermute(lax.slice_in_dim(block, 0, width, axis=dim), axis, backward)
        block = jnp.concatenate([low, block, high], axis=dim)
    return block


def layer_norm(values, gain, epsilon):
    centre = values - jnp.mean(values, axis=-1, keepdims=True)
    spread = jnp.mean(centre * centre, axis=-1, keepdims=True)
    return centre * lax.rsqrt(spread + epsilon) * gain


def by_heads(matrix):
    return matrix.reshape(matrix.shape[0], matrix.shape[1] // HD, HD)


def attend_local(queries, keys_all, values_all):
    scores = jnp.einsum(
        "qhd,khd->qhk", by_heads(queries), by_heads(keys_all), preferred_element_type=jnp.float32
    ) * HD ** (-0.5)
    probs = jnp.exp(scores - jnp.max(scores, axis=-1, keepdims=True))
    mixed = jnp.einsum(
        "qhk,khd->qhd",
        probs.astype(jnp.bfloat16),
        by_heads(values_all),
        preferred_element_type=jnp.float32,
    )
    mixed = mixed / jnp.sum(probs, axis=-1)[..., None]
    return mixed.reshape(queries.shape).astype(jnp.bfloat16)


def key_step(local_rows, portion_rows):
    amount = portion_rows // local_rows
    best = 1
    for factor in range(1, amount + 1):
        if amount % factor == 0 and local_rows * factor <= max(local_rows, 1024):
            best = factor
    return local_rows * best


def fresh_carry(queries):
    heads_q = by_heads(queries)
    return (
        jnp.full(heads_q.shape[:2], -jnp.inf, jnp.float32),
        jnp.zeros(heads_q.shape[:2], jnp.float32),
        jnp.zeros(heads_q.shape, jnp.float32),
    )


def finish(carry, queries):
    return (carry[2] / carry[1][..., None]).reshape(queries.shape).astype(jnp.bfloat16)


def fold_keys(queries, carry, portions, local_rows):
    keys_in, values_in = portions
    step_rows = key_step(local_rows, keys_in.shape[0])
    heads_q = by_heads(queries)
    key_blocks = keys_in.reshape(-1, step_rows, keys_in.shape[1])
    value_blocks = values_in.reshape(-1, step_rows, values_in.shape[1])

    def absorb(states, blocks_pair):
        running_max, running_sum, weighted = states
        scores = jnp.einsum(
            "qhd,khd->qhk", heads_q, by_heads(blocks_pair[0]), preferred_element_type=jnp.float32
        ) * HD ** (-0.5)
        new_max = jnp.maximum(running_max, jnp.max(scores, axis=-1))
        decay = jnp.exp(running_max - new_max)
        probs = jnp.exp(scores - new_max[..., None])
        running_sum = running_sum * decay + jnp.sum(probs, axis=-1)
        weighted = weighted * decay[..., None] + jnp.einsum(
            "qhk,khd->qhd",
            probs.astype(jnp.bfloat16),
            by_heads(blocks_pair[1]),
            preferred_element_type=jnp.float32,
        )
        return ((new_max, running_sum, weighted), None)

    carry, ignored = lax.scan(absorb, carry, (key_blocks, value_blocks))
    return carry


def attention_block(inputs, gain, qkv_weight, out_weight, wide):
    normed = layer_norm(inputs.astype(jnp.float32), gain, norm_eps).astype(jnp.bfloat16)
    gathered = lax.all_gather(normed, "head", axis=1, tiled=True)
    flattened = gathered.reshape(-1, gathered.shape[-1])
    query_rows = jnp.dot(flattened, qkv_weight[0], preferred_element_type=jnp.float32).astype(
        jnp.bfloat16
    )
    key_rows = jnp.dot(flattened, qkv_weight[1], preferred_element_type=jnp.float32).astype(
        jnp.bfloat16
    )
    value_rows = jnp.dot(flattened, qkv_weight[2], preferred_element_type=jnp.float32).astype(
        jnp.bfloat16
    )
    if wide:
        carry = fold_keys(
            query_rows,
            fresh_carry(query_rows),
            (
                lax.all_gather(key_rows, ("seq", "band"), axis=0, tiled=True),
                lax.all_gather(value_rows, ("seq", "band"), axis=0, tiled=True),
            ),
            key_rows.shape[0],
        )
        attended = finish(carry, query_rows)
    else:
        keys_all, values_all = (
            lax.all_gather(key_rows, "band", axis=0, tiled=True),
            lax.all_gather(value_rows, "band", axis=0, tiled=True),
        )
        attended = attend_local(query_rows, keys_all, values_all)
    band_rows = inputs.shape[1] * inputs.shape[2]
    own_rows = lax.all_to_all(attended, "head", split_axis=0, concat_axis=1, tiled=True)
    branch = jnp.dot(
        own_rows,
        lax.all_gather(out_weight, "head", axis=0, tiled=True),
        preferred_element_type=jnp.float32,
    )
    merged = inputs.astype(jnp.float32).reshape(band_rows, -1) + branch
    return merged.astype(jnp.bfloat16).reshape(inputs.shape)


def on_device(
    tokens,
    frame_gain,
    frame_qkv,
    frame_out,
    global_gain,
    global_qkv,
    global_out,
    head_gain,
    head_proj,
    head_bias,
    head_conv,
):
    first = attention_block(tokens, frame_gain, frame_qkv, frame_out, False)
    second = attention_block(first, global_gain, global_qkv, global_out, True)
    band_height = tokens.shape[1]
    grid_width = tokens.shape[2]
    stacked = jnp.concatenate([first.astype(jnp.float32), second.astype(jnp.float32)], axis=-1)
    normed = layer_norm(stacked, head_gain, head_eps).astype(jnp.bfloat16)
    projected = (
        jnp.dot(
            normed.reshape(-1, stacked.shape[-1]), head_proj, preferred_element_type=jnp.float32
        )
        + head_bias
    )
    projected = projected.astype(jnp.bfloat16).reshape(
        tokens.shape[0], band_height, grid_width, head_proj.shape[1]
    )
    padded = padded_2(projected, ((("head", "band"), 1),), 1)
    padded = jnp.pad(padded, ((0, 0), (0, 0), (1, 1), (0, 0)))
    totals = jnp.zeros(projected.shape, jnp.float32)
    for offset_row in range(3):
        for offset_col in range(3):
            window = padded[
                :, offset_row : offset_row + band_height, offset_col : offset_col + grid_width
            ]
            totals = totals + jnp.einsum(
                "frcx,xy->frcy",
                window,
                head_conv[offset_row, offset_col],
                preferred_element_type=jnp.float32,
            )
    return (second, totals.astype(jnp.bfloat16))


BF = jnp.bfloat16
F32 = jnp.float32
TILE = 16
LANES = 2 * HD
STEP_SHARES = ((3, 4), (4, 3))
QSCALE = HD ** (-0.5) * math.log2(math.e)


def up(count):
    return -(-count // TILE) * TILE


def mm(a, b):
    return jnp.dot(a, b, preferred_element_type=F32)


def swap(values):
    return pltpu.roll(values, HD, axis=1)


def dot_t(a, b):
    return lax.dot_general(a, b, (((1,), (1,)), ((), ())), preferred_element_type=F32)


def row_parts(rows):
    first = up(rows // 2)
    return [(0, first), (first, rows - first)]


def split_rows(rows, shares):
    units, sizes = rows // TILE, []
    for i, share in enumerate(shares):
        left = units - sum(sizes)
        size = left if i == len(shares) - 1 else max(1, units * share // sum(shares))
        sizes.append(size)
    return [size * TILE for size in sizes if size > 0]


def step_list(rows):
    steps, at = [], 0
    for j, shares in enumerate(STEP_SHARES):
        start = 0
        for size in split_rows(rows, shares):
            steps.append((j, start, size, at))
            at += 2 * size
            start += size
    return steps


def sem_layout(seq, count):
    names = [
        ("tok", 1), ("tok_x", 2), ("tok_f", 2), ("att", count), ("part", count), ("norm", count),
        ("kv", count * seq), ("q", 4 * seq), ("o", 4 * seq), ("go", 2), ("halo", 2),
    ]
    at, table = 0, {}
    for name, size in names:
        table[name] = at
        at += size
    return table, at


def scene_kernel(
    seq,
    height,
    width,
    tok_hbm,
    f_gain_hbm,
    f_qkv,
    f_out,
    g_gain_hbm,
    g_qkv,
    g_out,
    h_gain_hbm,
    h_proj,
    h_bias_hbm,
    h_conv,
    blocks_ref,
    feat_ref,
    tok_ref,
    f_gain,
    g_gain,
    h_gain,
    h_bias,
    stage,
    toks,
    wf,
    wg,
    wkv1,
    wkv2,
    fo,
    go,
    wp,
    wc,
    q1,
    kv1,
    vx1,
    att,
    att_in,
    p_own,
    p_out,
    p_in,
    n_own,
    n_in,
    fst,
    q2,
    skv,
    kv,
    vx,
    sq,
    rq,
    so,
    ro,
    a2,
    pj,
    halo,
    xbuf,
    send,
    recv,
    local,
):
    s, z = lax.axis_index("scene"), lax.axis_index("seq")
    x, c = lax.axis_index("head"), lax.axis_index("band")
    real = height * width
    rows, dim = fst.shape
    cols = wf.shape[2]
    pairs = cols // LANES
    frame = 4 * rows
    half = rows // 2
    steps = step_list(rows)
    parts = row_parts(rows)
    sems, _ = sem_layout(seq, len(steps))
    core, across = (s, z, x, 1 - c), (s, z, 1 - x, c)
    place = 2 * x + c

    def paired(k):
        bits = [1 << i for i in range(seq.bit_length()) if k >> i & 1]
        return z + sum(bit - 2 * bit * lax.rem(lax.div(z, bit), 2) for bit in bits)

    def z_peer(k):
        return (s, paired(k), x, c)

    def remote(name, index, source, target, device, back=None):
        return pltpu.make_async_remote_copy(
            src_ref=source,
            dst_ref=target,
            send_sem=send.at[sems[name] + index],
            recv_sem=recv.at[sems[name] + (index if back is None else back)],
            device_id=device,
            device_id_type=pl.DeviceIdType.MESH,
        )

    barrier = pltpu.get_barrier_semaphore()
    everyone = [core, across, (s, z, 1 - x, 1 - c)] + [z_peer(d) for d in range(1, seq)]
    for device in everyone:
        pl.semaphore_signal(
            barrier, inc=1, device_id=device, device_id_type=pl.DeviceIdType.MESH
        )

    started = []

    def put(name, index, source, target, device):
        copy = remote(name, index, source, target, device)
        copy.start()
        started.append(copy)
        return copy

    own_cols = pl.ds(pl.multiple_of(c * cols, cols), cols)
    loads = []

    def load(source, target):
        copy = pltpu.make_async_copy(source, target, local.at[len(loads)])
        copy.start()
        loads.append(copy)
        return copy

    tok_load = load(tok_hbm, tok_ref)
    f_gain_load = load(f_gain_hbm, f_gain)
    wf_load = load(f_qkv.at[:, :, own_cols], wf)
    fo_loads = []
    for r in range(2):
        owner = c if r == 0 else 1 - c
        for i in range(2 * pairs):
            source = f_out.at[pl.ds(pl.multiple_of(owner * cols + i * HD, HD), HD)]
            fo_loads.append(load(source, fo.at[pl.ds(r * cols + (i ^ 1) * HD, HD)]))
    wg_load = load(g_qkv.at[:, :, own_cols], wg)
    half_rows = pl.ds(pl.multiple_of(x * 2 * cols, 2 * cols), 2 * cols)
    g_gain_load = load(g_gain_hbm, g_gain)
    late_loads = [load(g_out, go.at[half_rows]), load(h_proj, wp), load(h_conv, wc)]
    late_loads += [load(h_gain_hbm, h_gain), load(h_bias_hbm, h_bias)]

    tok_load.wait()
    for r in range(height):
        stage[r * width : (r + 1) * width, :] = tok_ref[0, r].astype(F32)
    for r in range(real, rows):
        stage[r : r + 1, :] = stage[real - 1 : real, :]
    toks[0] = stage[0:rows, :].astype(BF)
    pl.semaphore_wait(barrier, len(everyone))

    tok_x = []
    for k, (start, size) in enumerate(parts):
        at = pl.ds(start, size)
        tok_x.append(put("tok_x", k, toks.at[0, at], toks.at[2, at], across))
    tok_core = put("tok", 0, toks.at[0], toks.at[1], core)

    low = lax.broadcasted_iota(jnp.int32, (1, LANES), 1) < HD
    lane = lax.broadcasted_iota(jnp.int32, (1, 2 * cols), 1)
    v_lanes = lax.rem(lax.div(lane, HD), 4)
    v_lanes = jnp.logical_or(v_lanes == 1, v_lanes == 2)

    def valid_rows(start, size):
        return lax.broadcasted_iota(jnp.int32, (size, 1), 0) + start < real

    f_gain_load.wait()
    wf_load.wait()
    for p in range(pairs):
        at = pl.ds(p * LANES, LANES)
        k_part, v_part = wf[1, :, at], swap(wf[2, :, at].astype(F32)).astype(BF)
        wkv1[:, pl.ds(2 * p * LANES, LANES)] = jnp.where(low, k_part, v_part)
        wkv1[:, pl.ds((2 * p + 1) * LANES, LANES)] = jnp.where(low, v_part, k_part)

    def qkv1(slot, start, size, band):
        n = layer_norm(toks[slot, pl.ds(start, size)].astype(F32), f_gain[...], norm_eps).astype(BF)
        at = pl.ds(pl.multiple_of(band * rows + start, TILE), size)
        q1[at, :] = (mm(n, wf[0]) * QSCALE).astype(BF)
        both = mm(n, wkv1[...]).astype(BF)
        kv1[at, :] = both
        one = jnp.where(v_lanes, both, jnp.ones_like(both))
        vx1[at, :] = jnp.where(valid_rows(start, size), one, jnp.zeros_like(one))

    qkv1(0, 0, rows, place)
    tok_core.wait_recv()
    qkv1(1, 0, rows, 2 * x + 1 - c)
    g_gain_load.wait()
    wg_load.wait()
    for p in range(pairs):
        at = pl.ds(p * LANES, LANES)
        k_part, v_part = wg[1, :, at], wg[2, :, at]
        k_swap, v_swap = swap(k_part.astype(F32)).astype(BF), swap(v_part.astype(F32)).astype(BF)
        wkv2[:, pl.ds(2 * p * LANES, LANES)] = jnp.where(low, k_part, v_swap)
        wkv2[:, pl.ds((2 * p + 1) * LANES, LANES)] = jnp.where(low, k_swap, v_part)
    tok_f = []
    for k, (start, size) in enumerate(parts):
        at = pl.ds(start, size)
        tok_x[k].wait_recv()
        tok_f.append(put("tok_f", k, toks.at[2, at], toks.at[3, at], core))
        qkv1(2, start, size, 2 * (1 - x) + c)
    for k, (start, size) in enumerate(parts):
        tok_f[k].wait_recv()
        qkv1(3, start, size, 2 * (1 - x) + 1 - c)

    att_copies, p_copies, n_copies = [], [], []

    def attend(k, p):
        j, start, size, _ = steps[k]
        at = pl.ds(p * LANES, LANES)
        qp = jnp.concatenate(
            [q1[pl.ds((2 * j + b) * rows + start, size), at] for b in range(2)], axis=0
        )
        mixed = []
        for e in range(2):
            tile = pl.ds((2 * p + e) * LANES, LANES)
            zero = jnp.zeros_like(qp)
            lhs = jnp.where(low, qp, zero) if e == 0 else jnp.where(low, zero, qp)
            scores = dot_t(lhs, kv1[:, tile])
            probs = jnp.exp2(scores - jnp.max(scores, axis=-1, keepdims=True))
            mixed.append(mm(probs.astype(BF), vx1[:, tile]))
        top = jnp.where(low, mixed[1], mixed[0])
        bottom = swap(jnp.where(low, mixed[0], mixed[1]))
        out = (top / bottom).astype(BF)
        for b in range(2):
            att[k, b, pl.ds(0, size), at] = out[b * size : (b + 1) * size]

    def send_att(k):
        at = pl.ds(0, steps[k][2])
        att_copies.append(put("att", k, att.at[k, 1 - c, at], att_in.at[k, at], core))

    def project(k):
        j, start, size, _ = steps[k]
        at = pl.ds(0, size)
        att_copies[k].wait_recv()
        lhs = jnp.concatenate([att[k, c, at], att_in[k, at]], axis=1)
        partial = mm(lhs, fo[...])
        p_own[k, at] = partial
        p_out[k, at] = partial.astype(BF)
        p_copies.append(put("part", k, p_out.at[k, at], p_in.at[k, at], across))

    def norm2(k):
        j, start, size, _ = steps[k]
        at = pl.ds(0, size)
        slot = jnp.where(x == j, 0, 2)
        p_copies[k].wait_recv()
        tok = toks[slot, pl.ds(start, size)].astype(F32)
        first = (tok + p_own[k, at] + p_in[k, at].astype(F32)).astype(BF)

        @pl.when(x == j)
        def _():
            fst[pl.ds(start, size), :] = first

        n_own[k, at] = layer_norm(first.astype(F32), g_gain[...], norm_eps).astype(BF)
        n_copies.append(put("norm", k, n_own.at[k, at], n_in.at[k, at], core))

    kv_copies = [[] for _ in range(seq)]

    def qkv2(k):
        j, start, size, offset = steps[k]
        n_copies[k].wait_recv()
        at = pl.ds(0, size)
        n = jnp.concatenate([n_own[k, at], n_in[k, at]], axis=0)
        both = mm(n, wkv2[...]).astype(BF)
        for h in range(2 * pairs):
            skv[h, pl.ds(offset, 2 * size), :] = both[:, h * LANES : (h + 1) * LANES]
        to = pl.ds(pl.multiple_of(z * frame + offset, TILE), 2 * size)
        for d in range(1, seq):
            source = skv.at[paired(d), pl.ds(offset, 2 * size)]
            kv_copies[d].append(put("kv", k * seq + d, source, kv.at[to], z_peer(d)))
        kv[to, :] = skv[z, pl.ds(offset, 2 * size), :]
        queries = mm(n, wg[0]) * QSCALE
        q2[2 * j + c, pl.ds(start, size), :] = queries[:size]
        q2[2 * j + 1 - c, pl.ds(start, size), :] = queries[size:]

    for copy in fo_loads:
        copy.wait()
    for p in range(pairs):
        attend(0, p)
    send_att(0)
    for k in range(1, len(steps)):
        for p in range(pairs):
            attend(k, p)
            if p == 0:
                project(k - 1)
        send_att(k)
    project(len(steps) - 1)
    go_part = pl.ds(pl.multiple_of(x * 2 * cols + c * cols, cols), cols)
    go_from = pl.ds(pl.multiple_of((1 - x) * 2 * cols + c * cols, cols), cols)
    go_x = put("go", 0, g_out.at[own_cols], go.at[go_part], across)
    for k in range(len(steps)):
        norm2(k)
        qkv2(k)
    for b in range(4):
        for p in range(pairs):
            tile = q2[b, :, pl.ds(p * LANES, LANES)]
            top, under = tile[:half], tile[half:]
            sq[2 * p, b] = jnp.where(low, top, swap(under)).astype(BF)
            sq[2 * p + 1, b] = jnp.where(low, swap(top), under).astype(BF)
    for pair in range(2):
        for d in range(1, seq):
            bands = pl.ds(2 * pair, 2)
            put("q", pair * seq + d, sq.at[paired(d), bands], rq.at[z, bands], z_peer(d))
    rq[z] = sq[z]

    frame_valid = jnp.concatenate(
        [valid_rows(start, size) for j, start, size, _ in steps for b in range(2)], axis=0
    )

    def spread(origin):
        at = pl.ds(pl.multiple_of(origin * frame, frame), frame)
        both = kv[at, :]
        one = jnp.where(low, jnp.ones_like(both), both)
        vx[at, :] = jnp.where(frame_valid, one, jnp.zeros_like(one))

    spread(z)
    for d in range(1, seq):
        for copy in kv_copies[d]:
            copy.wait_recv()
        spread(paired(d))

    mine = place * seq + z

    def q_copy(d, pair, origin):
        device, bands = (s, origin, x, c), pl.ds(2 * pair, 2)
        return remote("q", pair * seq + d, sq.at[0, bands], rq.at[origin, bands], device)

    def o_copy(d, pair, i, origin):
        b = 2 * pair + i
        device = (s, origin, pair, i)
        return remote("o", d * 4 + b, so.at[d, b], ro.at[mine], device, mine)

    def origin_of(d):
        origin = z
        for i in range((seq - 1).bit_length()):
            bit = 1 << i
            flip = lax.rem(lax.div(d, bit), 2)
            origin = origin + flip * (bit - 2 * bit * lax.rem(lax.div(z, bit), 2))
        return origin

    def each_o(d, pair, i, origin, act):
        itself = jnp.logical_and(d == 0, place == 2 * pair + i)

        @pl.when(jnp.logical_not(itself))
        def _():
            act(o_copy(d, pair, i, origin))

    @pl.loop(0, 2 * seq // 2)
    def _(turn):
        pair = lax.div(turn, seq // 2)
        group = lax.rem(turn, seq // 2)
        group = group + pair * (seq // 2 - 1 - 2 * group)
        ds = [2 * group + i for i in range(2)]
        origins = [origin_of(d) for d in ds]
        for d, origin in zip(ds, origins):

            @pl.when(d > 0)
            def _():
                q_copy(d, pair, origin).wait_recv()

        for d, origin in zip(ds, origins):
            q = []
            for i in range(2):
                packed = rq[origin, 2 * pair + i].astype(F32)
                q += [packed, swap(packed)]
            q = jnp.where(low, jnp.concatenate(q, axis=0), 0.0).astype(BF)
            scores = dot_t(q, kv[...])
            probs = jnp.exp2(scores - jnp.max(scores, axis=-1, keepdims=True))
            mixed = mm(probs.astype(BF), vx[...])
            out = mixed / jnp.where(low, 1.0, swap(mixed))
            for i in range(2):
                o = out[i * rows : (i + 1) * rows]
                so[d, 2 * pair + i] = jnp.where(low, swap(o)[:half], o[half:]).astype(BF)
                each_o(d, pair, i, origin, lambda copy: copy.start())

    ro_own = so[0, place]
    ro[mine] = ro_own
    go_x.wait_recv()
    go_f = put("go", 1, go.at[go_from], go.at[go_from], core)
    for copy in late_loads:
        copy.wait()
    for slot in range(4 * seq):

        @pl.when(slot != mine)
        def _():
            remote("o", 0, so.at[0, 0], ro.at[slot], core, slot).wait_recv()

    for i in range(2 * seq):
        at = pl.ds(i * LANES, LANES)
        even, odd = ro[2 * i].astype(F32), ro[2 * i + 1].astype(F32)
        pair = [jnp.where(low, even, swap(odd)), jnp.where(low, swap(even), odd)]
        a2[:, at] = jnp.concatenate(pair, axis=0).astype(BF)
    first = fst[...].astype(F32)
    go_f.wait_recv()
    second = (first + mm(a2[...], go[...])).astype(BF).astype(F32)
    stacked = jnp.concatenate([first, second], axis=-1)
    n3 = layer_norm(stacked, h_gain[...], head_eps).astype(BF)
    pj[...] = (mm(n3, wp[...]) + h_bias[...]).astype(BF)

    after = lax.rem(place + 1, 4)
    before = lax.rem(place + 3, 4)

    def frame_peer(index):
        return (s, z, index // 2, lax.rem(index, 2))

    start = (real - width) // TILE * TILE
    slab = halo.shape[1]
    down = put(
        "halo", 0, pj.at[pl.ds(start, rows - start)], halo.at[0, pl.ds(0, rows - start)],
        frame_peer(after),
    )
    upward = put("halo", 1, pj.at[pl.ds(0, slab)], halo.at[1], frame_peer(before))
    stage[0:rows, :] = second
    for r in range(height):
        blocks_ref[0, r] = stage[r * width : (r + 1) * width, :].astype(BF)
    base = 8
    xbuf[...] = jnp.zeros_like(xbuf)
    xbuf[base + width : base + width + real, :] = pj[...].astype(F32)[:real]
    down.wait_recv()
    upward.wait_recv()
    skip = real - width - start
    lower = jnp.where(place > 0, halo[0].astype(F32), 0.0)
    upper = jnp.where(place < 3, halo[1].astype(F32), 0.0)
    xbuf[base : base + width, :] = lower[skip : skip + width]
    xbuf[base + width + real : base + 2 * width + real, :] = upper[:width]
    col = lax.rem(lax.broadcasted_iota(jnp.int32, (rows, 1), 0), width)
    channels = pj.shape[1]
    total = jnp.zeros((rows, channels), F32)
    for i in range(3):
        for j in range(3):
            first_row = base + width * i + j - 1
            window = xbuf[first_row : first_row + rows, :]
            if j == 0:
                window = jnp.where(col > 0, window, 0.0)
            if j == 2:
                window = jnp.where(col < width - 1, window, 0.0)
            total = total + mm(window.astype(BF), wc[3 * i + j])
    stage[0:rows, 0:channels] = total
    for r in range(height):
        feat_ref[0, r] = stage[r * width : (r + 1) * width, 0:channels].astype(BF)

    for copy in started:
        copy.wait_send()

    @pl.loop(0, seq)
    def _(d):
        for b in range(4):
            each_o(d, b // 2, b % 2, origin_of(d), lambda copy: copy.wait_send())


def scene_program(seq, *arrays):
    (tokens, f_gain, f_qkv, f_out, g_gain, g_qkv, g_out, h_gain, h_proj, h_bias, h_conv) = arrays
    height, width, dim = tokens.shape[1:]
    real = height * width
    rows = up(real)
    cols = f_qkv.shape[2] // 2
    pairs = cols // LANES
    channels = h_proj.shape[1]
    frame = 4 * rows
    half = rows // 2
    count, most = len(step_list(rows)), max(step[2] for step in step_list(rows))
    vmem = pl.BlockSpec(memory_space=pltpu.VMEM)
    hbm = pl.BlockSpec(memory_space=pltpu.HBM)
    start = (real - width) // TILE * TILE
    slab = max(up(width), rows - start)
    _, copies = sem_layout(seq, count)
    return pl.pallas_call(
        functools.partial(scene_kernel, seq, height, width),
        out_shape=(
            jax.ShapeDtypeStruct(tokens.shape, BF),
            jax.ShapeDtypeStruct((1, height, width, channels), BF),
        ),
        in_specs=[hbm] * 11,
        out_specs=(vmem, vmem),
        scratch_shapes=[
            pltpu.VMEM(tokens.shape, BF),
            pltpu.VMEM((1, dim), F32),
            pltpu.VMEM((1, dim), F32),
            pltpu.VMEM((1, 2 * dim), F32),
            pltpu.VMEM((1, channels), F32),
            pltpu.VMEM((rows, dim), F32),
            pltpu.VMEM((4, rows, dim), BF),
            pltpu.VMEM((3, dim, cols), BF),
            pltpu.VMEM((3, dim, cols), BF),
            pltpu.VMEM((dim, 2 * cols), BF),
            pltpu.VMEM((dim, 2 * cols), BF),
            pltpu.VMEM((2 * cols, dim), BF),
            pltpu.VMEM((4 * cols, dim), BF),
            pltpu.VMEM(h_proj.shape, BF),
            pltpu.VMEM((9, channels, channels), BF),
            pltpu.VMEM((frame, cols), BF),
            pltpu.VMEM((frame, 2 * cols), BF),
            pltpu.VMEM((frame, 2 * cols), BF),
            pltpu.VMEM((count, 2, most, cols), BF),
            pltpu.VMEM((count, most, cols), BF),
            pltpu.VMEM((count, most, dim), F32),
            pltpu.VMEM((count, most, dim), BF),
            pltpu.VMEM((count, most, dim), BF),
            pltpu.VMEM((count, most, dim), BF),
            pltpu.VMEM((count, most, dim), BF),
            pltpu.VMEM((rows, dim), BF),
            pltpu.VMEM((4, rows, cols), F32),
            pltpu.VMEM((seq, frame, LANES), BF),
            pltpu.VMEM((seq * frame, LANES), BF),
            pltpu.VMEM((seq * frame, LANES), BF),
            pltpu.VMEM((seq, 4, half, LANES), BF),
            pltpu.VMEM((seq, 4, half, LANES), BF),
            pltpu.VMEM((seq, 4, half, LANES), BF),
            pltpu.VMEM((4 * seq, half, LANES), BF),
            pltpu.VMEM((rows, 4 * cols), BF),
            pltpu.VMEM((rows, channels), BF),
            pltpu.VMEM((2, slab, channels), BF),
            pltpu.VMEM((up(rows + 2 * width + 2 * TILE), channels), F32),
            pltpu.SemaphoreType.DMA((copies,)),
            pltpu.SemaphoreType.DMA((copies,)),
            pltpu.SemaphoreType.DMA((10 + 4 * pairs,)),
        ],
        compiler_params=pltpu.CompilerParams(
            collective_id=0, has_side_effects=True, vmem_limit_bytes=40 * 2**20
        ),
    )(
        *[
            pltpu.with_memory_space_constraint(array, pltpu.HBM)
            for array in (
                tokens,
                f_gain.reshape(1, -1),
                f_qkv,
                f_out,
                g_gain.reshape(1, -1),
                g_qkv,
                g_out,
                h_gain.reshape(1, -1),
                h_proj,
                h_bias.reshape(1, -1),
                h_conv.reshape(9, channels, channels),
            )
        ]
    )


def routed(mesh, *arrays):
    sizes = mesh.shape
    frames, height, width = arrays[0].shape[:3]
    heads = arrays[2].shape[2] // HD
    fits = (
        sizes["head"] == 2
        and sizes["band"] == 2
        and frames == 1
        and heads == 2 * sizes["seq"]
        and sizes["seq"] & (sizes["seq"] - 1) == 0
        and sizes["seq"] >= 2
        and arrays[0].shape[3] == 2 * arrays[2].shape[2]
        and arrays[10].shape[2] <= arrays[0].shape[3]
        and height * width >= up(width)
        and up(height * width) >= 2 * TILE
    )
    if fits:
        return scene_program(sizes["seq"], *arrays)
    return on_device(*arrays)


def solution(mesh):
    return jax.shard_map(
        functools.partial(routed, mesh),
        mesh=mesh,
        in_specs=(
            P(("scene", "seq"), ("head", "band"), None, None),
            P(),
            P(None, None, "head"),
            P("head", None),
            P(),
            P(None, None, "head"),
            P("head", None),
            P(),
            P(),
            P(),
            P(),
        ),
        out_specs=(
            P(("scene", "seq"), ("head", "band"), None, None),
            P(("scene", "seq"), ("head", "band"), None, None),
        ),
        check_vma=False,
    )
```

```python
import functools
import math

import jax
import jax.numpy as jnp
from jax import lax
from jax.experimental import pallas as pl
from jax.experimental.pallas import tpu as pltpu
from jax.sharding import PartitionSpec as P

HD = 64


norm_eps = 1e-06
head_eps = 1e-05


def padded_2(block, sides, width):
    for axis, dim in sides:
        count = lax.axis_size(axis)
        forward = [(i, i + 1) for i in range(count - 1)]
        backward = [(target, source) for source, target in forward]
        low = lax.ppermute(
            lax.slice_in_dim(block, block.shape[dim] - width, None, axis=dim), axis, forward
        )
        high = lax.ppermute(lax.slice_in_dim(block, 0, width, axis=dim), axis, backward)
        block = jnp.concatenate([low, block, high], axis=dim)
    return block


def layer_norm(values, gain, epsilon):
    centre = values - jnp.mean(values, axis=-1, keepdims=True)
    spread = jnp.mean(centre * centre, axis=-1, keepdims=True)
    return centre * lax.rsqrt(spread + epsilon) * gain


def by_heads(matrix):
    return matrix.reshape(matrix.shape[0], matrix.shape[1] // HD, HD)


def attend_local(queries, keys_all, values_all):
    scores = jnp.einsum(
        "qhd,khd->qhk", by_heads(queries), by_heads(keys_all), preferred_element_type=jnp.float32
    ) * HD ** (-0.5)
    probs = jnp.exp(scores - jnp.max(scores, axis=-1, keepdims=True))
    mixed = jnp.einsum(
        "qhk,khd->qhd",
        probs.astype(jnp.bfloat16),
        by_heads(values_all),
        preferred_element_type=jnp.float32,
    )
    mixed = mixed / jnp.sum(probs, axis=-1)[..., None]
    return mixed.reshape(queries.shape).astype(jnp.bfloat16)


def key_step(local_rows, portion_rows):
    amount = portion_rows // local_rows
    best = 1
    for factor in range(1, amount + 1):
        if amount % factor == 0 and local_rows * factor <= max(local_rows, 1024):
            best = factor
    return local_rows * best


def fresh_carry(queries):
    heads_q = by_heads(queries)
    return (
        jnp.full(heads_q.shape[:2], -jnp.inf, jnp.float32),
        jnp.zeros(heads_q.shape[:2], jnp.float32),
        jnp.zeros(heads_q.shape, jnp.float32),
    )


def finish(carry, queries):
    return (carry[2] / carry[1][..., None]).reshape(queries.shape).astype(jnp.bfloat16)


def fold_keys(queries, carry, portions, local_rows):
    keys_in, values_in = portions
    step_rows = key_step(local_rows, keys_in.shape[0])
    heads_q = by_heads(queries)
    key_blocks = keys_in.reshape(-1, step_rows, keys_in.shape[1])
    value_blocks = values_in.reshape(-1, step_rows, values_in.shape[1])

    def absorb(states, blocks_pair):
        running_max, running_sum, weighted = states
        scores = jnp.einsum(
            "qhd,khd->qhk", heads_q, by_heads(blocks_pair[0]), preferred_element_type=jnp.float32
        ) * HD ** (-0.5)
        new_max = jnp.maximum(running_max, jnp.max(scores, axis=-1))
        decay = jnp.exp(running_max - new_max)
        probs = jnp.exp(scores - new_max[..., None])
        running_sum = running_sum * decay + jnp.sum(probs, axis=-1)
        weighted = weighted * decay[..., None] + jnp.einsum(
            "qhk,khd->qhd",
            probs.astype(jnp.bfloat16),
            by_heads(blocks_pair[1]),
            preferred_element_type=jnp.float32,
        )
        return ((new_max, running_sum, weighted), None)

    carry, ignored = lax.scan(absorb, carry, (key_blocks, value_blocks))
    return carry


def attention_block(inputs, gain, qkv_weight, out_weight, wide):
    normed = layer_norm(inputs.astype(jnp.float32), gain, norm_eps).astype(jnp.bfloat16)
    gathered = lax.all_gather(normed, "head", axis=1, tiled=True)
    flattened = gathered.reshape(-1, gathered.shape[-1])
    query_rows = jnp.dot(flattened, qkv_weight[0], preferred_element_type=jnp.float32).astype(
        jnp.bfloat16
    )
    key_rows = jnp.dot(flattened, qkv_weight[1], preferred_element_type=jnp.float32).astype(
        jnp.bfloat16
    )
    value_rows = jnp.dot(flattened, qkv_weight[2], preferred_element_type=jnp.float32).astype(
        jnp.bfloat16
    )
    if wide:
        carry = fold_keys(
            query_rows,
            fresh_carry(query_rows),
            (
                lax.all_gather(key_rows, ("seq", "band"), axis=0, tiled=True),
                lax.all_gather(value_rows, ("seq", "band"), axis=0, tiled=True),
            ),
            key_rows.shape[0],
        )
        attended = finish(carry, query_rows)
    else:
        keys_all, values_all = (
            lax.all_gather(key_rows, "band", axis=0, tiled=True),
            lax.all_gather(value_rows, "band", axis=0, tiled=True),
        )
        attended = attend_local(query_rows, keys_all, values_all)
    band_rows = inputs.shape[1] * inputs.shape[2]
    own_rows = lax.all_to_all(attended, "head", split_axis=0, concat_axis=1, tiled=True)
    branch = jnp.dot(
        own_rows,
        lax.all_gather(out_weight, "head", axis=0, tiled=True),
        preferred_element_type=jnp.float32,
    )
    merged = inputs.astype(jnp.float32).reshape(band_rows, -1) + branch
    return merged.astype(jnp.bfloat16).reshape(inputs.shape)


def on_device(
    tokens,
    frame_gain,
    frame_qkv,
    frame_out,
    global_gain,
    global_qkv,
    global_out,
    head_gain,
    head_proj,
    head_bias,
    head_conv,
):
    first = attention_block(tokens, frame_gain, frame_qkv, frame_out, False)
    second = attention_block(first, global_gain, global_qkv, global_out, True)
    band_height = tokens.shape[1]
    grid_width = tokens.shape[2]
    stacked = jnp.concatenate([first.astype(jnp.float32), second.astype(jnp.float32)], axis=-1)
    normed = layer_norm(stacked, head_gain, head_eps).astype(jnp.bfloat16)
    projected = (
        jnp.dot(
            normed.reshape(-1, stacked.shape[-1]), head_proj, preferred_element_type=jnp.float32
        )
        + head_bias
    )
    projected = projected.astype(jnp.bfloat16).reshape(
        tokens.shape[0], band_height, grid_width, head_proj.shape[1]
    )
    padded = padded_2(projected, ((("head", "band"), 1),), 1)
    padded = jnp.pad(padded, ((0, 0), (0, 0), (1, 1), (0, 0)))
    totals = jnp.zeros(projected.shape, jnp.float32)
    for offset_row in range(3):
        for offset_col in range(3):
            window = padded[
                :, offset_row : offset_row + band_height, offset_col : offset_col + grid_width
            ]
            totals = totals + jnp.einsum(
                "frcx,xy->frcy",
                window,
                head_conv[offset_row, offset_col],
                preferred_element_type=jnp.float32,
            )
    return (second, totals.astype(jnp.bfloat16))


BF = jnp.bfloat16
F32 = jnp.float32
TILE = 16
LANES = 2 * HD
STEP_SHARES = ((3, 4), (5, 2))
QSCALE = HD ** (-0.5) * math.log2(math.e)


def up(count):
    return -(-count // TILE) * TILE


def mm(a, b):
    return jnp.dot(a, b, preferred_element_type=F32)


def swap(values):
    return pltpu.roll(values, HD, axis=1)


def dot_t(a, b):
    return lax.dot_general(a, b, (((1,), (1,)), ((), ())), preferred_element_type=F32)


def row_parts(rows):
    first = up(rows // 2)
    return [(0, first), (first, rows - first)]


def split_rows(rows, shares):
    units, sizes = rows // TILE, []
    for i, share in enumerate(shares):
        left = units - sum(sizes)
        size = left if i == len(shares) - 1 else max(1, units * share // sum(shares))
        sizes.append(size)
    return [size * TILE for size in sizes if size > 0]


def step_list(rows):
    steps, at = [], 0
    for j, shares in enumerate(STEP_SHARES):
        start = 0
        for size in split_rows(rows, shares):
            steps.append((j, start, size, at))
            at += 2 * size
            start += size
    return steps


def sem_layout(seq, count):
    names = [
        ("tok", 1), ("tok_x", 2), ("tok_f", 2), ("att", count), ("part", count), ("norm", count),
        ("kv", count * seq), ("q", 4 * seq), ("o", 4 * seq), ("go", 2), ("halo", 2),
    ]
    at, table = 0, {}
    for name, size in names:
        table[name] = at
        at += size
    return table, at


def scene_kernel(
    seq,
    height,
    width,
    tok_hbm,
    f_gain_hbm,
    f_qkv,
    f_out,
    g_gain_hbm,
    g_qkv,
    g_out,
    h_gain_hbm,
    h_proj,
    h_bias_hbm,
    h_conv,
    blocks_ref,
    feat_ref,
    tok_ref,
    f_gain,
    g_gain,
    h_gain,
    h_bias,
    stage,
    toks,
    wf,
    wg,
    wkv1,
    wkv2,
    fo,
    go,
    wp,
    wc,
    q1,
    kv1,
    vx1,
    att,
    att_in,
    p_own,
    p_out,
    p_in,
    n_own,
    n_in,
    fst,
    q2,
    skv,
    kv,
    vx,
    sq,
    rq,
    so,
    ro,
    a2,
    pj,
    halo,
    xbuf,
    send,
    recv,
    local,
):
    s, z = lax.axis_index("scene"), lax.axis_index("seq")
    x, c = lax.axis_index("head"), lax.axis_index("band")
    real = height * width
    rows, dim = fst.shape
    cols = wf.shape[2]
    pairs = cols // LANES
    frame = 4 * rows
    half = rows // 2
    steps = step_list(rows)
    parts = row_parts(rows)
    sems, _ = sem_layout(seq, len(steps))
    core, across = (s, z, x, 1 - c), (s, z, 1 - x, c)
    place = 2 * x + c

    def paired(k):
        bits = [1 << i for i in range(seq.bit_length()) if k >> i & 1]
        return z + sum(bit - 2 * bit * lax.rem(lax.div(z, bit), 2) for bit in bits)

    def z_peer(k):
        return (s, paired(k), x, c)

    def remote(name, index, source, target, device, back=None):
        return pltpu.make_async_remote_copy(
            src_ref=source,
            dst_ref=target,
            send_sem=send.at[sems[name] + index],
            recv_sem=recv.at[sems[name] + (index if back is None else back)],
            device_id=device,
            device_id_type=pl.DeviceIdType.MESH,
        )

    barrier = pltpu.get_barrier_semaphore()
    everyone = [core, across, (s, z, 1 - x, 1 - c)] + [z_peer(d) for d in range(1, seq)]
    for device in everyone:
        pl.semaphore_signal(
            barrier, inc=1, device_id=device, device_id_type=pl.DeviceIdType.MESH
        )

    started = []

    def put(name, index, source, target, device):
        copy = remote(name, index, source, target, device)
        copy.start()
        started.append(copy)
        return copy

    own_cols = pl.ds(pl.multiple_of(c * cols, cols), cols)
    loads = []

    def load(source, target):
        copy = pltpu.make_async_copy(source, target, local.at[len(loads)])
        copy.start()
        loads.append(copy)
        return copy

    tok_load = load(tok_hbm, tok_ref)
    f_gain_load = load(f_gain_hbm, f_gain)
    wf_load = load(f_qkv.at[:, :, own_cols], wf)
    fo_loads = []
    for r in range(2):
        owner = c if r == 0 else 1 - c
        for i in range(2 * pairs):
            source = f_out.at[pl.ds(pl.multiple_of(owner * cols + i * HD, HD), HD)]
            fo_loads.append(load(source, fo.at[pl.ds(r * cols + (i ^ 1) * HD, HD)]))
    wg_load = load(g_qkv.at[:, :, own_cols], wg)
    half_rows = pl.ds(pl.multiple_of(x * 2 * cols, 2 * cols), 2 * cols)
    g_gain_load = load(g_gain_hbm, g_gain)
    late_loads = [load(g_out, go.at[half_rows]), load(h_proj, wp), load(h_conv, wc)]
    late_loads += [load(h_gain_hbm, h_gain), load(h_bias_hbm, h_bias)]

    tok_load.wait()
    for r in range(height):
        stage[r * width : (r + 1) * width, :] = tok_ref[0, r].astype(F32)
    for r in range(real, rows):
        stage[r : r + 1, :] = stage[real - 1 : real, :]
    toks[0] = stage[0:rows, :].astype(BF)
    pl.semaphore_wait(barrier, len(everyone))

    tok_x = []
    for k, (start, size) in enumerate(parts):
        at = pl.ds(start, size)
        tok_x.append(put("tok_x", k, toks.at[0, at], toks.at[2, at], across))
    tok_core = put("tok", 0, toks.at[0], toks.at[1], core)

    low = lax.broadcasted_iota(jnp.int32, (1, LANES), 1) < HD
    lane = lax.broadcasted_iota(jnp.int32, (1, 2 * cols), 1)
    v_lanes = lax.rem(lax.div(lane, HD), 4)
    v_lanes = jnp.logical_or(v_lanes == 1, v_lanes == 2)

    def valid_rows(start, size):
        return lax.broadcasted_iota(jnp.int32, (size, 1), 0) + start < real

    f_gain_load.wait()
    wf_load.wait()
    for p in range(pairs):
        at = pl.ds(p * LANES, LANES)
        k_part, v_part = wf[1, :, at], swap(wf[2, :, at].astype(F32)).astype(BF)
        wkv1[:, pl.ds(2 * p * LANES, LANES)] = jnp.where(low, k_part, v_part)
        wkv1[:, pl.ds((2 * p + 1) * LANES, LANES)] = jnp.where(low, v_part, k_part)

    def qkv1(slot, start, size, band):
        n = layer_norm(toks[slot, pl.ds(start, size)].astype(F32), f_gain[...], norm_eps).astype(BF)
        at = pl.ds(pl.multiple_of(band * rows + start, TILE), size)
        q1[at, :] = (mm(n, wf[0]) * QSCALE).astype(BF)
        both = mm(n, wkv1[...]).astype(BF)
        kv1[at, :] = both
        one = jnp.where(v_lanes, both, jnp.ones_like(both))
        vx1[at, :] = jnp.where(valid_rows(start, size), one, jnp.zeros_like(one))

    qkv1(0, 0, rows, place)
    tok_core.wait_recv()
    qkv1(1, 0, rows, 2 * x + 1 - c)
    g_gain_load.wait()
    wg_load.wait()
    for p in range(pairs):
        at = pl.ds(p * LANES, LANES)
        k_part, v_part = wg[1, :, at], wg[2, :, at]
        k_swap, v_swap = swap(k_part.astype(F32)).astype(BF), swap(v_part.astype(F32)).astype(BF)
        wkv2[:, pl.ds(2 * p * LANES, LANES)] = jnp.where(low, k_part, v_swap)
        wkv2[:, pl.ds((2 * p + 1) * LANES, LANES)] = jnp.where(low, k_swap, v_part)
    tok_f = []
    for k, (start, size) in enumerate(parts):
        at = pl.ds(start, size)
        tok_x[k].wait_recv()
        tok_f.append(put("tok_f", k, toks.at[2, at], toks.at[3, at], core))
        qkv1(2, start, size, 2 * (1 - x) + c)
    for k, (start, size) in enumerate(parts):
        tok_f[k].wait_recv()
        qkv1(3, start, size, 2 * (1 - x) + 1 - c)

    att_copies, p_copies, n_copies = [], [], []

    def attend(k, p):
        j, start, size, _ = steps[k]
        at = pl.ds(p * LANES, LANES)
        qp = jnp.concatenate(
            [q1[pl.ds((2 * j + b) * rows + start, size), at] for b in range(2)], axis=0
        )
        mixed = []
        for e in range(2):
            tile = pl.ds((2 * p + e) * LANES, LANES)
            zero = jnp.zeros_like(qp)
            lhs = jnp.where(low, qp, zero) if e == 0 else jnp.where(low, zero, qp)
            scores = dot_t(lhs, kv1[:, tile])
            probs = jnp.exp2(scores - jnp.max(scores, axis=-1, keepdims=True))
            mixed.append(mm(probs.astype(BF), vx1[:, tile]))
        top = jnp.where(low, mixed[1], mixed[0])
        bottom = swap(jnp.where(low, mixed[0], mixed[1]))
        out = (top / bottom).astype(BF)
        for b in range(2):
            att[k, b, pl.ds(0, size), at] = out[b * size : (b + 1) * size]

    def send_att(k):
        at = pl.ds(0, steps[k][2])
        att_copies.append(put("att", k, att.at[k, 1 - c, at], att_in.at[k, at], core))

    def project(k):
        j, start, size, _ = steps[k]
        at = pl.ds(0, size)
        att_copies[k].wait_recv()
        lhs = jnp.concatenate([att[k, c, at], att_in[k, at]], axis=1)
        partial = mm(lhs, fo[...])
        p_own[k, at] = partial
        p_out[k, at] = partial.astype(BF)
        p_copies.append(put("part", k, p_out.at[k, at], p_in.at[k, at], across))

    def norm2(k):
        j, start, size, _ = steps[k]
        at = pl.ds(0, size)
        slot = jnp.where(x == j, 0, 2)
        p_copies[k].wait_recv()
        tok = toks[slot, pl.ds(start, size)].astype(F32)
        first = (tok + p_own[k, at] + p_in[k, at].astype(F32)).astype(BF)

        @pl.when(x == j)
        def _():
            fst[pl.ds(start, size), :] = first

        n_own[k, at] = layer_norm(first.astype(F32), g_gain[...], norm_eps).astype(BF)
        n_copies.append(put("norm", k, n_own.at[k, at], n_in.at[k, at], core))

    kv_copies = [[] for _ in range(seq)]

    def qkv2(k):
        j, start, size, offset = steps[k]
        n_copies[k].wait_recv()
        at = pl.ds(0, size)
        n = jnp.concatenate([n_own[k, at], n_in[k, at]], axis=0)
        both = mm(n, wkv2[...]).astype(BF)
        for h in range(2 * pairs):
            skv[h, pl.ds(offset, 2 * size), :] = both[:, h * LANES : (h + 1) * LANES]
        to = pl.ds(pl.multiple_of(z * frame + offset, TILE), 2 * size)
        for d in range(1, seq):
            source = skv.at[paired(d), pl.ds(offset, 2 * size)]
            kv_copies[d].append(put("kv", k * seq + d, source, kv.at[to], z_peer(d)))
        kv[to, :] = skv[z, pl.ds(offset, 2 * size), :]
        queries = mm(n, wg[0]) * QSCALE
        q2[2 * j + c, pl.ds(start, size), :] = queries[:size]
        q2[2 * j + 1 - c, pl.ds(start, size), :] = queries[size:]

    for copy in fo_loads:
        copy.wait()
    for p in range(pairs):
        attend(0, p)
    send_att(0)
    for k in range(1, len(steps)):
        for p in range(pairs):
            attend(k, p)
            if p == 0:
                project(k - 1)
        send_att(k)
    project(len(steps) - 1)
    go_part = pl.ds(pl.multiple_of(x * 2 * cols + c * cols, cols), cols)
    go_from = pl.ds(pl.multiple_of((1 - x) * 2 * cols + c * cols, cols), cols)
    go_x = put("go", 0, g_out.at[own_cols], go.at[go_part], across)
    for k in range(len(steps)):
        norm2(k)
        qkv2(k)
    for b in range(4):
        for p in range(pairs):
            tile = q2[b, :, pl.ds(p * LANES, LANES)]
            top, under = tile[:half], tile[half:]
            sq[2 * p, b] = jnp.where(low, top, swap(under)).astype(BF)
            sq[2 * p + 1, b] = jnp.where(low, swap(top), under).astype(BF)
    for pair in range(2):
        for d in range(1, seq):
            bands = pl.ds(2 * pair, 2)
            put("q", pair * seq + d, sq.at[paired(d), bands], rq.at[z, bands], z_peer(d))
    rq[z] = sq[z]

    frame_valid = jnp.concatenate(
        [valid_rows(start, size) for j, start, size, _ in steps for b in range(2)], axis=0
    )

    def spread(origin):
        at = pl.ds(pl.multiple_of(origin * frame, frame), frame)
        both = kv[at, :]
        one = jnp.where(low, jnp.ones_like(both), both)
        vx[at, :] = jnp.where(frame_valid, one, jnp.zeros_like(one))

    spread(z)
    for d in range(1, seq):
        for copy in kv_copies[d]:
            copy.wait_recv()
        spread(paired(d))

    mine = place * seq + z

    def q_copy(d, pair, origin):
        device, bands = (s, origin, x, c), pl.ds(2 * pair, 2)
        return remote("q", pair * seq + d, sq.at[0, bands], rq.at[origin, bands], device)

    def o_copy(d, pair, i, origin):
        b = 2 * pair + i
        device = (s, origin, pair, i)
        return remote("o", d * 4 + b, so.at[d, b], ro.at[mine], device, mine)

    def origin_of(d):
        origin = z
        for i in range((seq - 1).bit_length()):
            bit = 1 << i
            flip = lax.rem(lax.div(d, bit), 2)
            origin = origin + flip * (bit - 2 * bit * lax.rem(lax.div(z, bit), 2))
        return origin

    def each_o(d, pair, i, origin, act):
        itself = jnp.logical_and(d == 0, place == 2 * pair + i)

        @pl.when(jnp.logical_not(itself))
        def _():
            act(o_copy(d, pair, i, origin))

    @pl.loop(0, 2 * seq // 2)
    def _(turn):
        pair = lax.div(turn, seq // 2)
        group = lax.rem(turn, seq // 2)
        group = group + pair * (seq // 2 - 1 - 2 * group)
        ds = [2 * group + i for i in range(2)]
        origins = [origin_of(d) for d in ds]
        for d, origin in zip(ds, origins):

            @pl.when(d > 0)
            def _():
                q_copy(d, pair, origin).wait_recv()

        for d, origin in zip(ds, origins):
            q = []
            for i in range(2):
                packed = rq[origin, 2 * pair + i].astype(F32)
                q += [packed, swap(packed)]
            q = jnp.where(low, jnp.concatenate(q, axis=0), 0.0).astype(BF)
            scores = dot_t(q, kv[...])
            probs = jnp.exp2(scores - jnp.max(scores, axis=-1, keepdims=True))
            mixed = mm(probs.astype(BF), vx[...])
            out = mixed / jnp.where(low, 1.0, swap(mixed))
            for i in range(2):
                o = out[i * rows : (i + 1) * rows]
                so[d, 2 * pair + i] = jnp.where(low, swap(o)[:half], o[half:]).astype(BF)
                each_o(d, pair, i, origin, lambda copy: copy.start())

    ro_own = so[0, place]
    ro[mine] = ro_own
    go_x.wait_recv()
    go_f = put("go", 1, go.at[go_from], go.at[go_from], core)
    for copy in late_loads:
        copy.wait()
    for slot in range(4 * seq):

        @pl.when(slot != mine)
        def _():
            remote("o", 0, so.at[0, 0], ro.at[slot], core, slot).wait_recv()

    for i in range(2 * seq):
        at = pl.ds(i * LANES, LANES)
        even, odd = ro[2 * i].astype(F32), ro[2 * i + 1].astype(F32)
        pair = [jnp.where(low, even, swap(odd)), jnp.where(low, swap(even), odd)]
        a2[:, at] = jnp.concatenate(pair, axis=0).astype(BF)
    first = fst[...].astype(F32)
    go_f.wait_recv()
    second = (first + mm(a2[...], go[...])).astype(BF).astype(F32)
    stacked = jnp.concatenate([first, second], axis=-1)
    n3 = layer_norm(stacked, h_gain[...], head_eps).astype(BF)
    pj[...] = (mm(n3, wp[...]) + h_bias[...]).astype(BF)

    after = lax.rem(place + 1, 4)
    before = lax.rem(place + 3, 4)

    def frame_peer(index):
        return (s, z, index // 2, lax.rem(index, 2))

    start = (real - width) // TILE * TILE
    slab = halo.shape[1]
    down = put(
        "halo", 0, pj.at[pl.ds(start, rows - start)], halo.at[0, pl.ds(0, rows - start)],
        frame_peer(after),
    )
    upward = put("halo", 1, pj.at[pl.ds(0, slab)], halo.at[1], frame_peer(before))
    stage[0:rows, :] = second
    for r in range(height):
        blocks_ref[0, r] = stage[r * width : (r + 1) * width, :].astype(BF)
    base = 8
    xbuf[...] = jnp.zeros_like(xbuf)
    xbuf[base + width : base + width + real, :] = pj[...].astype(F32)[:real]
    down.wait_recv()
    upward.wait_recv()
    skip = real - width - start
    lower = jnp.where(place > 0, halo[0].astype(F32), 0.0)
    upper = jnp.where(place < 3, halo[1].astype(F32), 0.0)
    xbuf[base : base + width, :] = lower[skip : skip + width]
    xbuf[base + width + real : base + 2 * width + real, :] = upper[:width]
    col = lax.rem(lax.broadcasted_iota(jnp.int32, (rows, 1), 0), width)
    channels = pj.shape[1]
    total = jnp.zeros((rows, channels), F32)
    for i in range(3):
        for j in range(3):
            first_row = base + width * i + j - 1
            window = xbuf[first_row : first_row + rows, :]
            if j == 0:
                window = jnp.where(col > 0, window, 0.0)
            if j == 2:
                window = jnp.where(col < width - 1, window, 0.0)
            total = total + mm(window.astype(BF), wc[3 * i + j])
    stage[0:rows, 0:channels] = total
    for r in range(height):
        feat_ref[0, r] = stage[r * width : (r + 1) * width, 0:channels].astype(BF)

    for copy in started:
        copy.wait_send()

    @pl.loop(0, seq)
    def _(d):
        for b in range(4):
            each_o(d, b // 2, b % 2, origin_of(d), lambda copy: copy.wait_send())


def scene_program(seq, *arrays):
    (tokens, f_gain, f_qkv, f_out, g_gain, g_qkv, g_out, h_gain, h_proj, h_bias, h_conv) = arrays
    height, width, dim = tokens.shape[1:]
    real = height * width
    rows = up(real)
    cols = f_qkv.shape[2] // 2
    pairs = cols // LANES
    channels = h_proj.shape[1]
    frame = 4 * rows
    half = rows // 2
    count, most = len(step_list(rows)), max(step[2] for step in step_list(rows))
    vmem = pl.BlockSpec(memory_space=pltpu.VMEM)
    hbm = pl.BlockSpec(memory_space=pltpu.HBM)
    start = (real - width) // TILE * TILE
    slab = max(up(width), rows - start)
    _, copies = sem_layout(seq, count)
    return pl.pallas_call(
        functools.partial(scene_kernel, seq, height, width),
        out_shape=(
            jax.ShapeDtypeStruct(tokens.shape, BF),
            jax.ShapeDtypeStruct((1, height, width, channels), BF),
        ),
        in_specs=[hbm] * 11,
        out_specs=(vmem, vmem),
        scratch_shapes=[
            pltpu.VMEM(tokens.shape, BF),
            pltpu.VMEM((1, dim), F32),
            pltpu.VMEM((1, dim), F32),
            pltpu.VMEM((1, 2 * dim), F32),
            pltpu.VMEM((1, channels), F32),
            pltpu.VMEM((rows, dim), F32),
            pltpu.VMEM((4, rows, dim), BF),
            pltpu.VMEM((3, dim, cols), BF),
            pltpu.VMEM((3, dim, cols), BF),
            pltpu.VMEM((dim, 2 * cols), BF),
            pltpu.VMEM((dim, 2 * cols), BF),
            pltpu.VMEM((2 * cols, dim), BF),
            pltpu.VMEM((4 * cols, dim), BF),
            pltpu.VMEM(h_proj.shape, BF),
            pltpu.VMEM((9, channels, channels), BF),
            pltpu.VMEM((frame, cols), BF),
            pltpu.VMEM((frame, 2 * cols), BF),
            pltpu.VMEM((frame, 2 * cols), BF),
            pltpu.VMEM((count, 2, most, cols), BF),
            pltpu.VMEM((count, most, cols), BF),
            pltpu.VMEM((count, most, dim), F32),
            pltpu.VMEM((count, most, dim), BF),
            pltpu.VMEM((count, most, dim), BF),
            pltpu.VMEM((count, most, dim), BF),
            pltpu.VMEM((count, most, dim), BF),
            pltpu.VMEM((rows, dim), BF),
            pltpu.VMEM((4, rows, cols), F32),
            pltpu.VMEM((seq, frame, LANES), BF),
            pltpu.VMEM((seq * frame, LANES), BF),
            pltpu.VMEM((seq * frame, LANES), BF),
            pltpu.VMEM((seq, 4, half, LANES), BF),
            pltpu.VMEM((seq, 4, half, LANES), BF),
            pltpu.VMEM((seq, 4, half, LANES), BF),
            pltpu.VMEM((4 * seq, half, LANES), BF),
            pltpu.VMEM((rows, 4 * cols), BF),
            pltpu.VMEM((rows, channels), BF),
            pltpu.VMEM((2, slab, channels), BF),
            pltpu.VMEM((up(rows + 2 * width + 2 * TILE), channels), F32),
            pltpu.SemaphoreType.DMA((copies,)),
            pltpu.SemaphoreType.DMA((copies,)),
            pltpu.SemaphoreType.DMA((10 + 4 * pairs,)),
        ],
        compiler_params=pltpu.CompilerParams(
            collective_id=0, has_side_effects=True, vmem_limit_bytes=40 * 2**20
        ),
    )(
        *[
            pltpu.with_memory_space_constraint(array, pltpu.HBM)
            for array in (
                tokens,
                f_gain.reshape(1, -1),
                f_qkv,
                f_out,
                g_gain.reshape(1, -1),
                g_qkv,
                g_out,
                h_gain.reshape(1, -1),
                h_proj,
                h_bias.reshape(1, -1),
                h_conv.reshape(9, channels, channels),
            )
        ]
    )


def routed(mesh, *arrays):
    sizes = mesh.shape
    frames, height, width = arrays[0].shape[:3]
    heads = arrays[2].shape[2] // HD
    fits = (
        sizes["head"] == 2
        and sizes["band"] == 2
        and frames == 1
        and heads == 2 * sizes["seq"]
        and sizes["seq"] & (sizes["seq"] - 1) == 0
        and sizes["seq"] >= 2
        and arrays[0].shape[3] == 2 * arrays[2].shape[2]
        and arrays[10].shape[2] <= arrays[0].shape[3]
        and height * width >= up(width)
        and up(height * width) >= 2 * TILE
    )
    if fits:
        return scene_program(sizes["seq"], *arrays)
    return on_device(*arrays)


def solution(mesh):
    return jax.shard_map(
        functools.partial(routed, mesh),
        mesh=mesh,
        in_specs=(
            P(("scene", "seq"), ("head", "band"), None, None),
            P(),
            P(None, None, "head"),
            P("head", None),
            P(),
            P(None, None, "head"),
            P("head", None),
            P(),
            P(),
            P(),
            P(),
        ),
        out_specs=(
            P(("scene", "seq"), ("head", "band"), None, None),
            P(("scene", "seq"), ("head", "band"), None, None),
        ),
        check_vma=False,
    )
```

```python
import functools
import math

import jax
import jax.numpy as jnp
from jax import lax
from jax.experimental import pallas as pl
from jax.experimental.pallas import tpu as pltpu
from jax.sharding import PartitionSpec as P

HD = 64


norm_eps = 1e-06
head_eps = 1e-05


def padded_2(block, sides, width):
    for axis, dim in sides:
        count = lax.axis_size(axis)
        forward = [(i, i + 1) for i in range(count - 1)]
        backward = [(target, source) for source, target in forward]
        low = lax.ppermute(
            lax.slice_in_dim(block, block.shape[dim] - width, None, axis=dim), axis, forward
        )
        high = lax.ppermute(lax.slice_in_dim(block, 0, width, axis=dim), axis, backward)
        block = jnp.concatenate([low, block, high], axis=dim)
    return block


def layer_norm(values, gain, epsilon):
    centre = values - jnp.mean(values, axis=-1, keepdims=True)
    spread = jnp.mean(centre * centre, axis=-1, keepdims=True)
    return centre * lax.rsqrt(spread + epsilon) * gain


def by_heads(matrix):
    return matrix.reshape(matrix.shape[0], matrix.shape[1] // HD, HD)


def attend_local(queries, keys_all, values_all):
    scores = jnp.einsum(
        "qhd,khd->qhk", by_heads(queries), by_heads(keys_all), preferred_element_type=jnp.float32
    ) * HD ** (-0.5)
    probs = jnp.exp(scores - jnp.max(scores, axis=-1, keepdims=True))
    mixed = jnp.einsum(
        "qhk,khd->qhd",
        probs.astype(jnp.bfloat16),
        by_heads(values_all),
        preferred_element_type=jnp.float32,
    )
    mixed = mixed / jnp.sum(probs, axis=-1)[..., None]
    return mixed.reshape(queries.shape).astype(jnp.bfloat16)


def key_step(local_rows, portion_rows):
    amount = portion_rows // local_rows
    best = 1
    for factor in range(1, amount + 1):
        if amount % factor == 0 and local_rows * factor <= max(local_rows, 1024):
            best = factor
    return local_rows * best


def fresh_carry(queries):
    heads_q = by_heads(queries)
    return (
        jnp.full(heads_q.shape[:2], -jnp.inf, jnp.float32),
        jnp.zeros(heads_q.shape[:2], jnp.float32),
        jnp.zeros(heads_q.shape, jnp.float32),
    )


def finish(carry, queries):
    return (carry[2] / carry[1][..., None]).reshape(queries.shape).astype(jnp.bfloat16)


def fold_keys(queries, carry, portions, local_rows):
    keys_in, values_in = portions
    step_rows = key_step(local_rows, keys_in.shape[0])
    heads_q = by_heads(queries)
    key_blocks = keys_in.reshape(-1, step_rows, keys_in.shape[1])
    value_blocks = values_in.reshape(-1, step_rows, values_in.shape[1])

    def absorb(states, blocks_pair):
        running_max, running_sum, weighted = states
        scores = jnp.einsum(
            "qhd,khd->qhk", heads_q, by_heads(blocks_pair[0]), preferred_element_type=jnp.float32
        ) * HD ** (-0.5)
        new_max = jnp.maximum(running_max, jnp.max(scores, axis=-1))
        decay = jnp.exp(running_max - new_max)
        probs = jnp.exp(scores - new_max[..., None])
        running_sum = running_sum * decay + jnp.sum(probs, axis=-1)
        weighted = weighted * decay[..., None] + jnp.einsum(
            "qhk,khd->qhd",
            probs.astype(jnp.bfloat16),
            by_heads(blocks_pair[1]),
            preferred_element_type=jnp.float32,
        )
        return ((new_max, running_sum, weighted), None)

    carry, ignored = lax.scan(absorb, carry, (key_blocks, value_blocks))
    return carry


def attention_block(inputs, gain, qkv_weight, out_weight, wide):
    normed = layer_norm(inputs.astype(jnp.float32), gain, norm_eps).astype(jnp.bfloat16)
    gathered = lax.all_gather(normed, "head", axis=1, tiled=True)
    flattened = gathered.reshape(-1, gathered.shape[-1])
    query_rows = jnp.dot(flattened, qkv_weight[0], preferred_element_type=jnp.float32).astype(
        jnp.bfloat16
    )
    key_rows = jnp.dot(flattened, qkv_weight[1], preferred_element_type=jnp.float32).astype(
        jnp.bfloat16
    )
    value_rows = jnp.dot(flattened, qkv_weight[2], preferred_element_type=jnp.float32).astype(
        jnp.bfloat16
    )
    if wide:
        carry = fold_keys(
            query_rows,
            fresh_carry(query_rows),
            (
                lax.all_gather(key_rows, ("seq", "band"), axis=0, tiled=True),
                lax.all_gather(value_rows, ("seq", "band"), axis=0, tiled=True),
            ),
            key_rows.shape[0],
        )
        attended = finish(carry, query_rows)
    else:
        keys_all, values_all = (
            lax.all_gather(key_rows, "band", axis=0, tiled=True),
            lax.all_gather(value_rows, "band", axis=0, tiled=True),
        )
        attended = attend_local(query_rows, keys_all, values_all)
    band_rows = inputs.shape[1] * inputs.shape[2]
    own_rows = lax.all_to_all(attended, "head", split_axis=0, concat_axis=1, tiled=True)
    branch = jnp.dot(
        own_rows,
        lax.all_gather(out_weight, "head", axis=0, tiled=True),
        preferred_element_type=jnp.float32,
    )
    merged = inputs.astype(jnp.float32).reshape(band_rows, -1) + branch
    return merged.astype(jnp.bfloat16).reshape(inputs.shape)


def on_device(
    tokens,
    frame_gain,
    frame_qkv,
    frame_out,
    global_gain,
    global_qkv,
    global_out,
    head_gain,
    head_proj,
    head_bias,
    head_conv,
):
    first = attention_block(tokens, frame_gain, frame_qkv, frame_out, False)
    second = attention_block(first, global_gain, global_qkv, global_out, True)
    band_height = tokens.shape[1]
    grid_width = tokens.shape[2]
    stacked = jnp.concatenate([first.astype(jnp.float32), second.astype(jnp.float32)], axis=-1)
    normed = layer_norm(stacked, head_gain, head_eps).astype(jnp.bfloat16)
    projected = (
        jnp.dot(
            normed.reshape(-1, stacked.shape[-1]), head_proj, preferred_element_type=jnp.float32
        )
        + head_bias
    )
    projected = projected.astype(jnp.bfloat16).reshape(
        tokens.shape[0], band_height, grid_width, head_proj.shape[1]
    )
    padded = padded_2(projected, ((("head", "band"), 1),), 1)
    padded = jnp.pad(padded, ((0, 0), (0, 0), (1, 1), (0, 0)))
    totals = jnp.zeros(projected.shape, jnp.float32)
    for offset_row in range(3):
        for offset_col in range(3):
            window = padded[
                :, offset_row : offset_row + band_height, offset_col : offset_col + grid_width
            ]
            totals = totals + jnp.einsum(
                "frcx,xy->frcy",
                window,
                head_conv[offset_row, offset_col],
                preferred_element_type=jnp.float32,
            )
    return (second, totals.astype(jnp.bfloat16))


BF = jnp.bfloat16
F32 = jnp.float32
TILE = 16
LANES = 2 * HD
STEP_SHARES = ((3, 4), (6, 1))
QSCALE = HD ** (-0.5) * math.log2(math.e)


def up(count):
    return -(-count // TILE) * TILE


def mm(a, b):
    return jnp.dot(a, b, preferred_element_type=F32)


def swap(values):
    return pltpu.roll(values, HD, axis=1)


def dot_t(a, b):
    return lax.dot_general(a, b, (((1,), (1,)), ((), ())), preferred_element_type=F32)


def row_parts(rows):
    first = up(rows // 2)
    return [(0, first), (first, rows - first)]


def split_rows(rows, shares):
    units, sizes = rows // TILE, []
    for i, share in enumerate(shares):
        left = units - sum(sizes)
        size = left if i == len(shares) - 1 else max(1, units * share // sum(shares))
        sizes.append(size)
    return [size * TILE for size in sizes if size > 0]


def step_list(rows):
    steps, at = [], 0
    for j, shares in enumerate(STEP_SHARES):
        start = 0
        for size in split_rows(rows, shares):
            steps.append((j, start, size, at))
            at += 2 * size
            start += size
    return steps


def sem_layout(seq, count):
    names = [
        ("tok", 1), ("tok_x", 2), ("tok_f", 2), ("att", count), ("part", count), ("norm", count),
        ("kv", count * seq), ("q", 4 * seq), ("o", 4 * seq), ("go", 2), ("halo", 2),
    ]
    at, table = 0, {}
    for name, size in names:
        table[name] = at
        at += size
    return table, at


def scene_kernel(
    seq,
    height,
    width,
    tok_hbm,
    f_gain_hbm,
    f_qkv,
    f_out,
    g_gain_hbm,
    g_qkv,
    g_out,
    h_gain_hbm,
    h_proj,
    h_bias_hbm,
    h_conv,
    blocks_ref,
    feat_ref,
    tok_ref,
    f_gain,
    g_gain,
    h_gain,
    h_bias,
    stage,
    toks,
    wf,
    wg,
    wkv1,
    wkv2,
    fo,
    go,
    wp,
    wc,
    q1,
    kv1,
    vx1,
    att,
    att_in,
    p_own,
    p_out,
    p_in,
    n_own,
    n_in,
    fst,
    q2,
    skv,
    kv,
    vx,
    sq,
    rq,
    so,
    ro,
    a2,
    pj,
    halo,
    xbuf,
    send,
    recv,
    local,
):
    s, z = lax.axis_index("scene"), lax.axis_index("seq")
    x, c = lax.axis_index("head"), lax.axis_index("band")
    real = height * width
    rows, dim = fst.shape
    cols = wf.shape[2]
    pairs = cols // LANES
    frame = 4 * rows
    half = rows // 2
    steps = step_list(rows)
    parts = row_parts(rows)
    sems, _ = sem_layout(seq, len(steps))
    core, across = (s, z, x, 1 - c), (s, z, 1 - x, c)
    place = 2 * x + c

    def paired(k):
        bits = [1 << i for i in range(seq.bit_length()) if k >> i & 1]
        return z + sum(bit - 2 * bit * lax.rem(lax.div(z, bit), 2) for bit in bits)

    def z_peer(k):
        return (s, paired(k), x, c)

    def remote(name, index, source, target, device, back=None):
        return pltpu.make_async_remote_copy(
            src_ref=source,
            dst_ref=target,
            send_sem=send.at[sems[name] + index],
            recv_sem=recv.at[sems[name] + (index if back is None else back)],
            device_id=device,
            device_id_type=pl.DeviceIdType.MESH,
        )

    barrier = pltpu.get_barrier_semaphore()
    everyone = [core, across, (s, z, 1 - x, 1 - c)] + [z_peer(d) for d in range(1, seq)]
    for device in everyone:
        pl.semaphore_signal(
            barrier, inc=1, device_id=device, device_id_type=pl.DeviceIdType.MESH
        )

    started = []

    def put(name, index, source, target, device):
        copy = remote(name, index, source, target, device)
        copy.start()
        started.append(copy)
        return copy

    own_cols = pl.ds(pl.multiple_of(c * cols, cols), cols)
    loads = []

    def load(source, target):
        copy = pltpu.make_async_copy(source, target, local.at[len(loads)])
        copy.start()
        loads.append(copy)
        return copy

    tok_load = load(tok_hbm, tok_ref)
    f_gain_load = load(f_gain_hbm, f_gain)
    wf_load = load(f_qkv.at[:, :, own_cols], wf)
    fo_loads = []
    for r in range(2):
        owner = c if r == 0 else 1 - c
        for i in range(2 * pairs):
            source = f_out.at[pl.ds(pl.multiple_of(owner * cols + i * HD, HD), HD)]
            fo_loads.append(load(source, fo.at[pl.ds(r * cols + (i ^ 1) * HD, HD)]))
    wg_load = load(g_qkv.at[:, :, own_cols], wg)
    half_rows = pl.ds(pl.multiple_of(x * 2 * cols, 2 * cols), 2 * cols)
    g_gain_load = load(g_gain_hbm, g_gain)
    late_loads = [load(g_out, go.at[half_rows]), load(h_proj, wp), load(h_conv, wc)]
    late_loads += [load(h_gain_hbm, h_gain), load(h_bias_hbm, h_bias)]

    tok_load.wait()
    for r in range(height):
        stage[r * width : (r + 1) * width, :] = tok_ref[0, r].astype(F32)
    for r in range(real, rows):
        stage[r : r + 1, :] = stage[real - 1 : real, :]
    toks[0] = stage[0:rows, :].astype(BF)
    pl.semaphore_wait(barrier, len(everyone))

    tok_x = []
    for k, (start, size) in enumerate(parts):
        at = pl.ds(start, size)
        tok_x.append(put("tok_x", k, toks.at[0, at], toks.at[2, at], across))
    tok_core = put("tok", 0, toks.at[0], toks.at[1], core)

    low = lax.broadcasted_iota(jnp.int32, (1, LANES), 1) < HD
    lane = lax.broadcasted_iota(jnp.int32, (1, 2 * cols), 1)
    v_lanes = lax.rem(lax.div(lane, HD), 4)
    v_lanes = jnp.logical_or(v_lanes == 1, v_lanes == 2)

    def valid_rows(start, size):
        return lax.broadcasted_iota(jnp.int32, (size, 1), 0) + start < real

    f_gain_load.wait()
    wf_load.wait()
    for p in range(pairs):
        at = pl.ds(p * LANES, LANES)
        k_part, v_part = wf[1, :, at], swap(wf[2, :, at].astype(F32)).astype(BF)
        wkv1[:, pl.ds(2 * p * LANES, LANES)] = jnp.where(low, k_part, v_part)
        wkv1[:, pl.ds((2 * p + 1) * LANES, LANES)] = jnp.where(low, v_part, k_part)

    def qkv1(slot, start, size, band):
        n = layer_norm(toks[slot, pl.ds(start, size)].astype(F32), f_gain[...], norm_eps).astype(BF)
        at = pl.ds(pl.multiple_of(band * rows + start, TILE), size)
        q1[at, :] = (mm(n, wf[0]) * QSCALE).astype(BF)
        both = mm(n, wkv1[...]).astype(BF)
        kv1[at, :] = both
        one = jnp.where(v_lanes, both, jnp.ones_like(both))
        vx1[at, :] = jnp.where(valid_rows(start, size), one, jnp.zeros_like(one))

    qkv1(0, 0, rows, place)
    tok_core.wait_recv()
    qkv1(1, 0, rows, 2 * x + 1 - c)
    g_gain_load.wait()
    wg_load.wait()
    for p in range(pairs):
        at = pl.ds(p * LANES, LANES)
        k_part, v_part = wg[1, :, at], wg[2, :, at]
        k_swap, v_swap = swap(k_part.astype(F32)).astype(BF), swap(v_part.astype(F32)).astype(BF)
        wkv2[:, pl.ds(2 * p * LANES, LANES)] = jnp.where(low, k_part, v_swap)
        wkv2[:, pl.ds((2 * p + 1) * LANES, LANES)] = jnp.where(low, k_swap, v_part)
    tok_f = []
    for k, (start, size) in enumerate(parts):
        at = pl.ds(start, size)
        tok_x[k].wait_recv()
        tok_f.append(put("tok_f", k, toks.at[2, at], toks.at[3, at], core))
        qkv1(2, start, size, 2 * (1 - x) + c)
    for k, (start, size) in enumerate(parts):
        tok_f[k].wait_recv()
        qkv1(3, start, size, 2 * (1 - x) + 1 - c)

    att_copies, p_copies, n_copies = [], [], []

    def attend(k, p):
        j, start, size, _ = steps[k]
        at = pl.ds(p * LANES, LANES)
        qp = jnp.concatenate(
            [q1[pl.ds((2 * j + b) * rows + start, size), at] for b in range(2)], axis=0
        )
        mixed = []
        for e in range(2):
            tile = pl.ds((2 * p + e) * LANES, LANES)
            zero = jnp.zeros_like(qp)
            lhs = jnp.where(low, qp, zero) if e == 0 else jnp.where(low, zero, qp)
            scores = dot_t(lhs, kv1[:, tile])
            probs = jnp.exp2(scores - jnp.max(scores, axis=-1, keepdims=True))
            mixed.append(mm(probs.astype(BF), vx1[:, tile]))
        top = jnp.where(low, mixed[1], mixed[0])
        bottom = swap(jnp.where(low, mixed[0], mixed[1]))
        out = (top / bottom).astype(BF)
        for b in range(2):
            att[k, b, pl.ds(0, size), at] = out[b * size : (b + 1) * size]

    def send_att(k):
        at = pl.ds(0, steps[k][2])
        att_copies.append(put("att", k, att.at[k, 1 - c, at], att_in.at[k, at], core))

    def project(k):
        j, start, size, _ = steps[k]
        at = pl.ds(0, size)
        att_copies[k].wait_recv()
        lhs = jnp.concatenate([att[k, c, at], att_in[k, at]], axis=1)
        partial = mm(lhs, fo[...])
        p_own[k, at] = partial
        p_out[k, at] = partial.astype(BF)
        p_copies.append(put("part", k, p_out.at[k, at], p_in.at[k, at], across))

    def norm2(k):
        j, start, size, _ = steps[k]
        at = pl.ds(0, size)
        slot = jnp.where(x == j, 0, 2)
        p_copies[k].wait_recv()
        tok = toks[slot, pl.ds(start, size)].astype(F32)
        first = (tok + p_own[k, at] + p_in[k, at].astype(F32)).astype(BF)

        @pl.when(x == j)
        def _():
            fst[pl.ds(start, size), :] = first

        n_own[k, at] = layer_norm(first.astype(F32), g_gain[...], norm_eps).astype(BF)
        n_copies.append(put("norm", k, n_own.at[k, at], n_in.at[k, at], core))

    kv_copies = [[] for _ in range(seq)]

    def qkv2(k):
        j, start, size, offset = steps[k]
        n_copies[k].wait_recv()
        at = pl.ds(0, size)
        n = jnp.concatenate([n_own[k, at], n_in[k, at]], axis=0)
        both = mm(n, wkv2[...]).astype(BF)
        for h in range(2 * pairs):
            skv[h, pl.ds(offset, 2 * size), :] = both[:, h * LANES : (h + 1) * LANES]
        to = pl.ds(pl.multiple_of(z * frame + offset, TILE), 2 * size)
        for d in range(1, seq):
            source = skv.at[paired(d), pl.ds(offset, 2 * size)]
            kv_copies[d].append(put("kv", k * seq + d, source, kv.at[to], z_peer(d)))
        kv[to, :] = skv[z, pl.ds(offset, 2 * size), :]
        queries = mm(n, wg[0]) * QSCALE
        q2[2 * j + c, pl.ds(start, size), :] = queries[:size]
        q2[2 * j + 1 - c, pl.ds(start, size), :] = queries[size:]

    for copy in fo_loads:
        copy.wait()
    for p in range(pairs):
        attend(0, p)
    send_att(0)
    for k in range(1, len(steps)):
        for p in range(pairs):
            attend(k, p)
            if p == 0:
                project(k - 1)
        send_att(k)
    project(len(steps) - 1)
    go_part = pl.ds(pl.multiple_of(x * 2 * cols + c * cols, cols), cols)
    go_from = pl.ds(pl.multiple_of((1 - x) * 2 * cols + c * cols, cols), cols)
    go_x = put("go", 0, g_out.at[own_cols], go.at[go_part], across)
    for k in range(len(steps)):
        norm2(k)
        qkv2(k)
    for b in range(4):
        for p in range(pairs):
            tile = q2[b, :, pl.ds(p * LANES, LANES)]
            top, under = tile[:half], tile[half:]
            sq[2 * p, b] = jnp.where(low, top, swap(under)).astype(BF)
            sq[2 * p + 1, b] = jnp.where(low, swap(top), under).astype(BF)
    for pair in range(2):
        for d in range(1, seq):
            bands = pl.ds(2 * pair, 2)
            put("q", pair * seq + d, sq.at[paired(d), bands], rq.at[z, bands], z_peer(d))
    rq[z] = sq[z]

    frame_valid = jnp.concatenate(
        [valid_rows(start, size) for j, start, size, _ in steps for b in range(2)], axis=0
    )

    def spread(origin):
        at = pl.ds(pl.multiple_of(origin * frame, frame), frame)
        both = kv[at, :]
        one = jnp.where(low, jnp.ones_like(both), both)
        vx[at, :] = jnp.where(frame_valid, one, jnp.zeros_like(one))

    spread(z)
    for d in range(1, seq):
        for copy in kv_copies[d]:
            copy.wait_recv()
        spread(paired(d))

    mine = place * seq + z

    def q_copy(d, pair, origin):
        device, bands = (s, origin, x, c), pl.ds(2 * pair, 2)
        return remote("q", pair * seq + d, sq.at[0, bands], rq.at[origin, bands], device)

    def o_copy(d, pair, i, origin):
        b = 2 * pair + i
        device = (s, origin, pair, i)
        return remote("o", d * 4 + b, so.at[d, b], ro.at[mine], device, mine)

    def origin_of(d):
        origin = z
        for i in range((seq - 1).bit_length()):
            bit = 1 << i
            flip = lax.rem(lax.div(d, bit), 2)
            origin = origin + flip * (bit - 2 * bit * lax.rem(lax.div(z, bit), 2))
        return origin

    def each_o(d, pair, i, origin, act):
        itself = jnp.logical_and(d == 0, place == 2 * pair + i)

        @pl.when(jnp.logical_not(itself))
        def _():
            act(o_copy(d, pair, i, origin))

    @pl.loop(0, 2 * seq // 2)
    def _(turn):
        pair = lax.div(turn, seq // 2)
        group = lax.rem(turn, seq // 2)
        group = group + pair * (seq // 2 - 1 - 2 * group)
        ds = [2 * group + i for i in range(2)]
        origins = [origin_of(d) for d in ds]
        for d, origin in zip(ds, origins):

            @pl.when(d > 0)
            def _():
                q_copy(d, pair, origin).wait_recv()

        for d, origin in zip(ds, origins):
            q = []
            for i in range(2):
                packed = rq[origin, 2 * pair + i].astype(F32)
                q += [packed, swap(packed)]
            q = jnp.where(low, jnp.concatenate(q, axis=0), 0.0).astype(BF)
            scores = dot_t(q, kv[...])
            probs = jnp.exp2(scores - jnp.max(scores, axis=-1, keepdims=True))
            mixed = mm(probs.astype(BF), vx[...])
            out = mixed / jnp.where(low, 1.0, swap(mixed))
            for i in range(2):
                o = out[i * rows : (i + 1) * rows]
                so[d, 2 * pair + i] = jnp.where(low, swap(o)[:half], o[half:]).astype(BF)
                each_o(d, pair, i, origin, lambda copy: copy.start())

    ro_own = so[0, place]
    ro[mine] = ro_own
    go_x.wait_recv()
    go_f = put("go", 1, go.at[go_from], go.at[go_from], core)
    for copy in late_loads:
        copy.wait()
    for slot in range(4 * seq):

        @pl.when(slot != mine)
        def _():
            remote("o", 0, so.at[0, 0], ro.at[slot], core, slot).wait_recv()

    for i in range(2 * seq):
        at = pl.ds(i * LANES, LANES)
        even, odd = ro[2 * i].astype(F32), ro[2 * i + 1].astype(F32)
        pair = [jnp.where(low, even, swap(odd)), jnp.where(low, swap(even), odd)]
        a2[:, at] = jnp.concatenate(pair, axis=0).astype(BF)
    first = fst[...].astype(F32)
    go_f.wait_recv()
    second = (first + mm(a2[...], go[...])).astype(BF).astype(F32)
    stacked = jnp.concatenate([first, second], axis=-1)
    n3 = layer_norm(stacked, h_gain[...], head_eps).astype(BF)
    pj[...] = (mm(n3, wp[...]) + h_bias[...]).astype(BF)

    after = lax.rem(place + 1, 4)
    before = lax.rem(place + 3, 4)

    def frame_peer(index):
        return (s, z, index // 2, lax.rem(index, 2))

    start = (real - width) // TILE * TILE
    slab = halo.shape[1]
    down = put(
        "halo", 0, pj.at[pl.ds(start, rows - start)], halo.at[0, pl.ds(0, rows - start)],
        frame_peer(after),
    )
    upward = put("halo", 1, pj.at[pl.ds(0, slab)], halo.at[1], frame_peer(before))
    stage[0:rows, :] = second
    for r in range(height):
        blocks_ref[0, r] = stage[r * width : (r + 1) * width, :].astype(BF)
    base = 8
    xbuf[...] = jnp.zeros_like(xbuf)
    xbuf[base + width : base + width + real, :] = pj[...].astype(F32)[:real]
    down.wait_recv()
    upward.wait_recv()
    skip = real - width - start
    lower = jnp.where(place > 0, halo[0].astype(F32), 0.0)
    upper = jnp.where(place < 3, halo[1].astype(F32), 0.0)
    xbuf[base : base + width, :] = lower[skip : skip + width]
    xbuf[base + width + real : base + 2 * width + real, :] = upper[:width]
    col = lax.rem(lax.broadcasted_iota(jnp.int32, (rows, 1), 0), width)
    channels = pj.shape[1]
    total = jnp.zeros((rows, channels), F32)
    for i in range(3):
        for j in range(3):
            first_row = base + width * i + j - 1
            window = xbuf[first_row : first_row + rows, :]
            if j == 0:
                window = jnp.where(col > 0, window, 0.0)
            if j == 2:
                window = jnp.where(col < width - 1, window, 0.0)
            total = total + mm(window.astype(BF), wc[3 * i + j])
    stage[0:rows, 0:channels] = total
    for r in range(height):
        feat_ref[0, r] = stage[r * width : (r + 1) * width, 0:channels].astype(BF)

    for copy in started:
        copy.wait_send()

    @pl.loop(0, seq)
    def _(d):
        for b in range(4):
            each_o(d, b // 2, b % 2, origin_of(d), lambda copy: copy.wait_send())


def scene_program(seq, *arrays):
    (tokens, f_gain, f_qkv, f_out, g_gain, g_qkv, g_out, h_gain, h_proj, h_bias, h_conv) = arrays
    height, width, dim = tokens.shape[1:]
    real = height * width
    rows = up(real)
    cols = f_qkv.shape[2] // 2
    pairs = cols // LANES
    channels = h_proj.shape[1]
    frame = 4 * rows
    half = rows // 2
    count, most = len(step_list(rows)), max(step[2] for step in step_list(rows))
    vmem = pl.BlockSpec(memory_space=pltpu.VMEM)
    hbm = pl.BlockSpec(memory_space=pltpu.HBM)
    start = (real - width) // TILE * TILE
    slab = max(up(width), rows - start)
    _, copies = sem_layout(seq, count)
    return pl.pallas_call(
        functools.partial(scene_kernel, seq, height, width),
        out_shape=(
            jax.ShapeDtypeStruct(tokens.shape, BF),
            jax.ShapeDtypeStruct((1, height, width, channels), BF),
        ),
        in_specs=[hbm] * 11,
        out_specs=(vmem, vmem),
        scratch_shapes=[
            pltpu.VMEM(tokens.shape, BF),
            pltpu.VMEM((1, dim), F32),
            pltpu.VMEM((1, dim), F32),
            pltpu.VMEM((1, 2 * dim), F32),
            pltpu.VMEM((1, channels), F32),
            pltpu.VMEM((rows, dim), F32),
            pltpu.VMEM((4, rows, dim), BF),
            pltpu.VMEM((3, dim, cols), BF),
            pltpu.VMEM((3, dim, cols), BF),
            pltpu.VMEM((dim, 2 * cols), BF),
            pltpu.VMEM((dim, 2 * cols), BF),
            pltpu.VMEM((2 * cols, dim), BF),
            pltpu.VMEM((4 * cols, dim), BF),
            pltpu.VMEM(h_proj.shape, BF),
            pltpu.VMEM((9, channels, channels), BF),
            pltpu.VMEM((frame, cols), BF),
            pltpu.VMEM((frame, 2 * cols), BF),
            pltpu.VMEM((frame, 2 * cols), BF),
            pltpu.VMEM((count, 2, most, cols), BF),
            pltpu.VMEM((count, most, cols), BF),
            pltpu.VMEM((count, most, dim), F32),
            pltpu.VMEM((count, most, dim), BF),
            pltpu.VMEM((count, most, dim), BF),
            pltpu.VMEM((count, most, dim), BF),
            pltpu.VMEM((count, most, dim), BF),
            pltpu.VMEM((rows, dim), BF),
            pltpu.VMEM((4, rows, cols), F32),
            pltpu.VMEM((seq, frame, LANES), BF),
            pltpu.VMEM((seq * frame, LANES), BF),
            pltpu.VMEM((seq * frame, LANES), BF),
            pltpu.VMEM((seq, 4, half, LANES), BF),
            pltpu.VMEM((seq, 4, half, LANES), BF),
            pltpu.VMEM((seq, 4, half, LANES), BF),
            pltpu.VMEM((4 * seq, half, LANES), BF),
            pltpu.VMEM((rows, 4 * cols), BF),
            pltpu.VMEM((rows, channels), BF),
            pltpu.VMEM((2, slab, channels), BF),
            pltpu.VMEM((up(rows + 2 * width + 2 * TILE), channels), F32),
            pltpu.SemaphoreType.DMA((copies,)),
            pltpu.SemaphoreType.DMA((copies,)),
            pltpu.SemaphoreType.DMA((10 + 4 * pairs,)),
        ],
        compiler_params=pltpu.CompilerParams(
            collective_id=0, has_side_effects=True, vmem_limit_bytes=40 * 2**20
        ),
    )(
        *[
            pltpu.with_memory_space_constraint(array, pltpu.HBM)
            for array in (
                tokens,
                f_gain.reshape(1, -1),
                f_qkv,
                f_out,
                g_gain.reshape(1, -1),
                g_qkv,
                g_out,
                h_gain.reshape(1, -1),
                h_proj,
                h_bias.reshape(1, -1),
                h_conv.reshape(9, channels, channels),
            )
        ]
    )


def routed(mesh, *arrays):
    sizes = mesh.shape
    frames, height, width = arrays[0].shape[:3]
    heads = arrays[2].shape[2] // HD
    fits = (
        sizes["head"] == 2
        and sizes["band"] == 2
        and frames == 1
        and heads == 2 * sizes["seq"]
        and sizes["seq"] & (sizes["seq"] - 1) == 0
        and sizes["seq"] >= 2
        and arrays[0].shape[3] == 2 * arrays[2].shape[2]
        and arrays[10].shape[2] <= arrays[0].shape[3]
        and height * width >= up(width)
        and up(height * width) >= 2 * TILE
    )
    if fits:
        return scene_program(sizes["seq"], *arrays)
    return on_device(*arrays)


def solution(mesh):
    return jax.shard_map(
        functools.partial(routed, mesh),
        mesh=mesh,
        in_specs=(
            P(("scene", "seq"), ("head", "band"), None, None),
            P(),
            P(None, None, "head"),
            P("head", None),
            P(),
            P(None, None, "head"),
            P("head", None),
            P(),
            P(),
            P(),
            P(),
        ),
        out_specs=(
            P(("scene", "seq"), ("head", "band"), None, None),
            P(("scene", "seq"), ("head", "band"), None, None),
        ),
        check_vma=False,
    )
```

```python
import functools
import math

import jax
import jax.numpy as jnp
from jax import lax
from jax.experimental import pallas as pl
from jax.experimental.pallas import tpu as pltpu
from jax.sharding import PartitionSpec as P

HD = 64


norm_eps = 1e-06
head_eps = 1e-05


def padded_2(block, sides, width):
    for axis, dim in sides:
        count = lax.axis_size(axis)
        forward = [(i, i + 1) for i in range(count - 1)]
        backward = [(target, source) for source, target in forward]
        low = lax.ppermute(
            lax.slice_in_dim(block, block.shape[dim] - width, None, axis=dim), axis, forward
        )
        high = lax.ppermute(lax.slice_in_dim(block, 0, width, axis=dim), axis, backward)
        block = jnp.concatenate([low, block, high], axis=dim)
    return block


def layer_norm(values, gain, epsilon):
    centre = values - jnp.mean(values, axis=-1, keepdims=True)
    spread = jnp.mean(centre * centre, axis=-1, keepdims=True)
    return centre * lax.rsqrt(spread + epsilon) * gain


def by_heads(matrix):
    return matrix.reshape(matrix.shape[0], matrix.shape[1] // HD, HD)


def attend_local(queries, keys_all, values_all):
    scores = jnp.einsum(
        "qhd,khd->qhk", by_heads(queries), by_heads(keys_all), preferred_element_type=jnp.float32
    ) * HD ** (-0.5)
    probs = jnp.exp(scores - jnp.max(scores, axis=-1, keepdims=True))
    mixed = jnp.einsum(
        "qhk,khd->qhd",
        probs.astype(jnp.bfloat16),
        by_heads(values_all),
        preferred_element_type=jnp.float32,
    )
    mixed = mixed / jnp.sum(probs, axis=-1)[..., None]
    return mixed.reshape(queries.shape).astype(jnp.bfloat16)


def key_step(local_rows, portion_rows):
    amount = portion_rows // local_rows
    best = 1
    for factor in range(1, amount + 1):
        if amount % factor == 0 and local_rows * factor <= max(local_rows, 1024):
            best = factor
    return local_rows * best


def fresh_carry(queries):
    heads_q = by_heads(queries)
    return (
        jnp.full(heads_q.shape[:2], -jnp.inf, jnp.float32),
        jnp.zeros(heads_q.shape[:2], jnp.float32),
        jnp.zeros(heads_q.shape, jnp.float32),
    )


def finish(carry, queries):
    return (carry[2] / carry[1][..., None]).reshape(queries.shape).astype(jnp.bfloat16)


def fold_keys(queries, carry, portions, local_rows):
    keys_in, values_in = portions
    step_rows = key_step(local_rows, keys_in.shape[0])
    heads_q = by_heads(queries)
    key_blocks = keys_in.reshape(-1, step_rows, keys_in.shape[1])
    value_blocks = values_in.reshape(-1, step_rows, values_in.shape[1])

    def absorb(states, blocks_pair):
        running_max, running_sum, weighted = states
        scores = jnp.einsum(
            "qhd,khd->qhk", heads_q, by_heads(blocks_pair[0]), preferred_element_type=jnp.float32
        ) * HD ** (-0.5)
        new_max = jnp.maximum(running_max, jnp.max(scores, axis=-1))
        decay = jnp.exp(running_max - new_max)
        probs = jnp.exp(scores - new_max[..., None])
        running_sum = running_sum * decay + jnp.sum(probs, axis=-1)
        weighted = weighted * decay[..., None] + jnp.einsum(
            "qhk,khd->qhd",
            probs.astype(jnp.bfloat16),
            by_heads(blocks_pair[1]),
            preferred_element_type=jnp.float32,
        )
        return ((new_max, running_sum, weighted), None)

    carry, ignored = lax.scan(absorb, carry, (key_blocks, value_blocks))
    return carry


def attention_block(inputs, gain, qkv_weight, out_weight, wide):
    normed = layer_norm(inputs.astype(jnp.float32), gain, norm_eps).astype(jnp.bfloat16)
    gathered = lax.all_gather(normed, "head", axis=1, tiled=True)
    flattened = gathered.reshape(-1, gathered.shape[-1])
    query_rows = jnp.dot(flattened, qkv_weight[0], preferred_element_type=jnp.float32).astype(
        jnp.bfloat16
    )
    key_rows = jnp.dot(flattened, qkv_weight[1], preferred_element_type=jnp.float32).astype(
        jnp.bfloat16
    )
    value_rows = jnp.dot(flattened, qkv_weight[2], preferred_element_type=jnp.float32).astype(
        jnp.bfloat16
    )
    if wide:
        carry = fold_keys(
            query_rows,
            fresh_carry(query_rows),
            (
                lax.all_gather(key_rows, ("seq", "band"), axis=0, tiled=True),
                lax.all_gather(value_rows, ("seq", "band"), axis=0, tiled=True),
            ),
            key_rows.shape[0],
        )
        attended = finish(carry, query_rows)
    else:
        keys_all, values_all = (
            lax.all_gather(key_rows, "band", axis=0, tiled=True),
            lax.all_gather(value_rows, "band", axis=0, tiled=True),
        )
        attended = attend_local(query_rows, keys_all, values_all)
    band_rows = inputs.shape[1] * inputs.shape[2]
    own_rows = lax.all_to_all(attended, "head", split_axis=0, concat_axis=1, tiled=True)
    branch = jnp.dot(
        own_rows,
        lax.all_gather(out_weight, "head", axis=0, tiled=True),
        preferred_element_type=jnp.float32,
    )
    merged = inputs.astype(jnp.float32).reshape(band_rows, -1) + branch
    return merged.astype(jnp.bfloat16).reshape(inputs.shape)


def on_device(
    tokens,
    frame_gain,
    frame_qkv,
    frame_out,
    global_gain,
    global_qkv,
    global_out,
    head_gain,
    head_proj,
    head_bias,
    head_conv,
):
    first = attention_block(tokens, frame_gain, frame_qkv, frame_out, False)
    second = attention_block(first, global_gain, global_qkv, global_out, True)
    band_height = tokens.shape[1]
    grid_width = tokens.shape[2]
    stacked = jnp.concatenate([first.astype(jnp.float32), second.astype(jnp.float32)], axis=-1)
    normed = layer_norm(stacked, head_gain, head_eps).astype(jnp.bfloat16)
    projected = (
        jnp.dot(
            normed.reshape(-1, stacked.shape[-1]), head_proj, preferred_element_type=jnp.float32
        )
        + head_bias
    )
    projected = projected.astype(jnp.bfloat16).reshape(
        tokens.shape[0], band_height, grid_width, head_proj.shape[1]
    )
    padded = padded_2(projected, ((("head", "band"), 1),), 1)
    padded = jnp.pad(padded, ((0, 0), (0, 0), (1, 1), (0, 0)))
    totals = jnp.zeros(projected.shape, jnp.float32)
    for offset_row in range(3):
        for offset_col in range(3):
            window = padded[
                :, offset_row : offset_row + band_height, offset_col : offset_col + grid_width
            ]
            totals = totals + jnp.einsum(
                "frcx,xy->frcy",
                window,
                head_conv[offset_row, offset_col],
                preferred_element_type=jnp.float32,
            )
    return (second, totals.astype(jnp.bfloat16))


BF = jnp.bfloat16
F32 = jnp.float32
TILE = 16
LANES = 2 * HD
STEP_SHARES = ((2, 5), (6, 1))
QSCALE = HD ** (-0.5) * math.log2(math.e)


def up(count):
    return -(-count // TILE) * TILE


def mm(a, b):
    return jnp.dot(a, b, preferred_element_type=F32)


def swap(values):
    return pltpu.roll(values, HD, axis=1)


def dot_t(a, b):
    return lax.dot_general(a, b, (((1,), (1,)), ((), ())), preferred_element_type=F32)


def row_parts(rows):
    first = up(rows // 2)
    return [(0, first), (first, rows - first)]


def split_rows(rows, shares):
    units, sizes = rows // TILE, []
    for i, share in enumerate(shares):
        left = units - sum(sizes)
        size = left if i == len(shares) - 1 else max(1, units * share // sum(shares))
        sizes.append(size)
    return [size * TILE for size in sizes if size > 0]


def step_list(rows):
    steps, at = [], 0
    for j, shares in enumerate(STEP_SHARES):
        start = 0
        for size in split_rows(rows, shares):
            steps.append((j, start, size, at))
            at += 2 * size
            start += size
    return steps


def sem_layout(seq, count):
    names = [
        ("tok", 1), ("tok_x", 2), ("tok_f", 2), ("att", count), ("part", count), ("norm", count),
        ("kv", count * seq), ("q", 4 * seq), ("o", 4 * seq), ("go", 2), ("halo", 2),
    ]
    at, table = 0, {}
    for name, size in names:
        table[name] = at
        at += size
    return table, at


def scene_kernel(
    seq,
    height,
    width,
    tok_hbm,
    f_gain_hbm,
    f_qkv,
    f_out,
    g_gain_hbm,
    g_qkv,
    g_out,
    h_gain_hbm,
    h_proj,
    h_bias_hbm,
    h_conv,
    blocks_ref,
    feat_ref,
    tok_ref,
    f_gain,
    g_gain,
    h_gain,
    h_bias,
    stage,
    toks,
    wf,
    wg,
    wkv1,
    wkv2,
    fo,
    go,
    wp,
    wc,
    q1,
    kv1,
    vx1,
    att,
    att_in,
    p_own,
    p_out,
    p_in,
    n_own,
    n_in,
    fst,
    q2,
    skv,
    kv,
    vx,
    sq,
    rq,
    so,
    ro,
    a2,
    pj,
    halo,
    xbuf,
    send,
    recv,
    local,
):
    s, z = lax.axis_index("scene"), lax.axis_index("seq")
    x, c = lax.axis_index("head"), lax.axis_index("band")
    real = height * width
    rows, dim = fst.shape
    cols = wf.shape[2]
    pairs = cols // LANES
    frame = 4 * rows
    half = rows // 2
    steps = step_list(rows)
    parts = row_parts(rows)
    sems, _ = sem_layout(seq, len(steps))
    core, across = (s, z, x, 1 - c), (s, z, 1 - x, c)
    place = 2 * x + c

    def paired(k):
        bits = [1 << i for i in range(seq.bit_length()) if k >> i & 1]
        return z + sum(bit - 2 * bit * lax.rem(lax.div(z, bit), 2) for bit in bits)

    def z_peer(k):
        return (s, paired(k), x, c)

    def remote(name, index, source, target, device, back=None):
        return pltpu.make_async_remote_copy(
            src_ref=source,
            dst_ref=target,
            send_sem=send.at[sems[name] + index],
            recv_sem=recv.at[sems[name] + (index if back is None else back)],
            device_id=device,
            device_id_type=pl.DeviceIdType.MESH,
        )

    barrier = pltpu.get_barrier_semaphore()
    everyone = [core, across, (s, z, 1 - x, 1 - c)] + [z_peer(d) for d in range(1, seq)]
    for device in everyone:
        pl.semaphore_signal(
            barrier, inc=1, device_id=device, device_id_type=pl.DeviceIdType.MESH
        )

    started = []

    def put(name, index, source, target, device):
        copy = remote(name, index, source, target, device)
        copy.start()
        started.append(copy)
        return copy

    own_cols = pl.ds(pl.multiple_of(c * cols, cols), cols)
    loads = []

    def load(source, target):
        copy = pltpu.make_async_copy(source, target, local.at[len(loads)])
        copy.start()
        loads.append(copy)
        return copy

    tok_load = load(tok_hbm, tok_ref)
    f_gain_load = load(f_gain_hbm, f_gain)
    wf_load = load(f_qkv.at[:, :, own_cols], wf)
    fo_loads = []
    for r in range(2):
        owner = c if r == 0 else 1 - c
        for i in range(2 * pairs):
            source = f_out.at[pl.ds(pl.multiple_of(owner * cols + i * HD, HD), HD)]
            fo_loads.append(load(source, fo.at[pl.ds(r * cols + (i ^ 1) * HD, HD)]))
    wg_load = load(g_qkv.at[:, :, own_cols], wg)
    half_rows = pl.ds(pl.multiple_of(x * 2 * cols, 2 * cols), 2 * cols)
    g_gain_load = load(g_gain_hbm, g_gain)
    late_loads = [load(g_out, go.at[half_rows]), load(h_proj, wp), load(h_conv, wc)]
    late_loads += [load(h_gain_hbm, h_gain), load(h_bias_hbm, h_bias)]

    tok_load.wait()
    for r in range(height):
        stage[r * width : (r + 1) * width, :] = tok_ref[0, r].astype(F32)
    for r in range(real, rows):
        stage[r : r + 1, :] = stage[real - 1 : real, :]
    toks[0] = stage[0:rows, :].astype(BF)
    pl.semaphore_wait(barrier, len(everyone))

    tok_x = []
    for k, (start, size) in enumerate(parts):
        at = pl.ds(start, size)
        tok_x.append(put("tok_x", k, toks.at[0, at], toks.at[2, at], across))
    tok_core = put("tok", 0, toks.at[0], toks.at[1], core)

    low = lax.broadcasted_iota(jnp.int32, (1, LANES), 1) < HD
    lane = lax.broadcasted_iota(jnp.int32, (1, 2 * cols), 1)
    v_lanes = lax.rem(lax.div(lane, HD), 4)
    v_lanes = jnp.logical_or(v_lanes == 1, v_lanes == 2)

    def valid_rows(start, size):
        return lax.broadcasted_iota(jnp.int32, (size, 1), 0) + start < real

    f_gain_load.wait()
    wf_load.wait()
    for p in range(pairs):
        at = pl.ds(p * LANES, LANES)
        k_part, v_part = wf[1, :, at], swap(wf[2, :, at].astype(F32)).astype(BF)
        wkv1[:, pl.ds(2 * p * LANES, LANES)] = jnp.where(low, k_part, v_part)
        wkv1[:, pl.ds((2 * p + 1) * LANES, LANES)] = jnp.where(low, v_part, k_part)

    def qkv1(slot, start, size, band):
        n = layer_norm(toks[slot, pl.ds(start, size)].astype(F32), f_gain[...], norm_eps).astype(BF)
        at = pl.ds(pl.multiple_of(band * rows + start, TILE), size)
        q1[at, :] = (mm(n, wf[0]) * QSCALE).astype(BF)
        both = mm(n, wkv1[...]).astype(BF)
        kv1[at, :] = both
        one = jnp.where(v_lanes, both, jnp.ones_like(both))
        vx1[at, :] = jnp.where(valid_rows(start, size), one, jnp.zeros_like(one))

    qkv1(0, 0, rows, place)
    tok_core.wait_recv()
    qkv1(1, 0, rows, 2 * x + 1 - c)
    g_gain_load.wait()
    wg_load.wait()
    for p in range(pairs):
        at = pl.ds(p * LANES, LANES)
        k_part, v_part = wg[1, :, at], wg[2, :, at]
        k_swap, v_swap = swap(k_part.astype(F32)).astype(BF), swap(v_part.astype(F32)).astype(BF)
        wkv2[:, pl.ds(2 * p * LANES, LANES)] = jnp.where(low, k_part, v_swap)
        wkv2[:, pl.ds((2 * p + 1) * LANES, LANES)] = jnp.where(low, k_swap, v_part)
    tok_f = []
    for k, (start, size) in enumerate(parts):
        at = pl.ds(start, size)
        tok_x[k].wait_recv()
        tok_f.append(put("tok_f", k, toks.at[2, at], toks.at[3, at], core))
        qkv1(2, start, size, 2 * (1 - x) + c)
    for k, (start, size) in enumerate(parts):
        tok_f[k].wait_recv()
        qkv1(3, start, size, 2 * (1 - x) + 1 - c)

    att_copies, p_copies, n_copies = [], [], []

    def attend(k, p):
        j, start, size, _ = steps[k]
        at = pl.ds(p * LANES, LANES)
        qp = jnp.concatenate(
            [q1[pl.ds((2 * j + b) * rows + start, size), at] for b in range(2)], axis=0
        )
        mixed = []
        for e in range(2):
            tile = pl.ds((2 * p + e) * LANES, LANES)
            zero = jnp.zeros_like(qp)
            lhs = jnp.where(low, qp, zero) if e == 0 else jnp.where(low, zero, qp)
            scores = dot_t(lhs, kv1[:, tile])
            probs = jnp.exp2(scores - jnp.max(scores, axis=-1, keepdims=True))
            mixed.append(mm(probs.astype(BF), vx1[:, tile]))
        top = jnp.where(low, mixed[1], mixed[0])
        bottom = swap(jnp.where(low, mixed[0], mixed[1]))
        out = (top / bottom).astype(BF)
        for b in range(2):
            att[k, b, pl.ds(0, size), at] = out[b * size : (b + 1) * size]

    def send_att(k):
        at = pl.ds(0, steps[k][2])
        att_copies.append(put("att", k, att.at[k, 1 - c, at], att_in.at[k, at], core))

    def project(k):
        j, start, size, _ = steps[k]
        at = pl.ds(0, size)
        att_copies[k].wait_recv()
        lhs = jnp.concatenate([att[k, c, at], att_in[k, at]], axis=1)
        partial = mm(lhs, fo[...])
        p_own[k, at] = partial
        p_out[k, at] = partial.astype(BF)
        p_copies.append(put("part", k, p_out.at[k, at], p_in.at[k, at], across))

    def norm2(k):
        j, start, size, _ = steps[k]
        at = pl.ds(0, size)
        slot = jnp.where(x == j, 0, 2)
        p_copies[k].wait_recv()
        tok = toks[slot, pl.ds(start, size)].astype(F32)
        first = (tok + p_own[k, at] + p_in[k, at].astype(F32)).astype(BF)

        @pl.when(x == j)
        def _():
            fst[pl.ds(start, size), :] = first

        n_own[k, at] = layer_norm(first.astype(F32), g_gain[...], norm_eps).astype(BF)
        n_copies.append(put("norm", k, n_own.at[k, at], n_in.at[k, at], core))

    kv_copies = [[] for _ in range(seq)]

    def qkv2(k):
        j, start, size, offset = steps[k]
        n_copies[k].wait_recv()
        at = pl.ds(0, size)
        n = jnp.concatenate([n_own[k, at], n_in[k, at]], axis=0)
        both = mm(n, wkv2[...]).astype(BF)
        for h in range(2 * pairs):
            skv[h, pl.ds(offset, 2 * size), :] = both[:, h * LANES : (h + 1) * LANES]
        to = pl.ds(pl.multiple_of(z * frame + offset, TILE), 2 * size)
        for d in range(1, seq):
            source = skv.at[paired(d), pl.ds(offset, 2 * size)]
            kv_copies[d].append(put("kv", k * seq + d, source, kv.at[to], z_peer(d)))
        kv[to, :] = skv[z, pl.ds(offset, 2 * size), :]
        queries = mm(n, wg[0]) * QSCALE
        q2[2 * j + c, pl.ds(start, size), :] = queries[:size]
        q2[2 * j + 1 - c, pl.ds(start, size), :] = queries[size:]

    for copy in fo_loads:
        copy.wait()
    for p in range(pairs):
        attend(0, p)
    send_att(0)
    for k in range(1, len(steps)):
        for p in range(pairs):
            attend(k, p)
            if p == 0:
                project(k - 1)
        send_att(k)
    project(len(steps) - 1)
    go_part = pl.ds(pl.multiple_of(x * 2 * cols + c * cols, cols), cols)
    go_from = pl.ds(pl.multiple_of((1 - x) * 2 * cols + c * cols, cols), cols)
    go_x = put("go", 0, g_out.at[own_cols], go.at[go_part], across)
    for k in range(len(steps)):
        norm2(k)
        qkv2(k)
    for b in range(4):
        for p in range(pairs):
            tile = q2[b, :, pl.ds(p * LANES, LANES)]
            top, under = tile[:half], tile[half:]
            sq[2 * p, b] = jnp.where(low, top, swap(under)).astype(BF)
            sq[2 * p + 1, b] = jnp.where(low, swap(top), under).astype(BF)
    for pair in range(2):
        for d in range(1, seq):
            bands = pl.ds(2 * pair, 2)
            put("q", pair * seq + d, sq.at[paired(d), bands], rq.at[z, bands], z_peer(d))
    rq[z] = sq[z]

    frame_valid = jnp.concatenate(
        [valid_rows(start, size) for j, start, size, _ in steps for b in range(2)], axis=0
    )

    def spread(origin):
        at = pl.ds(pl.multiple_of(origin * frame, frame), frame)
        both = kv[at, :]
        one = jnp.where(low, jnp.ones_like(both), both)
        vx[at, :] = jnp.where(frame_valid, one, jnp.zeros_like(one))

    spread(z)
    for d in range(1, seq):
        for copy in kv_copies[d]:
            copy.wait_recv()
        spread(paired(d))

    mine = place * seq + z

    def q_copy(d, pair, origin):
        device, bands = (s, origin, x, c), pl.ds(2 * pair, 2)
        return remote("q", pair * seq + d, sq.at[0, bands], rq.at[origin, bands], device)

    def o_copy(d, pair, i, origin):
        b = 2 * pair + i
        device = (s, origin, pair, i)
        return remote("o", d * 4 + b, so.at[d, b], ro.at[mine], device, mine)

    def origin_of(d):
        origin = z
        for i in range((seq - 1).bit_length()):
            bit = 1 << i
            flip = lax.rem(lax.div(d, bit), 2)
            origin = origin + flip * (bit - 2 * bit * lax.rem(lax.div(z, bit), 2))
        return origin

    def each_o(d, pair, i, origin, act):
        itself = jnp.logical_and(d == 0, place == 2 * pair + i)

        @pl.when(jnp.logical_not(itself))
        def _():
            act(o_copy(d, pair, i, origin))

    @pl.loop(0, 2 * seq // 2)
    def _(turn):
        pair = lax.div(turn, seq // 2)
        group = lax.rem(turn, seq // 2)
        group = group + pair * (seq // 2 - 1 - 2 * group)
        ds = [2 * group + i for i in range(2)]
        origins = [origin_of(d) for d in ds]
        for d, origin in zip(ds, origins):

            @pl.when(d > 0)
            def _():
                q_copy(d, pair, origin).wait_recv()

        for d, origin in zip(ds, origins):
            q = []
            for i in range(2):
                packed = rq[origin, 2 * pair + i].astype(F32)
                q += [packed, swap(packed)]
            q = jnp.where(low, jnp.concatenate(q, axis=0), 0.0).astype(BF)
            scores = dot_t(q, kv[...])
            probs = jnp.exp2(scores - jnp.max(scores, axis=-1, keepdims=True))
            mixed = mm(probs.astype(BF), vx[...])
            out = mixed / jnp.where(low, 1.0, swap(mixed))
            for i in range(2):
                o = out[i * rows : (i + 1) * rows]
                so[d, 2 * pair + i] = jnp.where(low, swap(o)[:half], o[half:]).astype(BF)
                each_o(d, pair, i, origin, lambda copy: copy.start())

    ro_own = so[0, place]
    ro[mine] = ro_own
    go_x.wait_recv()
    go_f = put("go", 1, go.at[go_from], go.at[go_from], core)
    for copy in late_loads:
        copy.wait()
    for slot in range(4 * seq):

        @pl.when(slot != mine)
        def _():
            remote("o", 0, so.at[0, 0], ro.at[slot], core, slot).wait_recv()

    for i in range(2 * seq):
        at = pl.ds(i * LANES, LANES)
        even, odd = ro[2 * i].astype(F32), ro[2 * i + 1].astype(F32)
        pair = [jnp.where(low, even, swap(odd)), jnp.where(low, swap(even), odd)]
        a2[:, at] = jnp.concatenate(pair, axis=0).astype(BF)
    first = fst[...].astype(F32)
    go_f.wait_recv()
    second = (first + mm(a2[...], go[...])).astype(BF).astype(F32)
    stacked = jnp.concatenate([first, second], axis=-1)
    n3 = layer_norm(stacked, h_gain[...], head_eps).astype(BF)
    pj[...] = (mm(n3, wp[...]) + h_bias[...]).astype(BF)

    after = lax.rem(place + 1, 4)
    before = lax.rem(place + 3, 4)

    def frame_peer(index):
        return (s, z, index // 2, lax.rem(index, 2))

    start = (real - width) // TILE * TILE
    slab = halo.shape[1]
    down = put(
        "halo", 0, pj.at[pl.ds(start, rows - start)], halo.at[0, pl.ds(0, rows - start)],
        frame_peer(after),
    )
    upward = put("halo", 1, pj.at[pl.ds(0, slab)], halo.at[1], frame_peer(before))
    stage[0:rows, :] = second
    for r in range(height):
        blocks_ref[0, r] = stage[r * width : (r + 1) * width, :].astype(BF)
    base = 8
    xbuf[...] = jnp.zeros_like(xbuf)
    xbuf[base + width : base + width + real, :] = pj[...].astype(F32)[:real]
    down.wait_recv()
    upward.wait_recv()
    skip = real - width - start
    lower = jnp.where(place > 0, halo[0].astype(F32), 0.0)
    upper = jnp.where(place < 3, halo[1].astype(F32), 0.0)
    xbuf[base : base + width, :] = lower[skip : skip + width]
    xbuf[base + width + real : base + 2 * width + real, :] = upper[:width]
    col = lax.rem(lax.broadcasted_iota(jnp.int32, (rows, 1), 0), width)
    channels = pj.shape[1]
    total = jnp.zeros((rows, channels), F32)
    for i in range(3):
        for j in range(3):
            first_row = base + width * i + j - 1
            window = xbuf[first_row : first_row + rows, :]
            if j == 0:
                window = jnp.where(col > 0, window, 0.0)
            if j == 2:
                window = jnp.where(col < width - 1, window, 0.0)
            total = total + mm(window.astype(BF), wc[3 * i + j])
    stage[0:rows, 0:channels] = total
    for r in range(height):
        feat_ref[0, r] = stage[r * width : (r + 1) * width, 0:channels].astype(BF)

    for copy in started:
        copy.wait_send()

    @pl.loop(0, seq)
    def _(d):
        for b in range(4):
            each_o(d, b // 2, b % 2, origin_of(d), lambda copy: copy.wait_send())


def scene_program(seq, *arrays):
    (tokens, f_gain, f_qkv, f_out, g_gain, g_qkv, g_out, h_gain, h_proj, h_bias, h_conv) = arrays
    height, width, dim = tokens.shape[1:]
    real = height * width
    rows = up(real)
    cols = f_qkv.shape[2] // 2
    pairs = cols // LANES
    channels = h_proj.shape[1]
    frame = 4 * rows
    half = rows // 2
    count, most = len(step_list(rows)), max(step[2] for step in step_list(rows))
    vmem = pl.BlockSpec(memory_space=pltpu.VMEM)
    hbm = pl.BlockSpec(memory_space=pltpu.HBM)
    start = (real - width) // TILE * TILE
    slab = max(up(width), rows - start)
    _, copies = sem_layout(seq, count)
    return pl.pallas_call(
        functools.partial(scene_kernel, seq, height, width),
        out_shape=(
            jax.ShapeDtypeStruct(tokens.shape, BF),
            jax.ShapeDtypeStruct((1, height, width, channels), BF),
        ),
        in_specs=[hbm] * 11,
        out_specs=(vmem, vmem),
        scratch_shapes=[
            pltpu.VMEM(tokens.shape, BF),
            pltpu.VMEM((1, dim), F32),
            pltpu.VMEM((1, dim), F32),
            pltpu.VMEM((1, 2 * dim), F32),
            pltpu.VMEM((1, channels), F32),
            pltpu.VMEM((rows, dim), F32),
            pltpu.VMEM((4, rows, dim), BF),
            pltpu.VMEM((3, dim, cols), BF),
            pltpu.VMEM((3, dim, cols), BF),
            pltpu.VMEM((dim, 2 * cols), BF),
            pltpu.VMEM((dim, 2 * cols), BF),
            pltpu.VMEM((2 * cols, dim), BF),
            pltpu.VMEM((4 * cols, dim), BF),
            pltpu.VMEM(h_proj.shape, BF),
            pltpu.VMEM((9, channels, channels), BF),
            pltpu.VMEM((frame, cols), BF),
            pltpu.VMEM((frame, 2 * cols), BF),
            pltpu.VMEM((frame, 2 * cols), BF),
            pltpu.VMEM((count, 2, most, cols), BF),
            pltpu.VMEM((count, most, cols), BF),
            pltpu.VMEM((count, most, dim), F32),
            pltpu.VMEM((count, most, dim), BF),
            pltpu.VMEM((count, most, dim), BF),
            pltpu.VMEM((count, most, dim), BF),
            pltpu.VMEM((count, most, dim), BF),
            pltpu.VMEM((rows, dim), BF),
            pltpu.VMEM((4, rows, cols), F32),
            pltpu.VMEM((seq, frame, LANES), BF),
            pltpu.VMEM((seq * frame, LANES), BF),
            pltpu.VMEM((seq * frame, LANES), BF),
            pltpu.VMEM((seq, 4, half, LANES), BF),
            pltpu.VMEM((seq, 4, half, LANES), BF),
            pltpu.VMEM((seq, 4, half, LANES), BF),
            pltpu.VMEM((4 * seq, half, LANES), BF),
            pltpu.VMEM((rows, 4 * cols), BF),
            pltpu.VMEM((rows, channels), BF),
            pltpu.VMEM((2, slab, channels), BF),
            pltpu.VMEM((up(rows + 2 * width + 2 * TILE), channels), F32),
            pltpu.SemaphoreType.DMA((copies,)),
            pltpu.SemaphoreType.DMA((copies,)),
            pltpu.SemaphoreType.DMA((10 + 4 * pairs,)),
        ],
        compiler_params=pltpu.CompilerParams(
            collective_id=0, has_side_effects=True, vmem_limit_bytes=40 * 2**20
        ),
    )(
        *[
            pltpu.with_memory_space_constraint(array, pltpu.HBM)
            for array in (
                tokens,
                f_gain.reshape(1, -1),
                f_qkv,
                f_out,
                g_gain.reshape(1, -1),
                g_qkv,
                g_out,
                h_gain.reshape(1, -1),
                h_proj,
                h_bias.reshape(1, -1),
                h_conv.reshape(9, channels, channels),
            )
        ]
    )


def routed(mesh, *arrays):
    sizes = mesh.shape
    frames, height, width = arrays[0].shape[:3]
    heads = arrays[2].shape[2] // HD
    fits = (
        sizes["head"] == 2
        and sizes["band"] == 2
        and frames == 1
        and heads == 2 * sizes["seq"]
        and sizes["seq"] & (sizes["seq"] - 1) == 0
        and sizes["seq"] >= 2
        and arrays[0].shape[3] == 2 * arrays[2].shape[2]
        and arrays[10].shape[2] <= arrays[0].shape[3]
        and height * width >= up(width)
        and up(height * width) >= 2 * TILE
    )
    if fits:
        return scene_program(sizes["seq"], *arrays)
    return on_device(*arrays)


def solution(mesh):
    return jax.shard_map(
        functools.partial(routed, mesh),
        mesh=mesh,
        in_specs=(
            P(("scene", "seq"), ("head", "band"), None, None),
            P(),
            P(None, None, "head"),
            P("head", None),
            P(),
            P(None, None, "head"),
            P("head", None),
            P(),
            P(),
            P(),
            P(),
        ),
        out_specs=(
            P(("scene", "seq"), ("head", "band"), None, None),
            P(("scene", "seq"), ("head", "band"), None, None),
        ),
        check_vma=False,
    )
```
